32 devices in a mesh: gx: 4 (over y, x), gy: 4 (over z), gz: 2 (over core).
Axes of the slice: x: 2, y: 2, z: 4, core: 2. Of those that a mesh axis runs over, the one named last changes fastest.
Arguments:
- fields: float32 [4, 256, 256, 256], P(None, 'gx', 'gy', 'gz'), may hold values from -6 to 6
- sources: bfloat16 [4, 256, 256, 256], P(None, 'gx', 'gy', 'gz'), may hold values from -6 to 6
- material: int32 [256, 256, 256], P('gx', 'gy', 'gz'), may hold values from 0 to 3
- shift_real: float32 [4], replicated, may hold values from -2 to -0.5
- shift_imag: float32 [4], replicated, may hold values from 0.5 to 2
- design_share: float32 [4], replicated, may hold values from 0.2 to 1
- density: float32 [256, 256], P('gx', 'gy'), may hold values from 0 to 1
- owner_map: int32 [4, 4, 64, 1], P('gx', 'gy'), may hold values from 0 to 15; in each aligned block of 64 rows (0 to 63, 64 to 127, ..., all dimensions but the last counted through in order) at most 8 rows name the same one
Outputs:
- fields_out: float32 [4, 256, 256, 256], P(None, 'gx', 'gy', 'gz')
- owner_gradient: float32 [16, 16, 512], P(('gx', 'gy'))
The draws below stay inside these ranges and needn't reach their ends.
Inputs may be any that keep to these rules, and one draw needn't show every extreme that they name: `owner_map`: within the 64 tiles of one column (aligned blocks of the map's rows), no owner is named more than 8 times, and in some column some owner is named exactly 8 times.
All inputs are finite; a program needn't handle non-finite values.
Results may differ from the reference program's by a relative error of at most 0.0003.
Values may be sent and summed in bfloat16 or wider, within the bound.
No kernel may reach another device: no remote copies, remote signals or barrier semaphores. Data moves between devices by JAX's collectives and lax.ppermute only.
A program may use at most 320 MiB of HBM per device.

```python
import math
import jax
import jax.numpy as jnp
import numpy as np
from jax import lax

CX = 64
CY = 64
NMAT = 4
R = 8
TS = 8
MOST = 8
NX = 256
NY = 256
NZ = 256
TPC = 64
OWNERS = 16
N_GX = 4
N_GY = 4


def draw_density(key, part):
    subkeys = jax.random.split(key, 3)
    row_pos = jnp.arange(NX, dtype=jnp.float32)[:, None]
    col_pos = jnp.arange(NY, dtype=jnp.float32)[None, :]
    wave_numbers = jax.random.uniform(subkeys[0], (3, 2), jnp.float32, 0.08, 0.2)
    phases = jax.random.uniform(subkeys[1], (3,), jnp.float32, 0.0, 6.283)
    smooth = (jnp.cos(wave_numbers[0, 0] * row_pos + wave_numbers[0, 1] * col_pos + phases[0]) + jnp.cos(wave_numbers[1, 0] * row_pos - wave_numbers[1, 1] * col_pos + phases[1]) + jnp.cos(wave_numbers[2, 0] * row_pos + 0.5 * wave_numbers[2, 1] * col_pos + phases[2])) / 3.0
    noise_part = jax.random.uniform(subkeys[2], (NX, NY), jnp.float32, -1.0, 1.0)
    return 0.5 + 0.35 * smooth + 0.15 * noise_part


def set_ends(drawn, own_key, least, high):
    longest = drawn.shape.index(max(drawn.shape))
    spots = []
    for shift in (0, 1):
        where = [jax.random.randint(jax.random.fold_in(own_key, axis), (), 0, length) for axis, length in enumerate(drawn.shape)]
        where[longest] = (where[longest] + shift) % drawn.shape[longest]
        spots.append(tuple(where))
    return drawn.at[spots[0]].set(least).at[spots[1]].set(high)


def shard_levels(key, dims, cuts, smallest, top_value):
    factor_of, own = 1.0, jax.random.fold_in(key, 6)
    for dim, shards_of in cuts:
        draws = jnp.exp(jax.random.uniform(jax.random.fold_in(own, dim), (shards_of,), jnp.float32, smallest / len(cuts), top_value / len(cuts)))
        factor_of = factor_of * jnp.repeat(draws, dims[dim] // shards_of).reshape([-1 if axis == dim else 1 for axis in range(len(dims))])
    return factor_of


def routed_block(own_key, own, number, rows, number_of, top, most, slope):
    ranking = jax.random.permutation(own_key, number_of)
    crowded, usual = load_shares(number_of, rows * top, most, slope, True), load_shares(number_of, rows * top, most, slope, False)
    places = jnp.arange(number_of)

    def named(lengths, turn):
        used = int((lengths > 0).sum())
        fixed = max(1, used // 4)
        moved = fixed + (places - fixed + turn * (used - fixed)) % max(1, number_of - fixed)
        return jnp.zeros((number_of,), jnp.int32).at[ranking[jnp.where(places < fixed, places, moved)]].set(jnp.asarray(lengths, jnp.int32))

    lengths = jnp.where(number % 4 == 0, named(crowded, number // 4), named(usual, number - number // 4 - 1))
    mixed = jax.random.permutation(jax.random.fold_in(own, 3), number_of)
    giver, taker = mixed[0:number_of // 2 * 2:2], mixed[1:number_of // 2 * 2:2]
    room = jnp.minimum(lengths[giver] - 1, most - lengths[taker]) // 2
    room = jnp.where((giver == ranking[0]) | (taker == ranking[0]) | (lengths[taker] == 0), 0, jnp.maximum(room, 0))
    moved = jax.random.randint(jax.random.fold_in(own, 4), (number_of // 2,), 0, 1 << 20) % (room + 1)
    lengths = lengths.at[giver].add(-moved).at[taker].add(moved)
    members = jnp.searchsorted(jnp.cumsum(lengths), jnp.arange(rows * top), side="right").astype(jnp.int32)
    grid = members.reshape(top, rows).T
    grid = grid[jax.random.permutation(jax.random.fold_in(own, 1), rows)]
    turn = jax.random.randint(jax.random.fold_in(own, 2), (rows, 1), 0, top)
    return jnp.take_along_axis(grid, (jnp.arange(top)[None, :] + turn) % top, axis=1)


def load_shares(count, total, limit, skew, full):
    loads = [(1 << 20) // math.isqrt(rank ** skew) + 1 for rank in range(1, count + 1)]
    largest = limit if full else min(limit, max(-(-total // count), total * loads[0] // sum(loads)))
    least = 1 if total - largest >= count - 1 else 0
    counts, surplus = [largest] + [least] * (count - 1), total - largest - least * (count - 1)
    while surplus > 0:
        candidates = [i for i in range(1, count) if counts[i] < largest] or [i for i in range(1, count) if counts[i] < limit]
        pool, budget = sum([loads[i] for i in candidates]), surplus
        for i in candidates:
            addition = min(limit - counts[i], max(1, budget * loads[i] // pool), surplus)
            counts[i] = counts[i] + addition
            surplus = surplus - addition
    return np.array(counts)


def centred(stream_key, extent, width, bound, cuts=(), kind=jnp.bfloat16):
    drawn = width * jax.random.normal(stream_key, extent, jnp.float32)
    if cuts:
        drawn = drawn * shard_levels(stream_key, extent, cuts, -0.22, 0.18)
    return jnp.clip(drawn, -bound, bound).astype(kind)


def setup_inputs(seed: int = 0) -> dict:
    arg_keys = jax.random.split(jax.random.key(seed), 9)
    fields = centred(arg_keys[0], (4, NX, NY, NZ), 1.0, 6.0, ((1, 4), (2, 4), (3, 2)), jnp.float32)
    sources = centred(arg_keys[1], (4, NX, NY, NZ), 1.0, 6.0, ((1, 4), (2, 4), (3, 2)))
    material = set_ends(jax.random.randint(arg_keys[2], (NX, NY, NZ), 0, NMAT), jax.random.fold_in(arg_keys[2], 1), 0, NMAT - 1).astype(jnp.int32)
    shift_real = jnp.clip(jax.random.uniform(arg_keys[3], (NMAT,), jnp.float32, -2.0, -0.5), -2.0, -0.5)
    shift_imag = jnp.clip(jax.random.uniform(arg_keys[4], (NMAT,), jnp.float32, 0.5, 2.0), 0.5, 2.0)
    design_share = jnp.clip(jax.random.uniform(arg_keys[5], (NMAT,), jnp.float32, 0.2, 1.0), 0.2, 1.0)
    density = draw_density(jax.random.fold_in(arg_keys[8], 71), 0)
    owner_map_keys = jax.random.split(jax.random.fold_in(arg_keys[7], 1), N_GX * N_GY * TPC // TPC)
    owner_map_turns = jax.random.permutation(jax.random.fold_in(arg_keys[7], 3), N_GX * N_GY * TPC // TPC)
    owner_map = jax.vmap(lambda own, number: routed_block(jax.random.fold_in(arg_keys[7], 2), own, number, TPC, OWNERS, 1, MOST, 2))(owner_map_keys, owner_map_turns).reshape((N_GX, N_GY, TPC, 1))
    return dict(fields=fields, sources=sources, material=material, shift_real=shift_real, shift_imag=shift_imag, design_share=design_share, density=density, owner_map=owner_map)


RELAXATION = 0.8
SHARPNESS = 8.0
THRESHOLD = 0.5
SLAB_ROWS = 8

def lookup(material, level_table):
    result = jnp.zeros(material.shape, jnp.float32)
    for level_index in range(level_table.shape[0]):
        result = result + jnp.where(material == level_index, level_table[level_index], jnp.float32(0.0))
    return result

def coef_fields(material, shift_real, shift_imag):
    diag_real = 6.0 + shift_real
    diag_imag = shift_imag
    magnitude = diag_real * diag_real + diag_imag * diag_imag
    return (lookup(material, diag_real), lookup(material, diag_imag), lookup(material, diag_real / magnitude), lookup(material, -diag_imag / magnitude))

def sweep_box(padded, source, coefficients):
    diag_real, diag_imag, inverse_real, inverse_imag = coefficients
    center = padded[:, 1:-1, 1:-1, 1:-1]
    beside = padded[:, 2:, 1:-1, 1:-1] + padded[:, :-2, 1:-1, 1:-1] + padded[:, 1:-1, 2:, 1:-1] + padded[:, 1:-1, :-2, 1:-1] + padded[:, 1:-1, 1:-1, 2:] + padded[:, 1:-1, 1:-1, :-2]
    real_part = center[0::2]
    imag_part = center[1::2]
    applied_real = diag_real * real_part - diag_imag * imag_part - beside[0::2]
    applied_imag = diag_real * imag_part + diag_imag * real_part - beside[1::2]
    residual_real = source[0::2] - applied_real
    residual_imag = source[1::2] - applied_imag
    new_real = real_part + RELAXATION * (inverse_real * residual_real - inverse_imag * residual_imag)
    new_imag = imag_part + RELAXATION * (inverse_real * residual_imag + inverse_imag * residual_real)
    return jnp.stack([new_real[0], new_imag[0], new_real[1], new_imag[1]])

def band_matrix(cell_count):
    row_index = jnp.arange(cell_count)[:, None]
    col_index = jnp.arange(cell_count + 2 * R)[None, :]
    offset = jnp.abs(col_index - R - row_index)
    weight = jnp.maximum(R + 1 - offset, 0).astype(jnp.float32)
    return weight / float((R + 1) * (R + 1))

def filter_box(padded, band_rows, band_cols):
    partial_rows = jnp.dot(band_rows, padded, precision=lax.Precision.HIGHEST, preferred_element_type=jnp.float32)
    return jnp.dot(partial_rows, band_cols.T, precision=lax.Precision.HIGHEST, preferred_element_type=jnp.float32)

def projection_slope(filtered):
    tangent = jnp.tanh(SHARPNESS * (filtered - THRESHOLD))
    scale_total = math.tanh(SHARPNESS * THRESHOLD) + math.tanh(SHARPNESS * (1.0 - THRESHOLD))
    return SHARPNESS * (1.0 - tangent * tangent) / scale_total

def select_matrix(route_list, owner_count):
    tile_count = route_list.shape[0]
    earlier = jnp.arange(tile_count)[None, :] < jnp.arange(tile_count)[:, None]
    same_owner = route_list[None, :] == route_list[:, None]
    rank_within = lax.optimization_barrier(jnp.sum(jnp.where(same_owner & earlier, 1, 0), axis=1)).astype(jnp.int32)
    slot_index = route_list.astype(jnp.int32) * MOST + rank_within
    slot_range = jnp.arange(owner_count * MOST).astype(jnp.int32)
    return jnp.where(slot_range[:, None] == slot_index[None, :], 1.0, 0.0).astype(jnp.float32)

def pack_column(tile_rows, route_list):
    selector = select_matrix(route_list, OWNERS)
    packed = jnp.dot(selector, tile_rows, precision=lax.Precision.HIGHEST, preferred_element_type=jnp.float32)
    return packed.reshape(OWNERS, MOST * TS * TS)

def reference(fields, sources, material, shift_real, shift_imag, design_share, density, owner_map):
    padded_fields = jnp.pad(fields, ((0, 0), (2, 2), (2, 2), (2, 2)))
    padded_sources = jnp.pad(sources, ((0, 0), (1, 1), (1, 1), (1, 1)))
    padded_material = jnp.pad(material, 1)
    col_position = jnp.arange(NY + 2) - 1
    col_inside = (col_position >= 0) & (col_position < NY)
    depth_position = jnp.arange(NZ + 2) - 1
    depth_inside = (depth_position >= 0) & (depth_position < NZ)

    def one_slab(slab_index):
        row_start = slab_index * SLAB_ROWS
        field_block = lax.dynamic_slice_in_dim(padded_fields, row_start, SLAB_ROWS + 4, 1)
        wide_source = lax.dynamic_slice_in_dim(padded_sources, row_start, SLAB_ROWS + 2, 1).astype(jnp.float32)
        wide_material = lax.dynamic_slice_in_dim(padded_material, row_start, SLAB_ROWS + 2, 0)
        row_position = jnp.arange(SLAB_ROWS + 2) - 1 + row_start
        row_inside = (row_position >= 0) & (row_position < NX)
        domain_mask = row_inside[:, None, None] & col_inside[None, :, None] & depth_inside[None, None, :]
        first_sweep = sweep_box(field_block, wide_source, coef_fields(wide_material, shift_real, shift_imag))
        first_sweep = first_sweep * domain_mask.astype(first_sweep.dtype)
        center_material = wide_material[1:-1, 1:-1, 1:-1]
        final_sweep = sweep_box(first_sweep, wide_source[:, 1:-1, 1:-1, 1:-1], coef_fields(center_material, shift_real, shift_imag))
        share_field = lookup(center_material, design_share)
        product = final_sweep[0] * final_sweep[2] - final_sweep[1] * final_sweep[3]
        sensitivity = lax.optimization_barrier(jnp.sum(share_field * product, axis=2)) / math.sqrt(NZ)
        return (final_sweep, sensitivity)
    finals, sensitivity = lax.map(one_slab, jnp.arange(NX // SLAB_ROWS, dtype=jnp.int32))
    fields_out = jnp.transpose(finals, (1, 0, 2, 3, 4)).reshape(4, NX, NY, NZ)
    sensitivity = sensitivity.reshape(NX, NY)
    band_rows = band_matrix(NX)
    band_cols = band_matrix(NY)
    filtered = filter_box(jnp.pad(density, R), band_rows, band_cols)
    weighted = projection_slope(filtered) * sensitivity
    plane_gradient = filter_box(jnp.pad(weighted, R), band_rows, band_cols)
    tile_rows = plane_gradient.reshape(N_GX, CX // TS, TS, N_GY, CY // TS, TS)
    tile_rows = jnp.transpose(tile_rows, (0, 3, 1, 4, 2, 5)).reshape(OWNERS, TPC, TS * TS)
    route_table = owner_map.reshape(OWNERS, TPC)
    packed = jax.vmap(pack_column)(tile_rows, route_table)
    owner_gradient = jnp.transpose(packed, (1, 0, 2))
    return (fields_out, owner_gradient)
```

```python
import functools
import math

import jax
import jax.numpy as jnp
from jax import lax
from jax.experimental import pallas as pl
from jax.experimental.pallas import tpu as pltpu
from jax.sharding import PartitionSpec as P

R = 8
TS = 8
MOST = 8
RELAXATION = 0.8
SHARPNESS = 8.0
THRESHOLD = 0.5
XB = 16
F32 = jnp.float32
BF16 = jnp.bfloat16


def lanes_of(shape):
    return lax.broadcasted_iota(jnp.int32, shape, len(shape) - 1)


def put_faces(c, x, xx, new, gs, ylo, yhi):
    ylo[c, pl.ds(xx, 1), :] = new[0:1, :]
    yhi[c, pl.ds(xx, 1), :] = new[-1:, :]
    turned = pltpu.roll(new, 2 * x + 1, 1)
    gs[c] = jnp.where(lanes_of(new.shape) // 2 == x, turned, gs[c])


def pack_kernel(v_ref, xlo_ref, xhi_ref, ylo_ref, yhi_ref, g_ref, gs, ylo, yhi):
    step, steps = pl.program_id(0), pl.num_programs(0)

    @pl.when(step == 0)
    def _():
        gs[...] = jnp.zeros_like(gs)
        xlo_ref[...] = v_ref[:, 0].astype(BF16)

    def plane(xx, carry):
        for c in range(4):
            put_faces(c, step * XB + xx, xx, v_ref[c, xx], gs, ylo, yhi)
        return carry

    lax.fori_loop(0, XB, plane, 0)
    ylo_ref[...] = ylo[...].astype(BF16)
    yhi_ref[...] = yhi[...].astype(BF16)

    @pl.when(step == steps - 1)
    def _():
        g_ref[...] = gs[...].astype(BF16)
        xhi_ref[...] = v_ref[:, XB - 1].astype(BF16)


def sweep_kernel(last, nz, *refs):
    (sr_ref, si_ref, sh_ref, v_ref, vp_ref, vn_ref, s_ref, m_ref, xl_ref, xr_ref,
     yl_ref, yr_ref, gl_ref, gr_ref) = refs[:14]
    if last:
        o_ref, sens_ref, hs, yl, yr, sens = refs[14:]
    else:
        o_ref, xlo_ref, xhi_ref, ylo_ref, yhi_ref, g_ref, hs, yl, yr, gs, ylo, yhi = refs[14:]
    step, steps = pl.program_id(0), pl.num_programs(0)
    rows, depth = v_ref.shape[2:]
    lane = lanes_of((rows, depth))

    @pl.when(step == 0)
    def _():
        if nz == 2:
            here = lax.axis_index("gz").astype(F32)
            keep_l, keep_r = here, 1.0 - here
        else:
            keep_l, keep_r = 1.0, 1.0
        for c in range(4):
            left = pltpu.roll(gl_ref[c].astype(F32), 1, 1) * keep_l
            right = pltpu.roll(gr_ref[c].astype(F32), depth - 1, 1) * keep_r
            hs[c] = jnp.where(lane % 2 == 1, left, right)
        if last:
            sens[...] = jnp.zeros_like(sens)
        else:
            gs[...] = jnp.zeros_like(gs)

    yl[...] = yl_ref[...].astype(F32)
    yr[...] = yr_ref[...].astype(F32)

    levels = sr_ref.shape[0]
    tile = (8, depth)
    wr, wi, share = [], [], []
    for m in range(levels):
        d = 6.0 + jnp.full(tile, sr_ref[m], F32)
        s = jnp.full(tile, si_ref[m], F32)
        mag = d * d + s * s
        wr.append(RELAXATION * d / mag)
        wi.append(-RELAXATION * s / mag)
        if last:
            share.append(jnp.full(tile, sh_ref[m], F32))

    def lookup(masks, table):
        out = jnp.broadcast_to(table[0], (rows // 8, 8, depth))
        for mask, value in zip(masks, table[1:]):
            out = jnp.where(mask, value, out)
        return out.reshape(rows, depth)

    row8 = lax.broadcasted_iota(jnp.int32, tile, 0)

    def plane(xx, before, after):
        x = step * XB + xx
        mat = m_ref[xx].reshape(rows // 8, 8, depth)
        masks = [mat == m for m in range(1, levels)]
        w_r, w_i = lookup(masks, wr), lookup(masks, wi)

        def drive(c):
            v = v_ref[c, xx]
            total = before(c) + after(c) + s_ref[c, xx].astype(F32)
            up = pltpu.roll(v, 1, 0)
            down = pltpu.roll(v, rows - 1, 0)
            top = jnp.where(row8 == 0, yl[c, pl.ds(xx, 1), :], up[:8])
            low = jnp.where(row8 == 7, yr[c, pl.ds(xx, 1), :], down[-8:])
            total = total + jnp.concatenate([top, up[8:]], 0) + jnp.concatenate([down[:-8], low], 0)
            h = pltpu.roll(hs[c], depth - 1 - 2 * x, 1)
            total = total + jnp.where(lane == 0, h, pltpu.roll(v, 1, 1))
            return v, total + jnp.where(lane == depth - 1, h, pltpu.roll(v, depth - 1, 1))

        news = []
        for re in (0, 2):
            v_r, t_r = drive(re)
            v_i, t_i = drive(re + 1)
            keep = 1.0 - RELAXATION
            n_r = keep * v_r + (w_r * t_r - w_i * t_i)
            n_i = keep * v_i + (w_r * t_i + w_i * t_r)
            o_ref[re, xx] = n_r
            o_ref[re + 1, xx] = n_i
            if last:
                news += [n_r, n_i]
            else:
                put_faces(re, x, xx, n_r, gs, ylo, yhi)
                put_faces(re + 1, x, xx, n_i, gs, ylo, yhi)
        if last:
            value = lookup(masks, share) * (news[0] * news[2] - news[1] * news[3])
            column = jnp.sum(value, axis=1, keepdims=True)
            sens[...] = jnp.where(lane == x, column, sens[...])

    plane(
        0,
        lambda c: jnp.where(step == 0, xl_ref[c].astype(F32), vp_ref[c, 0]),
        lambda c: v_ref[c, 1],
    )

    def middle(xx, carry):
        plane(xx, lambda c: v_ref[c, xx - 1], lambda c: v_ref[c, xx + 1])
        return carry

    lax.fori_loop(1, XB - 1, middle, 0)
    plane(
        XB - 1,
        lambda c: v_ref[c, XB - 2],
        lambda c: jnp.where(step == steps - 1, xr_ref[c].astype(F32), vn_ref[c, 0]),
    )
    if not last:
        ylo_ref[...] = ylo[...].astype(BF16)
        yhi_ref[...] = yhi[...].astype(BF16)

        @pl.when(step == 0)
        def _():
            xlo_ref[...] = o_ref[:, 0].astype(BF16)

    @pl.when(step == steps - 1)
    def _():
        if last:
            half = rows // 2
            both = pltpu.roll(sens[half:], depth // 2, 1)
            sens_ref[...] = jnp.where(lane[:half] < depth // 2, sens[:half], both)
        else:
            g_ref[...] = gs[...].astype(BF16)
            xhi_ref[...] = o_ref[:, XB - 1].astype(BF16)


def whole(shape):
    return pl.BlockSpec(shape, lambda i: (0,) * len(shape))


SMEM_SPEC = pl.BlockSpec(memory_space=pltpu.SMEM)


def face_outs(nx, ny, nz):
    shapes = [(4, ny, nz), (4, ny, nz), (4, nx, nz), (4, nx, nz), (4, ny, nz)]
    y_spec = pl.BlockSpec((4, XB, nz), lambda i: (0, i, 0))
    specs = [whole((4, ny, nz)), whole((4, ny, nz)), y_spec, y_spec, whole((4, ny, nz))]
    return [jax.ShapeDtypeStruct(s, BF16) for s in shapes], specs


def face_scratch(ny, nz):
    return [
        pltpu.VMEM((4, ny, nz), F32),
        pltpu.VMEM((4, XB, nz), F32),
        pltpu.VMEM((4, XB, nz), F32),
    ]


def pack(fields):
    _, nx, ny, nz = fields.shape
    shapes, specs = face_outs(nx, ny, nz)
    return pl.pallas_call(
        pack_kernel,
        grid=(nx // XB,),
        in_specs=[pl.BlockSpec((4, XB, ny, nz), lambda i: (0, i, 0, 0))],
        out_specs=specs,
        out_shape=shapes,
        scratch_shapes=face_scratch(ny, nz),
        compiler_params=pltpu.CompilerParams(vmem_limit_bytes=24 << 20),
        cost_estimate=pl.CostEstimate(
            flops=fields.size * 4, bytes_accessed=fields.size * 4, transcendentals=0
        ),
        name="pack_faces",
    )(fields)


def sweep(last, tables, current, sources, material, halos):
    _, nx, ny, nz = current.shape
    steps = nx // XB
    block = pl.BlockSpec((4, XB, ny, nz), lambda i: (0, i, 0, 0))
    y_spec = pl.BlockSpec((4, XB, nz), lambda i: (0, i, 0))
    x_spec = whole((4, ny, nz))
    in_specs = [SMEM_SPEC] * 3 + [
        block,
        pl.BlockSpec((4, 1, ny, nz), lambda i: (0, jnp.maximum(i * XB - 1, 0), 0, 0)),
        pl.BlockSpec((4, 1, ny, nz), lambda i: (0, jnp.minimum(i * XB + XB, nx - 1), 0, 0)),
        block,
        pl.BlockSpec((XB, ny, nz), lambda i: (i, 0, 0)),
        x_spec,
        x_spec,
        y_spec,
        y_spec,
        x_spec,
        x_spec,
    ]
    scratch = [
        pltpu.VMEM((4, ny, nz), F32),
        pltpu.VMEM((4, XB, nz), F32),
        pltpu.VMEM((4, XB, nz), F32),
    ]
    shapes, specs = [jax.ShapeDtypeStruct(current.shape, F32)], [block]
    if last:
        shapes.append(jax.ShapeDtypeStruct((ny // 2, nz), F32))
        specs.append(whole((ny // 2, nz)))
        scratch.append(pltpu.VMEM((ny, nz), F32))
    else:
        more_shapes, more_specs = face_outs(nx, ny, nz)
        shapes += more_shapes
        specs += more_specs
        scratch += face_scratch(ny, nz)
    return pl.pallas_call(
        functools.partial(sweep_kernel, last, lax.axis_size("gz")),
        grid=(steps,),
        in_specs=in_specs,
        out_specs=specs,
        out_shape=shapes,
        scratch_shapes=scratch,
        compiler_params=pltpu.CompilerParams(vmem_limit_bytes=32 << 20),
        cost_estimate=pl.CostEstimate(
            flops=current.size * 24, bytes_accessed=current.size * 11, transcendentals=0
        ),
        name="sweep_last" if last else "sweep_first",
    )(*tables, current, current, current, sources, material, *halos)


def exchange(xlo, xhi, ylo, yhi, g):
    out = []
    for axis, low, high in (("gx", xlo, xhi), ("gy", ylo, yhi)):
        count = lax.axis_size(axis)
        up = [(i, i + 1) for i in range(count - 1)]
        out.append(lax.ppermute(high, axis, up))
        out.append(lax.ppermute(low, axis, [(j, i) for i, j in up]))
    count = lax.axis_size("gz")
    if count == 2:
        other = lax.ppermute(g, "gz", [(0, 1), (1, 0)])
        return out + [other, other]
    up = [(i, i + 1) for i in range(count - 1)]
    return out + [lax.ppermute(g, "gz", up), lax.ppermute(g, "gz", [(j, i) for i, j in up])]


def split(value):
    high = value.astype(BF16)
    return high, (value - high.astype(F32)).astype(BF16)


def mm(a, b):
    return lax.dot_general(a, b, (((1,), (0,)), ((), ())), preferred_element_type=F32)


def plane_kernel(ngx, ngy, scale, me_ref, sens_ref, den_ref, own_ref, out_ref, w_ref, d_ref):
    cells = 64
    nx, ny = ngx * cells, ngy * cells
    columns = ngx * ngy
    half = cells // 2
    for cx in range(ngx):
        for cy in range(ngy):
            c = cx * ngy + cy
            for part in range(2):
                w_ref[pl.ds(cy * cells + part * half, half), pl.ds(cx * cells, cells)] = sens_ref[
                    c, :, pl.ds(part * cells, cells)
                ]
            d_ref[pl.ds(cx * cells, cells), pl.ds(cy * cells, cells)] = den_ref[c]

    def band(n):
        i = lax.broadcasted_iota(jnp.int32, (n, n), 0)
        j = lax.broadcasted_iota(jnp.int32, (n, n), 1)
        return jnp.maximum(R + 1 - jnp.abs(i - j), 0).astype(F32).astype(BF16)

    band_x, band_y = band(nx), band(ny)
    unit = float((R + 1) ** 4)

    def twice(value, right):
        high, low = split(value)
        return mm(high, right) + mm(low, right)

    def left_twice(left, value):
        high, low = split(value)
        return mm(left, high) + mm(left, low)

    density = jnp.transpose(d_ref[...], (1, 0))
    filtered = left_twice(band_y, twice(density, band_x)) / unit
    tangent = jnp.tanh(SHARPNESS * (filtered - THRESHOLD))
    total = math.tanh(SHARPNESS * THRESHOLD) + math.tanh(SHARPNESS * (1.0 - THRESHOLD))
    slope = SHARPNESS * (1.0 - tangent * tangent) / total
    weighted = twice(slope * w_ref[...] * scale, band_x)

    tiles = own_ref.shape[1]
    mine = own_ref[...] == me_ref[0].astype(F32)
    flag = jnp.where(mine, 1.0, 0.0)
    a = lax.broadcasted_iota(jnp.int32, (tiles, tiles), 0)
    b = lax.broadcasted_iota(jnp.int32, (tiles, tiles), 1)
    rank = mm(flag.astype(BF16), jnp.where(a < b, 1.0, 0.0).astype(BF16))
    number = lanes_of((columns, tiles))
    column = lax.broadcasted_iota(jnp.int32, (columns, 1), 0)
    rows, blocks = [], []
    for k in range(MOST):
        chosen = mine & (rank == float(k))
        tile = jnp.sum(jnp.where(chosen, number, 0), axis=1, keepdims=True)
        there = jnp.sum(jnp.where(chosen, 1, 0), axis=1, keepdims=True)
        rows.append((column % ngy) * cells + (tile % (cells // TS)) * TS)
        block = (column // ngy) * (cells // TS) + tile // (cells // TS)
        blocks.append(jnp.where(there > 0, block, -1))
    row = jnp.concatenate(rows, 0)
    block = jnp.concatenate(blocks, 0)
    slots = MOST * columns
    across = lax.broadcasted_iota(jnp.int32, (slots, ny), 1)
    lefts = [
        jnp.maximum(R + 1 - jnp.abs(row + j - across), 0).astype(F32).astype(BF16)
        for j in range(TS)
    ]
    lines = left_twice(jnp.concatenate(lefts, 0), weighted)
    keep = lanes_of((slots, nx)) // TS == block
    from_x = lax.broadcasted_iota(jnp.int32, (nx, TS * TS), 0) % TS
    to_q = lanes_of((nx, TS * TS))
    out = jnp.zeros((slots, TS * TS), F32)
    for j in range(TS):
        fold = jnp.where(to_q == from_x * TS + j, 1.0, 0.0).astype(BF16)
        out = out + twice(jnp.where(keep, lines[j * slots : (j + 1) * slots], 0.0), fold)
    out = out / unit
    for k in range(MOST):
        out_ref[0, :, pl.ds(k * TS * TS, TS * TS)] = out[k * columns : (k + 1) * columns]


def on_device(fields, sources, material, shift_real, shift_imag, design_share, density, owner_map):
    ngx, ngy, ngz = (lax.axis_size(a) for a in ("gx", "gy", "gz"))
    columns = ngx * ngy
    cells = density.shape[0]
    tables = (shift_real, shift_imag, design_share)
    known = jnp.concatenate([density, owner_map.reshape(1, -1).astype(F32)], 0)
    known = lax.all_gather(known, ("gx", "gy"))
    halos = exchange(*pack(fields))
    middle, *faces = sweep(False, tables, fields, sources, material, halos)
    final, partial = sweep(True, tables, middle, sources, material, exchange(*faces))
    partial = jnp.sum(lax.all_gather(partial, "gz"), 0)
    copies = jnp.broadcast_to(partial[None], (columns, *partial.shape))
    plane = lax.all_to_all(copies, ("gx", "gy"), split_axis=0, concat_axis=0)
    me = (lax.axis_index("gx") * ngy + lax.axis_index("gy")).reshape(1)
    vmem = pl.BlockSpec(memory_space=pltpu.VMEM)
    owned = pl.pallas_call(
        functools.partial(
            plane_kernel, ngx, ngy, 1.0 / math.sqrt(material.shape[2] * ngz)
        ),
        in_specs=[SMEM_SPEC, vmem, vmem, vmem],
        out_specs=vmem,
        out_shape=jax.ShapeDtypeStruct((1, columns, MOST * TS * TS), F32),
        scratch_shapes=[
            pltpu.VMEM((ngy * cells, ngx * cells), F32),
            pltpu.VMEM((ngx * cells, ngy * cells), F32),
        ],
        compiler_params=pltpu.CompilerParams(vmem_limit_bytes=32 << 20),
        name="plane",
    )(me, plane, known[:, :cells], known[:, cells])
    return (final, owned)


def solution(mesh):
    placed = (
        P(None, "gx", "gy", "gz"),
        P(None, "gx", "gy", "gz"),
        P("gx", "gy", "gz"),
        P(),
        P(),
        P(),
        P("gx", "gy"),
        P("gx", "gy", None, None),
    )
    return jax.shard_map(
        on_device,
        mesh=mesh,
        in_specs=placed,
        out_specs=(P(None, "gx", "gy", "gz"), P(("gx", "gy"), None, None)),
        check_vma=False,
    )
```

```python
import functools
import math

import jax
import jax.numpy as jnp
from jax import lax
from jax.experimental import pallas as pl
from jax.experimental.pallas import tpu as pltpu
from jax.sharding import PartitionSpec as P

R = 8
TS = 8
MOST = 8
RELAXATION = 0.8
SHARPNESS = 8.0
THRESHOLD = 0.5
XB = 16
PB = 8
F32 = jnp.float32
BF16 = jnp.bfloat16


def lanes_of(shape):
    return lax.broadcasted_iota(jnp.int32, shape, len(shape) - 1)


def put_faces(first, xx, ref, ends, gs, ylo, yhi):
    rows, depth = ref.shape[2:]
    value = ref[:, pl.ds(xx, PB)]
    for p in range(PB):
        for c in range(4):
            ylo[c, pl.ds(xx + p, 1), :] = value[c, p, 0:1, :]
            yhi[c, pl.ds(xx + p, 1), :] = value[c, p, rows - 1 :, :]
    picked = mm(value.astype(BF16).reshape(4 * PB * rows, depth), ends).reshape(4, PB, rows, depth)
    pair = lanes_of((rows, depth)) // 2
    for c in range(4):
        g = gs[c]
        for p in range(PB):
            g = jnp.where(pair == first + xx + p, picked[c, p], g)
        gs[c] = g


def ends_matrix(depth):
    z = lax.broadcasted_iota(jnp.int32, (depth, depth), 0)
    j = lax.broadcasted_iota(jnp.int32, (depth, depth), 1)
    even = (z == 0) & (j % 2 == 0)
    odd = (z == depth - 1) & (j % 2 == 1)
    return jnp.where(even | odd, 1.0, 0.0).astype(BF16)


def beside_matrix(depth):
    z = lax.broadcasted_iota(jnp.int32, (depth, depth), 0)
    j = lax.broadcasted_iota(jnp.int32, (depth, depth), 1)
    return jnp.where(jnp.abs(z - j) == 1, 1.0, 0.0).astype(BF16)


def halo_matrix(depth):
    j = lax.broadcasted_iota(jnp.int32, (depth, depth), 0)
    z = lax.broadcasted_iota(jnp.int32, (depth, depth), 1)
    even = (z == 0) & (j % 2 == 0)
    odd = (z == depth - 1) & (j % 2 == 1)
    return jnp.where(even | odd, 1.0, 0.0).astype(BF16)


def split(value):
    high = value.astype(BF16)
    return high, (value - high.astype(F32)).astype(BF16)


def mm(a, b):
    return lax.dot_general(a, b, (((1,), (0,)), ((), ())), preferred_element_type=F32)


def pack_kernel(v_ref, xlo_ref, xhi_ref, ylo_ref, yhi_ref, g_ref, gs, ylo, yhi, ends):
    step, steps = pl.program_id(0), pl.num_programs(0)

    @pl.when(step == 0)
    def _():
        gs[...] = jnp.zeros_like(gs)
        ends[...] = ends_matrix(v_ref.shape[3])
        xlo_ref[...] = v_ref[:, 0].astype(BF16)

    def planes(i, carry):
        put_faces(step * XB, i * PB, v_ref, ends[...], gs, ylo, yhi)
        return carry

    lax.fori_loop(0, XB // PB, planes, 0)
    ylo_ref[...] = ylo[...].astype(BF16)
    yhi_ref[...] = yhi[...].astype(BF16)

    @pl.when(step == steps - 1)
    def _():
        g_ref[...] = gs[...].astype(BF16)
        xhi_ref[...] = v_ref[:, XB - 1].astype(BF16)


def sweep_kernel(last, nz, *refs):
    (sr_ref, si_ref, sh_ref, v_ref, vp_ref, vn_ref, s_ref, m_ref, xl_ref, xr_ref,
     yl_ref, yr_ref, gl_ref, gr_ref) = refs[:14]
    if last:
        o_ref, sens_ref, hs, yl, yr, near, far, zt, sens, value = refs[14:]
    else:
        o_ref, xlo_ref, xhi_ref, ylo_ref, yhi_ref, g_ref, hs, yl, yr, near, far, zt, gs, ylo, yhi, ends = refs[14:]
    step, steps = pl.program_id(0), pl.num_programs(0)
    rows, depth = v_ref.shape[2:]
    lane = lanes_of((rows, depth))

    @pl.when(step == 0)
    def _():
        if nz == 2:
            here = lax.axis_index("gz").astype(F32)
            keep_l, keep_r = here, 1.0 - here
        else:
            keep_l, keep_r = 1.0, 1.0
        for c in range(4):
            left = pltpu.roll(gl_ref[c].astype(F32), depth - 1, 1) * keep_l
            right = pltpu.roll(gr_ref[c].astype(F32), 1, 1) * keep_r
            hs[c] = jnp.where(lane % 2 == 0, left, right)
        near[...] = jnp.concatenate([beside_matrix(depth)] * 2, 0)
        far[...] = halo_matrix(depth)
        if last:
            sens[...] = jnp.zeros_like(sens)
        else:
            gs[...] = jnp.zeros_like(gs)
            ends[...] = ends_matrix(depth)

    yl[...] = yl_ref[...].astype(F32)
    yr[...] = yr_ref[...].astype(F32)

    levels = sr_ref.shape[0]
    tile = (8, depth)
    wr, wi, share = [], [], []
    for m in range(levels):
        d = 6.0 + jnp.full(tile, sr_ref[m], F32)
        s = jnp.full(tile, si_ref[m], F32)
        mag = d * d + s * s
        wr.append(RELAXATION * d / mag)
        wi.append(-RELAXATION * s / mag)
        if last:
            share.append(jnp.full(tile, sh_ref[m], F32))

    def lookup(masks, table):
        out = jnp.broadcast_to(table[0], (rows // 8, 8, depth))
        for mask, value in zip(masks, table[1:]):
            out = jnp.where(mask, value, out)
        return out.reshape(rows, depth)

    row8 = lax.broadcasted_iota(jnp.int32, tile, 0)

    def along_z(xx):
        v = v_ref[:, pl.ds(xx, PB)].reshape(4 * PB * rows, depth)
        masked = [
            jnp.where(lane // 2 == step * XB + xx + p, hs[c], 0.0).astype(BF16)
            for c in range(4)
            for p in range(PB)
        ]
        out = mm(jnp.concatenate(split(v), 1), near[...]) + mm(jnp.concatenate(masked, 0), far[...])
        zt[...] = out.reshape(4, PB, rows, depth)

    def plane(xx, slot, before, after):
        x = step * XB + xx
        mat = m_ref[xx].reshape(rows // 8, 8, depth)
        masks = [mat == m for m in range(1, levels)]
        w_r, w_i = lookup(masks, wr), lookup(masks, wi)

        def drive(c):
            v = v_ref[c, xx]
            total = before(c) + after(c) + s_ref[c, xx].astype(F32)
            up = pltpu.roll(v, 1, 0)
            down = pltpu.roll(v, rows - 1, 0)
            top = jnp.where(row8 == 0, yl[c, pl.ds(xx, 1), :], up[:8])
            low = jnp.where(row8 == 7, yr[c, pl.ds(xx, 1), :], down[-8:])
            total = total + jnp.concatenate([top, up[8:]], 0) + jnp.concatenate([down[:-8], low], 0)
            return v, total + zt[c, slot]

        news = []
        for re in (0, 2):
            v_r, t_r = drive(re)
            v_i, t_i = drive(re + 1)
            keep = 1.0 - RELAXATION
            n_r = keep * v_r + (w_r * t_r - w_i * t_i)
            n_i = keep * v_i + (w_r * t_i + w_i * t_r)
            o_ref[re, xx] = n_r
            o_ref[re + 1, xx] = n_i
            news += [n_r, n_i]
        if last:
            value[slot] = lookup(masks, share) * (news[0] * news[2] - news[1] * news[3])

    def before(xx):
        return lambda c: v_ref[c, xx - 1]

    def after(xx):
        return lambda c: v_ref[c, xx + 1]

    def first(c):
        return jnp.where(step == 0, xl_ref[c].astype(F32), vp_ref[c, 0])

    def final(c):
        return jnp.where(step == steps - 1, xr_ref[c].astype(F32), vn_ref[c, 0])

    def planes(xx, start=False, end=False):
        along_z(xx)
        for p in range(PB):
            plane(
                xx + p,
                p,
                first if start and p == 0 else before(xx + p),
                final if end and p == PB - 1 else after(xx + p),
            )
        if last:
            ones = jnp.ones((2 * depth, depth), BF16)
            parts = split(value[...].reshape(PB * rows, depth))
            sums = mm(jnp.concatenate(parts, 1), ones).reshape(PB, rows, depth)
            held = sens[...]
            for p in range(PB):
                held = jnp.where(lane == step * XB + xx + p, sums[p], held)
            sens[...] = held
        else:
            put_faces(step * XB, xx, o_ref, ends[...], gs, ylo, yhi)

    def middle(i, carry):
        planes(i * PB)
        return carry

    planes(0, start=True)
    lax.fori_loop(1, XB // PB - 1, middle, 0)
    planes(XB - PB, end=True)
    if not last:
        ylo_ref[...] = ylo[...].astype(BF16)
        yhi_ref[...] = yhi[...].astype(BF16)

        @pl.when(step == 0)
        def _():
            xlo_ref[...] = o_ref[:, 0].astype(BF16)

    @pl.when(step == steps - 1)
    def _():
        if last:
            half = rows // 2
            both = pltpu.roll(sens[half:], depth // 2, 1)
            sens_ref[...] = jnp.where(lane[:half] < depth // 2, sens[:half], both)
        else:
            g_ref[...] = gs[...].astype(BF16)
            xhi_ref[...] = o_ref[:, XB - 1].astype(BF16)


def whole(shape):
    return pl.BlockSpec(shape, lambda i: (0,) * len(shape))


SMEM_SPEC = pl.BlockSpec(memory_space=pltpu.SMEM)


def face_outs(nx, ny, nz):
    shapes = [(4, ny, nz), (4, ny, nz), (4, nx, nz), (4, nx, nz), (4, ny, nz)]
    y_spec = pl.BlockSpec((4, XB, nz), lambda i: (0, i, 0))
    specs = [whole((4, ny, nz)), whole((4, ny, nz)), y_spec, y_spec, whole((4, ny, nz))]
    return [jax.ShapeDtypeStruct(s, BF16) for s in shapes], specs


def face_scratch(ny, nz):
    return [
        pltpu.VMEM((4, ny, nz), F32),
        pltpu.VMEM((4, XB, nz), F32),
        pltpu.VMEM((4, XB, nz), F32),
        pltpu.VMEM((nz, nz), BF16),
    ]


def pack(fields):
    _, nx, ny, nz = fields.shape
    shapes, specs = face_outs(nx, ny, nz)
    return pl.pallas_call(
        pack_kernel,
        grid=(nx // XB,),
        in_specs=[pl.BlockSpec((4, XB, ny, nz), lambda i: (0, i, 0, 0))],
        out_specs=specs,
        out_shape=shapes,
        scratch_shapes=face_scratch(ny, nz),
        compiler_params=pltpu.CompilerParams(vmem_limit_bytes=24 << 20),
        cost_estimate=pl.CostEstimate(
            flops=fields.size * 4, bytes_accessed=fields.size * 4, transcendentals=0
        ),
        name="pack_faces",
    )(fields)


def sweep(last, tables, current, sources, material, halos):
    _, nx, ny, nz = current.shape
    steps = nx // XB
    block = pl.BlockSpec((4, XB, ny, nz), lambda i: (0, i, 0, 0))
    y_spec = pl.BlockSpec((4, XB, nz), lambda i: (0, i, 0))
    x_spec = whole((4, ny, nz))
    in_specs = [SMEM_SPEC] * 3 + [
        block,
        pl.BlockSpec((4, 1, ny, nz), lambda i: (0, jnp.maximum(i * XB - 1, 0), 0, 0)),
        pl.BlockSpec((4, 1, ny, nz), lambda i: (0, jnp.minimum(i * XB + XB, nx - 1), 0, 0)),
        block,
        pl.BlockSpec((XB, ny, nz), lambda i: (i, 0, 0)),
        x_spec,
        x_spec,
        y_spec,
        y_spec,
        x_spec,
        x_spec,
    ]
    scratch = [
        pltpu.VMEM((4, ny, nz), F32),
        pltpu.VMEM((4, XB, nz), F32),
        pltpu.VMEM((4, XB, nz), F32),
        pltpu.VMEM((2 * nz, nz), BF16),
        pltpu.VMEM((nz, nz), BF16),
        pltpu.VMEM((4, PB, ny, nz), F32),
    ]
    shapes, specs = [jax.ShapeDtypeStruct(current.shape, F32)], [block]
    if last:
        shapes.append(jax.ShapeDtypeStruct((ny // 2, nz), F32))
        specs.append(whole((ny // 2, nz)))
        scratch += [pltpu.VMEM((ny, nz), F32), pltpu.VMEM((PB, ny, nz), F32)]
    else:
        more_shapes, more_specs = face_outs(nx, ny, nz)
        shapes += more_shapes
        specs += more_specs
        scratch += face_scratch(ny, nz)
    return pl.pallas_call(
        functools.partial(sweep_kernel, last, lax.axis_size("gz")),
        grid=(steps,),
        in_specs=in_specs,
        out_specs=specs,
        out_shape=shapes,
        scratch_shapes=scratch,
        compiler_params=pltpu.CompilerParams(vmem_limit_bytes=32 << 20),
        cost_estimate=pl.CostEstimate(
            flops=current.size * 24, bytes_accessed=current.size * 11, transcendentals=0
        ),
        name="sweep_last" if last else "sweep_first",
    )(*tables, current, current, current, sources, material, *halos)


def exchange(xlo, xhi, ylo, yhi, g):
    out = []
    for axis, low, high in (("gx", xlo, xhi), ("gy", ylo, yhi)):
        count = lax.axis_size(axis)
        up = [(i, i + 1) for i in range(count - 1)]
        out.append(lax.ppermute(high, axis, up))
        out.append(lax.ppermute(low, axis, [(j, i) for i, j in up]))
    count = lax.axis_size("gz")
    if count == 2:
        other = lax.ppermute(g, "gz", [(0, 1), (1, 0)])
        return out + [other, other]
    up = [(i, i + 1) for i in range(count - 1)]
    return out + [lax.ppermute(g, "gz", up), lax.ppermute(g, "gz", [(j, i) for i, j in up])]


def plane_kernel(ngx, ngy, scale, me_ref, got_ref, out_ref, w_ref, d_ref):
    cells = 64
    nx, ny = ngx * cells, ngy * cells
    columns = ngx * ngy
    half = cells // 2
    for cx in range(ngx):
        for cy in range(ngy):
            c = cx * ngy + cy
            for part in range(2):
                lanes = pl.ds(part * cells, cells)
                w_ref[pl.ds(cy * cells + part * half, half), pl.ds(cx * cells, cells)] = got_ref[
                    c, pl.ds(0, half), lanes
                ]
                d_ref[pl.ds(cx * cells + part * half, half), pl.ds(cy * cells, cells)] = got_ref[
                    c, pl.ds(half, half), lanes
                ]

    def band(n):
        i = lax.broadcasted_iota(jnp.int32, (n, n), 0)
        j = lax.broadcasted_iota(jnp.int32, (n, n), 1)
        return jnp.maximum(R + 1 - jnp.abs(i - j), 0).astype(F32).astype(BF16)

    band_x, band_y = band(nx), band(ny)
    unit = float((R + 1) ** 4)

    def twice(value, right):
        high, low = split(value)
        return mm(high, right) + mm(low, right)

    def left_twice(left, value):
        high, low = split(value)
        return mm(left, high) + mm(left, low)

    density = jnp.transpose(d_ref[...], (1, 0))
    filtered = left_twice(band_y, twice(density, band_x)) / unit
    tangent = jnp.tanh(SHARPNESS * (filtered - THRESHOLD))
    total = math.tanh(SHARPNESS * THRESHOLD) + math.tanh(SHARPNESS * (1.0 - THRESHOLD))
    slope = SHARPNESS * (1.0 - tangent * tangent) / total
    weighted = twice(slope * w_ref[...] * scale, band_x)

    tiles = cells
    owner = jnp.concatenate([got_ref[c, pl.ds(2 * half, 1), pl.ds(0, tiles)] for c in range(columns)], 0)
    mine = owner == me_ref[0].astype(F32)
    flag = jnp.where(mine, 1.0, 0.0)
    a = lax.broadcasted_iota(jnp.int32, (tiles, tiles), 0)
    b = lax.broadcasted_iota(jnp.int32, (tiles, tiles), 1)
    rank = mm(flag.astype(BF16), jnp.where(a < b, 1.0, 0.0).astype(BF16))
    number = lanes_of((columns, tiles))
    column = lax.broadcasted_iota(jnp.int32, (columns, 1), 0)
    rows, blocks = [], []
    for k in range(MOST):
        chosen = mine & (rank == float(k))
        tile = jnp.sum(jnp.where(chosen, number, 0), axis=1, keepdims=True)
        there = jnp.sum(jnp.where(chosen, 1, 0), axis=1, keepdims=True)
        rows.append((column % ngy) * cells + (tile % (cells // TS)) * TS)
        block = (column // ngy) * (cells // TS) + tile // (cells // TS)
        blocks.append(jnp.where(there > 0, block, -1))
    row = jnp.concatenate(rows, 0)
    block = jnp.concatenate(blocks, 0)
    slots = MOST * columns
    across = lax.broadcasted_iota(jnp.int32, (slots, ny), 1)
    lefts = [
        jnp.maximum(R + 1 - jnp.abs(row + j - across), 0).astype(F32).astype(BF16)
        for j in range(TS)
    ]
    lines = left_twice(jnp.concatenate(lefts, 0), weighted)
    keep = lanes_of((slots, nx)) // TS == block
    from_x = lax.broadcasted_iota(jnp.int32, (nx, TS * TS), 0) % TS
    to_q = lanes_of((nx, TS * TS))
    out = jnp.zeros((slots, TS * TS), F32)
    for j in range(TS):
        fold = jnp.where(to_q == from_x * TS + j, 1.0, 0.0).astype(BF16)
        out = out + twice(jnp.where(keep, lines[j * slots : (j + 1) * slots], 0.0), fold)
    out = out / unit
    for k in range(MOST):
        out_ref[0, :, pl.ds(k * TS * TS, TS * TS)] = out[k * columns : (k + 1) * columns]


def on_device(fields, sources, material, shift_real, shift_imag, design_share, density, owner_map):
    ngx, ngy, ngz = (lax.axis_size(a) for a in ("gx", "gy", "gz"))
    columns = ngx * ngy
    cells = density.shape[0]
    tables = (shift_real, shift_imag, design_share)
    half = cells // 2
    packed = jnp.concatenate([density[:half], density[half:]], 1)
    owners = jnp.pad(owner_map.reshape(1, -1).astype(F32), ((0, 7), (0, cells)))
    halos = exchange(*pack(fields))
    middle, *faces = sweep(False, tables, fields, sources, material, halos)
    final, partial = sweep(True, tables, middle, sources, material, exchange(*faces))
    partial = jnp.sum(lax.all_gather(partial, "gz"), 0)
    partial = jnp.concatenate([partial, packed, owners], 0)
    copies = jnp.broadcast_to(partial[None], (columns, *partial.shape))
    plane = lax.all_to_all(copies, ("gx", "gy"), split_axis=0, concat_axis=0)
    me = (lax.axis_index("gx") * ngy + lax.axis_index("gy")).reshape(1)
    vmem = pl.BlockSpec(memory_space=pltpu.VMEM)
    owned = pl.pallas_call(
        functools.partial(
            plane_kernel, ngx, ngy, 1.0 / math.sqrt(material.shape[2] * ngz)
        ),
        in_specs=[SMEM_SPEC, vmem],
        out_specs=vmem,
        out_shape=jax.ShapeDtypeStruct((1, columns, MOST * TS * TS), F32),
        scratch_shapes=[
            pltpu.VMEM((ngy * cells, ngx * cells), F32),
            pltpu.VMEM((ngx * cells, ngy * cells), F32),
        ],
        compiler_params=pltpu.CompilerParams(vmem_limit_bytes=32 << 20),
        name="plane",
    )(me, plane)
    return (final, owned)


def solution(mesh):
    placed = (
        P(None, "gx", "gy", "gz"),
        P(None, "gx", "gy", "gz"),
        P("gx", "gy", "gz"),
        P(),
        P(),
        P(),
        P("gx", "gy"),
        P("gx", "gy", None, None),
    )
    return jax.shard_map(
        on_device,
        mesh=mesh,
        in_specs=placed,
        out_specs=(P(None, "gx", "gy", "gz"), P(("gx", "gy"), None, None)),
        check_vma=False,
    )
```

```python
import functools
import math

import jax
import jax.numpy as jnp
from jax import lax
from jax.experimental import pallas as pl
from jax.experimental.pallas import tpu as pltpu
from jax.sharding import PartitionSpec as P

R = 8
TS = 8
MOST = 8
RELAXATION = 0.8
SHARPNESS = 8.0
THRESHOLD = 0.5
PB = 8
F32 = jnp.float32
BF16 = jnp.bfloat16


def lanes_of(shape):
    return lax.broadcasted_iota(jnp.int32, shape, len(shape) - 1)


def ends_matrix(depth):
    z = lax.broadcasted_iota(jnp.int32, (depth, depth), 0)
    j = lax.broadcasted_iota(jnp.int32, (depth, depth), 1)
    even = (z == 0) & (j % 2 == 0)
    odd = (z == depth - 1) & (j % 2 == 1)
    return jnp.where(even | odd, 1.0, 0.0).astype(BF16)


def beside_matrix(depth):
    z = lax.broadcasted_iota(jnp.int32, (depth, depth), 0)
    j = lax.broadcasted_iota(jnp.int32, (depth, depth), 1)
    return jnp.where(jnp.abs(z - j) == 1, 1.0, 0.0).astype(BF16)


def halo_matrix(depth):
    j = lax.broadcasted_iota(jnp.int32, (depth, depth), 0)
    z = lax.broadcasted_iota(jnp.int32, (depth, depth), 1)
    even = (z == 0) & (j % 2 == 0)
    odd = (z == depth - 1) & (j % 2 == 1)
    return jnp.where(even | odd, 1.0, 0.0).astype(BF16)


def split(value):
    high = value.astype(BF16)
    return high, (value - high.astype(F32)).astype(BF16)


def mm(a, b):
    return lax.dot_general(a, b, (((1,), (0,)), ((), ())), preferred_element_type=F32)


def put_faces(first, ref, start, ends, gs, ylo, yhi):
    rows, depth = ref.shape[2:]
    value = ref[:, pl.ds(start, PB)]
    for p in range(PB):
        for c in range(4):
            ylo[c, pl.ds(first + p, 1), :] = value[c, p, 0:1, :]
            yhi[c, pl.ds(first + p, 1), :] = value[c, p, rows - 1 :, :]
    picked = mm(value.astype(BF16).reshape(4 * PB * rows, depth), ends).reshape(4, PB, rows, depth)
    pair = lanes_of((rows, depth)) // 2
    for c in range(4):
        g = gs[c]
        for p in range(PB):
            g = jnp.where(pair == first + p, picked[c, p], g)
        gs[c] = g


def put_plane(out_ref, value):
    rows = value.shape[1]
    out_ref[: 4 * rows] = value.astype(BF16).reshape(4 * rows, value.shape[2])


def paired(value):
    high = value.astype(BF16).astype(F32)
    return jnp.concatenate([high, value - high], 1)


def pack_kernel(v_ref, d_ref, xlo_ref, xhi_ref, ylo_ref, yhi_ref, g_ref, gs, ylo, yhi, ends):
    step, steps = pl.program_id(0), pl.num_programs(0)
    rows, depth = v_ref.shape[2:]

    @pl.when(step == 0)
    def _():
        gs[...] = jnp.zeros_like(gs)
        ends[...] = ends_matrix(depth)
        put_plane(xlo_ref, v_ref[:, 0])
        cells = d_ref.shape[0]
        none = jnp.zeros((R, depth), F32)
        for out_ref, start in ((xlo_ref, 0), (xhi_ref, cells - R)):
            strip = jnp.concatenate([paired(d_ref[start : start + R, :]), none], 0)
            out_ref[4 * rows :] = strip.astype(BF16)

    put_faces(step * PB, v_ref, 0, ends[...], gs, ylo, yhi)

    @pl.when(step == steps - 1)
    def _():
        g_ref[...] = gs[...].astype(BF16)
        ylo_ref[...] = ylo[...].astype(BF16)
        yhi_ref[...] = yhi[...].astype(BF16)
        put_plane(xhi_ref, v_ref[:, PB - 1])


def sweep_kernel(last, nz, scale, *refs):
    sr_ref, si_ref, v_ref, s_ref, m_ref, xl_ref, xr_ref, yl_ref, yr_ref, gl_ref, gr_ref = refs[:11]
    if last:
        sh_ref, mid_ref, own_ref, o_ref, sens_ref = refs[11:16]
        hs, yl, yr, near, far, zt, sens, value, news, sems = refs[16:]
    else:
        d_ref, o_ref, xlo_ref, xhi_ref, ylo_ref, yhi_ref, g_ref = refs[11:18]
        hs, yl, yr, near, far, zt, gs, ylo, yhi, ends = refs[18:]
    planes_here, rows, depth = v_ref.shape[1:]
    lane = lanes_of((rows, depth))

    if nz == 2:
        here = lax.axis_index("gz").astype(F32)
        keep_l, keep_r = here, 1.0 - here
    else:
        keep_l, keep_r = 1.0, 1.0
    for c in range(4):
        left = pltpu.roll(gl_ref[c].astype(F32), depth - 1, 1) * keep_l
        right = pltpu.roll(gr_ref[c].astype(F32), 1, 1) * keep_r
        hs[c] = jnp.where(lane % 2 == 0, left, right)
    near[...] = jnp.concatenate([beside_matrix(depth)] * 2, 0)
    far[...] = halo_matrix(depth)
    if last:
        sens[...] = jnp.zeros_like(sens)
    else:
        gs[...] = jnp.zeros_like(gs)
        ends[...] = ends_matrix(depth)
    yl[...] = yl_ref[:4].astype(F32)
    yr[...] = yr_ref[:4].astype(F32)

    levels = sr_ref.shape[0]
    tile = (8, depth)
    wr, wi, share = [], [], []
    for m in range(levels):
        d = 6.0 + jnp.full(tile, sr_ref[m], F32)
        s = jnp.full(tile, si_ref[m], F32)
        mag = d * d + s * s
        wr.append(RELAXATION * d / mag)
        wi.append(-RELAXATION * s / mag)
        if last:
            share.append(jnp.full(tile, sh_ref[m], F32))

    def lookup(masks, table):
        out = jnp.broadcast_to(table[0], (rows // 8, 8, depth))
        for mask, entry in zip(masks, table[1:]):
            out = jnp.where(mask, entry, out)
        return out.reshape(rows, depth)

    row8 = lax.broadcasted_iota(jnp.int32, tile, 0)

    def along_z(first):
        v = v_ref[:, pl.ds(first, PB)].reshape(4 * PB * rows, depth)
        masked = [
            jnp.where(lane // 2 == first + p, hs[c], 0.0).astype(BF16)
            for c in range(4)
            for p in range(PB)
        ]
        out = mm(jnp.concatenate(split(v), 1), near[...]) + mm(jnp.concatenate(masked, 0), far[...])
        zt[...] = out.reshape(4, PB, rows, depth)

    def plane(first, p, put):
        x = first + p
        mat = m_ref[x].reshape(rows // 8, 8, depth)
        masks = [mat == m for m in range(1, levels)]
        w_r, w_i = lookup(masks, wr), lookup(masks, wi)

        def drive(c):
            v = v_ref[c, x]
            if p == 0:
                before = v_ref[c, jnp.maximum(x - 1, 0)]
                before = jnp.where(x == 0, xl_ref[c * rows : (c + 1) * rows].astype(F32), before)
            else:
                before = v_ref[c, x - 1]
            if p == PB - 1:
                after = v_ref[c, jnp.minimum(x + 1, planes_here - 1)]
                edge = xr_ref[c * rows : (c + 1) * rows].astype(F32)
                after = jnp.where(x == planes_here - 1, edge, after)
            else:
                after = v_ref[c, x + 1]
            total = before + after + s_ref[c, x].astype(F32) + zt[c, p]
            up = pltpu.roll(v, 1, 0)
            down = pltpu.roll(v, rows - 1, 0)
            top = jnp.where(row8 == 0, yl[c, pl.ds(x, 1), :], up[:8])
            low = jnp.where(row8 == 7, yr[c, pl.ds(x, 1), :], down[-8:])
            total = total + jnp.concatenate([top, up[8:]], 0)
            return v, total + jnp.concatenate([down[:-8], low], 0)

        new = []
        for re in (0, 2):
            v_r, t_r = drive(re)
            v_i, t_i = drive(re + 1)
            keep = 1.0 - RELAXATION
            n_r = keep * v_r + (w_r * t_r - w_i * t_i)
            n_i = keep * v_i + (w_r * t_i + w_i * t_r)
            put(re, n_r)
            put(re + 1, n_i)
            new += [n_r, n_i]
        if last:
            value[p] = lookup(masks, share) * (new[0] * new[2] - new[1] * new[3])

    groups = planes_here // PB

    def store(slot, first):
        return pltpu.make_async_copy(
            news.at[slot], o_ref.at[:, pl.ds(first, PB)], sems.at[slot]
        )

    def group(i, carry):
        first = i * PB
        along_z(first)
        if last:
            slot = i % 2

            @pl.when(i >= 2)
            def _():
                store(slot, first - 2 * PB).wait()

        for p in range(PB):

            def put(c, new, p=p):
                if last:
                    news[slot, c, p] = new
                else:
                    o_ref[c, first + p] = new

            plane(first, p, put)
        if last:
            store(slot, first).start()
            ones = jnp.ones((2 * depth, depth), BF16)
            parts = split(value[...].reshape(PB * rows, depth))
            sums = mm(jnp.concatenate(parts, 1), ones).reshape(PB, rows, depth)
            held = sens[...]
            for p in range(PB):
                held = jnp.where(lane == first + p, sums[p], held)
            sens[...] = held
        else:
            put_faces(first, o_ref, first, ends[...], gs, ylo, yhi)
        return carry

    lax.fori_loop(0, groups, group, 0)

    if not last:
        put_plane(xlo_ref, o_ref[:, 0])
        put_plane(xhi_ref, o_ref[:, planes_here - 1])
        g_ref[...] = gs[...].astype(BF16)
        xlo_ref[4 * rows :] = jnp.zeros((2 * R, depth), BF16)
        xhi_ref[4 * rows :] = jnp.zeros((2 * R, depth), BF16)
        cells = d_ref.shape[0]
        strips = [r[4 * rows : 4 * rows + 2 * R].astype(F32)[:R] for r in (xl_ref, xr_ref)]
        filler = jnp.zeros((2 * cells - cells - 2 * R, depth), F32)
        tall = jnp.concatenate([strips[0], paired(d_ref[...]), strips[1], filler], 0)
        tall = tall.astype(BF16).reshape(2, cells, depth)
        for out_ref, rows_out in ((ylo_ref, ylo), (yhi_ref, yhi)):
            out_ref[:4] = rows_out[...].astype(BF16)
            out_ref[4:] = tall
    else:
        cells = rows
        row = lax.broadcasted_iota(jnp.int32, (cells, 2 * cells), 0)
        col = lanes_of((cells, 2 * cells))
        half_sum = jnp.zeros((cells, 2 * cells), F32)
        for shift, ref in ((-cells, yl_ref), (0, mid_ref), (cells, yr_ref)):
            weight = jnp.maximum(R + 1 - jnp.abs(col % cells + shift - row), 0)
            tall = ref[4:].reshape(2 * cells, depth)
            half_sum = half_sum + lax.dot_general(
                weight.astype(F32).astype(BF16),
                tall,
                (((1,), (1,)), ((), ())),
                preferred_element_type=F32,
            )
        row = lax.broadcasted_iota(jnp.int32, (2 * cells, depth), 0)
        col = lanes_of((2 * cells, depth))
        weight = jnp.maximum(R + 1 - jnp.abs(row - R - col), 0).astype(F32).astype(BF16)
        filtered = twice(half_sum, weight) / float((R + 1) ** 4)
        tangent = jnp.tanh(SHARPNESS * (filtered - THRESHOLD))
        total = math.tanh(SHARPNESS * THRESHOLD) + math.tanh(SHARPNESS * (1.0 - THRESHOLD))
        slope = SHARPNESS * (1.0 - tangent * tangent) / total
        weighted = slope * sens[...] * scale
        half = rows // 2
        both = pltpu.roll(weighted[half:], depth // 2, 1)
        sens_ref[:half] = jnp.where(lane[:half] < depth // 2, weighted[:half], both)
        mine = jnp.where(lax.axis_index("gz") == 0, own_ref[...].astype(F32), 0.0)
        sens_ref[half:] = jnp.concatenate([mine, jnp.zeros((8, depth - rows), F32)], 1)
        store((groups - 2) % 2, (groups - 2) * PB).wait()
        store((groups - 1) % 2, (groups - 1) * PB).wait()


def twice(value, right):
    high, low = split(value)
    return mm(high, right) + mm(low, right)


def left_twice(left, value):
    high, low = split(value)
    return mm(left, high) + mm(left, low)


def whole(shape):
    return pl.BlockSpec(shape, lambda i: (0,) * len(shape))


SMEM_SPEC = pl.BlockSpec(memory_space=pltpu.SMEM)
VMEM_SPEC = pl.BlockSpec(memory_space=pltpu.VMEM)


def message_shapes(nx, ny, nz, parts):
    tall = (4 * ny + 2 * R, nz)
    return [tall, tall, (parts, nx, nz), (parts, nx, nz), (4, ny, nz)]


def face_scratch(nx, ny, nz):
    return [
        pltpu.VMEM((4, ny, nz), F32),
        pltpu.VMEM((4, nx, nz), F32),
        pltpu.VMEM((4, nx, nz), F32),
        pltpu.VMEM((nz, nz), BF16),
    ]


def pack(fields, density):
    _, nx, ny, nz = fields.shape
    shapes = message_shapes(nx, ny, nz, 4)
    return pl.pallas_call(
        pack_kernel,
        grid=(nx // PB,),
        in_specs=[
            pl.BlockSpec((4, PB, ny, nz), lambda i: (0, i, 0, 0)),
            whole(density.shape),
        ],
        out_specs=[whole(s) for s in shapes],
        out_shape=[jax.ShapeDtypeStruct(s, BF16) for s in shapes],
        scratch_shapes=face_scratch(nx, ny, nz),
        compiler_params=pltpu.CompilerParams(vmem_limit_bytes=12 << 20),
        cost_estimate=pl.CostEstimate(
            flops=fields.size * 4, bytes_accessed=fields.size * 4, transcendentals=0
        ),
        name="pack_faces",
    )(pltpu.with_memory_space_constraint(fields, pltpu.HBM), density)


def sweep(last, tables, current, sources, material, halos, more):
    _, nx, ny, nz = current.shape
    scratch = [
        pltpu.VMEM((4, ny, nz), F32),
        pltpu.VMEM((4, nx, nz), F32),
        pltpu.VMEM((4, nx, nz), F32),
        pltpu.VMEM((2 * nz, nz), BF16),
        pltpu.VMEM((nz, nz), BF16),
        pltpu.VMEM((4, PB, ny, nz), F32),
    ]
    if last:
        shapes = [
            jax.ShapeDtypeStruct(current.shape, F32),
            jax.ShapeDtypeStruct((ny // 2 + 8, nz), F32),
        ]
        specs = [pl.BlockSpec(memory_space=pltpu.HBM), VMEM_SPEC]
        more_specs = [SMEM_SPEC, VMEM_SPEC, VMEM_SPEC]
        scratch += [
            pltpu.VMEM((ny, nz), F32),
            pltpu.VMEM((PB, ny, nz), F32),
            pltpu.VMEM((2, 4, PB, ny, nz), F32),
            pltpu.SemaphoreType.DMA((2,)),
        ]
    else:
        faces = message_shapes(nx, ny, nz, 6)
        shapes = [pltpu.VMEM(current.shape, F32)]
        shapes += [jax.ShapeDtypeStruct(s, BF16) for s in faces]
        specs = [VMEM_SPEC] * len(shapes)
        more_specs = [VMEM_SPEC]
        scratch += face_scratch(nx, ny, nz)

    def near(value):
        return pltpu.with_memory_space_constraint(value, pltpu.VMEM)

    return pl.pallas_call(
        functools.partial(
            sweep_kernel,
            last,
            lax.axis_size("gz"),
            1.0 / math.sqrt(nz * lax.axis_size("gz")),
        ),
        in_specs=[SMEM_SPEC] * 2 + [VMEM_SPEC] * 9 + more_specs,
        out_specs=specs,
        out_shape=shapes,
        scratch_shapes=scratch,
        compiler_params=pltpu.CompilerParams(vmem_limit_bytes=20 << 20),
        cost_estimate=pl.CostEstimate(
            flops=current.size * 24, bytes_accessed=current.size * 11, transcendentals=0
        ),
        name="sweep_last" if last else "sweep_first",
    )(*tables, near(current), near(sources), near(material), *halos, *more)


def exchange(xlo, xhi, ylo, yhi, g):
    out = []
    for axis, low, high in (("gx", xlo, xhi), ("gy", ylo, yhi)):
        count = lax.axis_size(axis)
        up = [(i, i + 1) for i in range(count - 1)]
        out.append(lax.ppermute(high, axis, up))
        out.append(lax.ppermute(low, axis, [(j, i) for i, j in up]))
    count = lax.axis_size("gz")
    if count == 2:
        other = lax.ppermute(g, "gz", [(0, 1), (1, 0)])
        return out + [other, other]
    up = [(i, i + 1) for i in range(count - 1)]
    return out + [lax.ppermute(g, "gz", up), lax.ppermute(g, "gz", [(j, i) for i, j in up])]


def plane_kernel(ngx, ngy, me_ref, got_ref, out_ref, w_ref):
    cells = 64
    nx, ny = ngx * cells, ngy * cells
    columns = ngx * ngy
    half = cells // 2
    for cx in range(ngx):
        for cy in range(ngy):
            c = cx * ngy + cy
            for part in range(2):
                lanes = pl.ds(part * cells, cells)
                w_ref[pl.ds(cy * cells + part * half, half), pl.ds(cx * cells, cells)] = got_ref[
                    c, pl.ds(0, half), lanes
                ]

    def band(n):
        i = lax.broadcasted_iota(jnp.int32, (n, n), 0)
        j = lax.broadcasted_iota(jnp.int32, (n, n), 1)
        return jnp.maximum(R + 1 - jnp.abs(i - j), 0).astype(F32).astype(BF16)

    unit = float((R + 1) ** 4)
    weighted = twice(w_ref[...], band(nx))

    tiles = cells
    owner = jnp.concatenate([got_ref[c, pl.ds(half, 1), pl.ds(0, tiles)] for c in range(columns)], 0)
    mine = owner == me_ref[0].astype(F32)
    flag = jnp.where(mine, 1.0, 0.0)
    a = lax.broadcasted_iota(jnp.int32, (tiles, tiles), 0)
    b = lax.broadcasted_iota(jnp.int32, (tiles, tiles), 1)
    rank = mm(flag.astype(BF16), jnp.where(a < b, 1.0, 0.0).astype(BF16))
    number = lanes_of((columns, tiles))
    column = lax.broadcasted_iota(jnp.int32, (columns, 1), 0)
    rows, blocks = [], []
    for k in range(MOST):
        chosen = mine & (rank == float(k))
        tile = jnp.sum(jnp.where(chosen, number, 0), axis=1, keepdims=True)
        there = jnp.sum(jnp.where(chosen, 1, 0), axis=1, keepdims=True)
        rows.append((column % ngy) * cells + (tile % (cells // TS)) * TS)
        block = (column // ngy) * (cells // TS) + tile // (cells // TS)
        blocks.append(jnp.where(there > 0, block, -1))
    row = jnp.concatenate(rows, 0)
    block = jnp.concatenate(blocks, 0)
    slots = MOST * columns
    across = lax.broadcasted_iota(jnp.int32, (slots, ny), 1)
    lefts = [
        jnp.maximum(R + 1 - jnp.abs(row + j - across), 0).astype(F32).astype(BF16)
        for j in range(TS)
    ]
    lines = left_twice(jnp.concatenate(lefts, 0), weighted)
    keep = lanes_of((slots, nx)) // TS == block
    from_x = lax.broadcasted_iota(jnp.int32, (nx, TS * TS), 0) % TS
    to_q = lanes_of((nx, TS * TS))
    out = jnp.zeros((slots, TS * TS), F32)
    for j in range(TS):
        fold = jnp.where(to_q == from_x * TS + j, 1.0, 0.0).astype(BF16)
        out = out + twice(jnp.where(keep, lines[j * slots : (j + 1) * slots], 0.0), fold)
    out = out / unit
    for k in range(MOST):
        out_ref[0, :, pl.ds(k * TS * TS, TS * TS)] = out[k * columns : (k + 1) * columns]


def on_device(fields, sources, material, shift_real, shift_imag, design_share, density, owner_map):
    ngx, ngy = lax.axis_size("gx"), lax.axis_size("gy")
    columns = ngx * ngy
    cells = density.shape[0]
    tables = (shift_real, shift_imag)
    owners = jnp.broadcast_to(owner_map.reshape(1, -1), (8, cells))
    halos = exchange(*pack(fields, density))
    middle, *faces = sweep(False, tables, fields, sources, material, halos, [density])
    final, partial = sweep(
        True, tables, middle, sources, material, exchange(*faces), [design_share, faces[2], owners]
    )
    partial = jnp.sum(lax.all_gather(partial, "gz"), 0)
    copies = jnp.broadcast_to(partial[None], (columns, *partial.shape))
    plane = lax.all_to_all(copies, ("gx", "gy"), split_axis=0, concat_axis=0)
    me = (lax.axis_index("gx") * ngy + lax.axis_index("gy")).reshape(1)
    owned = pl.pallas_call(
        functools.partial(plane_kernel, ngx, ngy),
        in_specs=[SMEM_SPEC, VMEM_SPEC],
        out_specs=VMEM_SPEC,
        out_shape=jax.ShapeDtypeStruct((1, columns, MOST * TS * TS), F32),
        scratch_shapes=[pltpu.VMEM((ngy * cells, ngx * cells), F32)],
        compiler_params=pltpu.CompilerParams(vmem_limit_bytes=16 << 20),
        name="plane",
    )(me, plane)
    return (final, owned)


def solution(mesh):
    placed = (
        P(None, "gx", "gy", "gz"),
        P(None, "gx", "gy", "gz"),
        P("gx", "gy", "gz"),
        P(),
        P(),
        P(),
        P("gx", "gy"),
        P("gx", "gy", None, None),
    )
    return jax.shard_map(
        on_device,
        mesh=mesh,
        in_specs=placed,
        out_specs=(P(None, "gx", "gy", "gz"), P(("gx", "gy"), None, None)),
        check_vma=False,
    )
```

```python
import functools
import math

import jax
import jax.numpy as jnp
from jax import lax
from jax.experimental import pallas as pl
from jax.experimental.pallas import tpu as pltpu
from jax.sharding import PartitionSpec as P

R = 8
TS = 8
MOST = 8
RELAXATION = 0.8
SHARPNESS = 8.0
THRESHOLD = 0.5
PB = 8
RC = 16
F32 = jnp.float32
BF16 = jnp.bfloat16


def lanes_of(shape):
    return lax.broadcasted_iota(jnp.int32, shape, len(shape) - 1)


def ends_matrix(depth):
    k = lax.broadcasted_iota(jnp.int32, (PB * depth, depth), 0)
    j = lax.broadcasted_iota(jnp.int32, (PB * depth, depth), 1) % (2 * PB)
    even = (k % depth == 0) & (j == 2 * (k // depth))
    odd = (k % depth == depth - 1) & (j == 2 * (k // depth) + 1)
    return jnp.where(even | odd, 1.0, 0.0).astype(BF16)


def beside_matrix(depth):
    z = lax.broadcasted_iota(jnp.int32, (depth, depth), 0)
    j = lax.broadcasted_iota(jnp.int32, (depth, depth), 1)
    return jnp.where(jnp.abs(z - j) == 1, 1.0, 0.0).astype(BF16)


def halo_matrix(depth):
    j = lax.broadcasted_iota(jnp.int32, (depth, depth), 0)
    z = lax.broadcasted_iota(jnp.int32, (depth, depth), 1)
    even = (z == 0) & (j % 2 == 0)
    odd = (z == depth - 1) & (j % 2 == 1)
    return jnp.where(even | odd, 1.0, 0.0).astype(BF16)


def sum_matrix(depth):
    k = lax.broadcasted_iota(jnp.int32, (2 * PB * depth, depth), 0) // (2 * depth)
    j = lax.broadcasted_iota(jnp.int32, (2 * PB * depth, depth), 1) % PB
    return jnp.where(k == j, 1.0, 0.0).astype(BF16)


def split(value):
    high = value.astype(BF16)
    return high, (value - high.astype(F32)).astype(BF16)


def mm(a, b):
    return lax.dot_general(a, b, (((1,), (0,)), ((), ())), preferred_element_type=F32)


def put_faces(first, ref, start, ends, gs, ylo, yhi):
    rows, depth = ref.shape[2:]
    value = ref[:, pl.ds(start, PB)]
    for p in range(PB):
        for c in range(4):
            ylo[c, pl.ds(first + p, 1), :] = value[c, p, 0:1, :]
            yhi[c, pl.ds(first + p, 1), :] = value[c, p, rows - 1 :, :]
    high = value.astype(BF16)
    beside = [high[:, p].reshape(4 * rows, depth) for p in range(PB)]
    picked = mm(jnp.concatenate(beside, 1), ends).reshape(4, rows, depth)
    here = lanes_of((rows, depth)) // (2 * PB) == first // PB
    for c in range(4):
        gs[c] = jnp.where(here, picked[c], gs[c])


def put_plane(out_ref, value):
    rows = value.shape[1]
    out_ref[: 4 * rows] = value.astype(BF16).reshape(4 * rows, value.shape[2])


def paired(value):
    high = value.astype(BF16).astype(F32)
    return jnp.concatenate([high, value - high], 1)


def x_kernel(v_ref, d_ref, xlo_ref, xhi_ref, planes, sems):
    far = v_ref.shape[1] - 1
    rows, depth = v_ref.shape[2:]
    copies = [
        pltpu.make_async_copy(v_ref.at[:, x], planes.at[i], sems.at[i])
        for i, x in enumerate((0, far))
    ]
    for copy in copies:
        copy.start()
    cells = d_ref.shape[0]
    none = jnp.zeros((R, depth), F32)
    for i, (out_ref, start) in enumerate(((xlo_ref, 0), (xhi_ref, cells - R))):
        strip = jnp.concatenate([paired(d_ref[start : start + R, :]), none], 0)
        out_ref[4 * rows :] = strip.astype(BF16)
        copies[i].wait()
        put_plane(out_ref, planes[i])


def pack_kernel(v_ref, ylo_ref, yhi_ref, g_ref, gs, ylo, yhi, ends):
    gs[...] = jnp.zeros_like(gs)
    ends[...] = ends_matrix(v_ref.shape[3])

    def group(i, carry):
        put_faces(i * PB, v_ref, i * PB, ends[...], gs, ylo, yhi)
        return carry

    lax.fori_loop(0, v_ref.shape[1] // PB, group, 0)
    g_ref[...] = gs[...].astype(BF16)
    ylo_ref[...] = ylo[...].astype(BF16)
    yhi_ref[...] = yhi[...].astype(BF16)


def sweep_kernel(last, nz, scale, *refs):
    sr_ref, si_ref, v_ref, s_ref, m_ref, xl_ref, xr_ref, yl_ref, yr_ref, gl_ref, gr_ref = refs[:11]
    if last:
        sh_ref, mid_ref, own_ref, o_ref, sens_ref = refs[11:16]
        hs, yl, yr, near, far, zt0, zt1, sens, value, news, sums, sems = refs[16:]
    else:
        d_ref, o_ref, xlo_ref, xhi_ref, ylo_ref, yhi_ref, g_ref = refs[11:18]
        hs, yl, yr, near, far, zt0, zt1, gs, ylo, yhi, ends = refs[18:]
    planes_here, rows, depth = v_ref.shape[1:]
    lane = lanes_of((rows, depth))

    if nz == 2:
        here = lax.axis_index("gz").astype(F32)
        keep_l, keep_r = here, 1.0 - here
    else:
        keep_l, keep_r = 1.0, 1.0
    for c in range(4):
        left = pltpu.roll(gl_ref[c].astype(F32), depth - 1, 1) * keep_l
        right = pltpu.roll(gr_ref[c].astype(F32), 1, 1) * keep_r
        hs[c] = jnp.where(lane % 2 == 0, left, right)
    near[...] = jnp.concatenate([beside_matrix(depth)] * 2, 0)
    far[...] = halo_matrix(depth)
    if last:
        sens[...] = jnp.zeros_like(sens)
        sums[...] = sum_matrix(depth)
    else:
        gs[...] = jnp.zeros_like(gs)
        ends[...] = ends_matrix(depth)
    yl[...] = yl_ref[:4].astype(F32)
    yr[...] = yr_ref[:4].astype(F32)

    levels = sr_ref.shape[0]
    tile = (8, depth)
    wr, wi, share = [], [], []
    for m in range(levels):
        d = 6.0 + jnp.full(tile, sr_ref[m], F32)
        s = jnp.full(tile, si_ref[m], F32)
        mag = d * d + s * s
        wr.append(RELAXATION * d / mag)
        wi.append(-RELAXATION * s / mag)
        if last:
            share.append(jnp.full(tile, sh_ref[m], F32))

    def lookup(masks, table):
        out = jnp.broadcast_to(table[0], (RC // 8, 8, depth))
        for mask, entry in zip(masks, table[1:]):
            out = jnp.where(mask, entry, out)
        return out.reshape(RC, depth)

    row8 = lax.broadcasted_iota(jnp.int32, tile, 0)

    def along_z(first, zt):
        v = v_ref[:, pl.ds(first, PB)].reshape(4 * PB * rows, depth)
        masked = [
            jnp.where(lane // 2 == first + p, hs[c], 0.0).astype(BF16)
            for c in range(4)
            for p in range(PB)
        ]
        out = mm(jnp.concatenate(split(v), 1), near[...]) + mm(jnp.concatenate(masked, 0), far[...])
        zt[...] = out.reshape(4, PB, rows, depth)

    def plane(first, p, zt, put):
        for low in range(0, rows, RC):
            chunk(first, p, low, zt, put)

    def chunk(first, p, low, zt, put):
        x = first + p
        span = slice(low, low + RC)
        mat = m_ref[x, span].reshape(RC // 8, 8, depth)
        masks = [mat == m for m in range(1, levels)]
        w_r, w_i = lookup(masks, wr), lookup(masks, wi)

        def drive(c):
            v = v_ref[c, x, span]
            part = slice(c * rows + low, c * rows + low + RC)
            if p == 0:
                before = v_ref[c, jnp.maximum(x - 1, 0), span]
                before = jnp.where(x == 0, xl_ref[part].astype(F32), before)
            else:
                before = v_ref[c, x - 1, span]
            if p == PB - 1:
                after = v_ref[c, jnp.minimum(x + 1, planes_here - 1), span]
                after = jnp.where(x == planes_here - 1, xr_ref[part].astype(F32), after)
            else:
                after = v_ref[c, x + 1, span]
            total = before + after + s_ref[c, x, span].astype(F32) + zt[c, p, span]
            if low == 0:
                up = pltpu.roll(v, 1, 0)
                top = jnp.where(row8 == 0, yl[c, pl.ds(x, 1), :], up[:8])
                up = jnp.concatenate([top, up[8:]], 0)
            else:
                up = v_ref[c, x, low - 1 : low - 1 + RC]
            if low == rows - RC:
                down = pltpu.roll(v, RC - 1, 0)
                tail = jnp.where(row8 == 7, yr[c, pl.ds(x, 1), :], down[-8:])
                down = jnp.concatenate([down[:-8], tail], 0)
            else:
                down = v_ref[c, x, low + 1 : low + 1 + RC]
            return v, total + up + down

        new = []
        for re in (0, 2):
            v_r, t_r = drive(re)
            v_i, t_i = drive(re + 1)
            keep = 1.0 - RELAXATION
            n_r = keep * v_r + (w_r * t_r - w_i * t_i)
            n_i = keep * v_i + (w_r * t_i + w_i * t_r)
            put(re, span, n_r)
            put(re + 1, span, n_i)
            new += [n_r, n_i]
        if last:
            value[p, span] = lookup(masks, share) * (new[0] * new[2] - new[1] * new[3])

    groups = planes_here // PB

    def store(i):
        part = pl.ds(i * PB, PB)
        return pltpu.make_async_copy(news.at[:, part], o_ref.at[:, part], sems.at[i])

    result = news if last else o_ref

    def group(i, zt, zt_next):
        first = i * PB
        along_z(jnp.minimum(first + PB, planes_here - PB), zt_next)
        for p in range(PB):

            def put(c, span, new, p=p):
                result[c, first + p, span] = new

            plane(first, p, zt, put)
        if last:
            store(i).start()
            parts = [part for p in range(PB) for part in split(value[p])]
            picked = mm(jnp.concatenate(parts, 1), sums[...])
            sens[...] = jnp.where(lane // PB == i, picked, sens[...])
        else:
            put_faces(first, o_ref, first, ends[...], gs, ylo, yhi)

    def two(i, carry):
        group(2 * i, zt0, zt1)
        group(2 * i + 1, zt1, zt0)
        return carry

    along_z(0, zt0)
    lax.fori_loop(0, groups // 2, two, 0)

    if not last:
        put_plane(xlo_ref, o_ref[:, 0])
        put_plane(xhi_ref, o_ref[:, planes_here - 1])
        g_ref[...] = gs[...].astype(BF16)
        xlo_ref[4 * rows :] = jnp.zeros((2 * R, depth), BF16)
        xhi_ref[4 * rows :] = jnp.zeros((2 * R, depth), BF16)
        cells = d_ref.shape[0]
        strips = [r[4 * rows : 4 * rows + 2 * R].astype(F32)[:R] for r in (xl_ref, xr_ref)]
        filler = jnp.zeros((2 * cells - cells - 2 * R, depth), F32)
        tall = jnp.concatenate([strips[0], paired(d_ref[...]), strips[1], filler], 0)
        tall = tall.astype(BF16).reshape(2, cells, depth)
        for out_ref, rows_out in ((ylo_ref, ylo), (yhi_ref, yhi)):
            out_ref[:4] = rows_out[...].astype(BF16)
            out_ref[4:] = tall
    else:
        cells = rows
        row = lax.broadcasted_iota(jnp.int32, (cells, 2 * cells), 0)
        col = lanes_of((cells, 2 * cells))
        half_sum = jnp.zeros((cells, 2 * cells), F32)
        for shift, ref in ((-cells, yl_ref), (0, mid_ref), (cells, yr_ref)):
            weight = jnp.maximum(R + 1 - jnp.abs(col % cells + shift - row), 0)
            tall = ref[4:].reshape(2 * cells, depth)
            half_sum = half_sum + lax.dot_general(
                weight.astype(F32).astype(BF16),
                tall,
                (((1,), (1,)), ((), ())),
                preferred_element_type=F32,
            )
        row = lax.broadcasted_iota(jnp.int32, (2 * cells, depth), 0)
        col = lanes_of((2 * cells, depth))
        weight = jnp.maximum(R + 1 - jnp.abs(row - R - col), 0).astype(F32).astype(BF16)
        filtered = twice(half_sum, weight) / float((R + 1) ** 4)
        tangent = jnp.tanh(SHARPNESS * (filtered - THRESHOLD))
        total = math.tanh(SHARPNESS * THRESHOLD) + math.tanh(SHARPNESS * (1.0 - THRESHOLD))
        slope = SHARPNESS * (1.0 - tangent * tangent) / total
        weighted = slope * sens[...] * scale
        half = rows // 2
        both = pltpu.roll(weighted[half:], depth // 2, 1)
        sens_ref[:half] = jnp.where(lane[:half] < depth // 2, weighted[:half], both)
        mine = jnp.where(lax.axis_index("gz") == 0, own_ref[...].astype(F32), 0.0)
        sens_ref[half:] = jnp.concatenate([mine, jnp.zeros((8, depth - rows), F32)], 1)
        for i in range(groups):
            store(i).wait()


def twice(value, right):
    high, low = split(value)
    return mm(high, right) + mm(low, right)


def left_twice(left, value):
    high, low = split(value)
    return mm(left, high) + mm(left, low)


def whole(shape):
    return pl.BlockSpec(shape, lambda i: (0,) * len(shape))


SMEM_SPEC = pl.BlockSpec(memory_space=pltpu.SMEM)
VMEM_SPEC = pl.BlockSpec(memory_space=pltpu.VMEM)


def message_shapes(nx, ny, nz, parts):
    tall = (4 * ny + 2 * R, nz)
    return [tall, tall, (parts, nx, nz), (parts, nx, nz), (4, ny, nz)]


def face_scratch(nx, ny, nz):
    return [
        pltpu.VMEM((4, ny, nz), F32),
        pltpu.VMEM((4, nx, nz), F32),
        pltpu.VMEM((4, nx, nz), F32),
        pltpu.VMEM((PB * nz, nz), BF16),
    ]


def near(value):
    return pltpu.with_memory_space_constraint(value, pltpu.VMEM)


def pack(fields, density):
    _, nx, ny, nz = fields.shape
    shapes = [jax.ShapeDtypeStruct(s, BF16) for s in message_shapes(nx, ny, nz, 4)]
    xlo, xhi = pl.pallas_call(
        x_kernel,
        in_specs=[pl.BlockSpec(memory_space=pltpu.HBM), VMEM_SPEC],
        out_specs=[VMEM_SPEC] * 2,
        out_shape=shapes[:2],
        scratch_shapes=[pltpu.VMEM((2, 4, ny, nz), F32), pltpu.SemaphoreType.DMA((2,))],
        compiler_params=pltpu.CompilerParams(vmem_limit_bytes=4 << 20),
        cost_estimate=pl.CostEstimate(flops=ny * nz * 8, bytes_accessed=ny * nz * 48, transcendentals=0),
        name="x_faces",
    )(pltpu.with_memory_space_constraint(fields, pltpu.HBM), density)
    held = near(fields)
    ylo, yhi, g = pl.pallas_call(
        pack_kernel,
        in_specs=[VMEM_SPEC],
        out_specs=[VMEM_SPEC] * 3,
        out_shape=shapes[2:],
        scratch_shapes=face_scratch(nx, ny, nz),
        compiler_params=pltpu.CompilerParams(vmem_limit_bytes=12 << 20),
        cost_estimate=pl.CostEstimate(
            flops=fields.size * 4, bytes_accessed=fields.size * 4, transcendentals=0
        ),
        name="pack_faces",
    )(held)
    return held, (xlo, xhi, ylo, yhi, g)


def sweep(last, tables, current, sources, material, halos, more):
    _, nx, ny, nz = current.shape
    scratch = [
        pltpu.VMEM((4, ny, nz), F32),
        pltpu.VMEM((4, nx, nz), F32),
        pltpu.VMEM((4, nx, nz), F32),
        pltpu.VMEM((2 * nz, nz), BF16),
        pltpu.VMEM((nz, nz), BF16),
        pltpu.VMEM((4, PB, ny, nz), F32),
        pltpu.VMEM((4, PB, ny, nz), F32),
    ]
    if last:
        shapes = [
            jax.ShapeDtypeStruct(current.shape, F32),
            jax.ShapeDtypeStruct((ny // 2 + 8, nz), F32),
        ]
        specs = [pl.BlockSpec(memory_space=pltpu.HBM), VMEM_SPEC]
        more_specs = [SMEM_SPEC, VMEM_SPEC, VMEM_SPEC]
        scratch += [
            pltpu.VMEM((ny, nz), F32),
            pltpu.VMEM((PB, ny, nz), F32),
            pltpu.VMEM(current.shape, F32),
            pltpu.VMEM((2 * PB * nz, nz), BF16),
            pltpu.SemaphoreType.DMA((nx // PB,)),
        ]
    else:
        faces = message_shapes(nx, ny, nz, 6)
        shapes = [pltpu.VMEM(current.shape, F32)]
        shapes += [jax.ShapeDtypeStruct(s, BF16) for s in faces]
        specs = [VMEM_SPEC] * len(shapes)
        more_specs = [VMEM_SPEC]
        scratch += face_scratch(nx, ny, nz)

    return pl.pallas_call(
        functools.partial(
            sweep_kernel,
            last,
            lax.axis_size("gz"),
            1.0 / math.sqrt(nz * lax.axis_size("gz")),
        ),
        in_specs=[SMEM_SPEC] * 2 + [VMEM_SPEC] * 9 + more_specs,
        out_specs=specs,
        out_shape=shapes,
        scratch_shapes=scratch,
        compiler_params=pltpu.CompilerParams(vmem_limit_bytes=20 << 20),
        cost_estimate=pl.CostEstimate(
            flops=current.size * 24, bytes_accessed=current.size * 11, transcendentals=0
        ),
        name="sweep_last" if last else "sweep_first",
    )(*tables, near(current), near(sources), near(material), *halos, *more)


def exchange(xlo, xhi, ylo, yhi, g):
    out = []
    for axis, low, high in (("gx", xlo, xhi), ("gy", ylo, yhi)):
        count = lax.axis_size(axis)
        up = [(i, i + 1) for i in range(count - 1)]
        out.append(lax.ppermute(high, axis, up))
        out.append(lax.ppermute(low, axis, [(j, i) for i, j in up]))
    count = lax.axis_size("gz")
    if count == 2:
        other = lax.ppermute(g, "gz", [(0, 1), (1, 0)])
        return out + [other, other]
    up = [(i, i + 1) for i in range(count - 1)]
    return out + [lax.ppermute(g, "gz", up), lax.ppermute(g, "gz", [(j, i) for i, j in up])]


def plane_kernel(ngx, ngy, me_ref, got_ref, out_ref, w_ref):
    cells = 64
    nx, ny = ngx * cells, ngy * cells
    columns = ngx * ngy
    half = cells // 2
    for cx in range(ngx):
        for cy in range(ngy):
            c = cx * ngy + cy
            for part in range(2):
                lanes = pl.ds(part * cells, cells)
                w_ref[pl.ds(cy * cells + part * half, half), pl.ds(cx * cells, cells)] = got_ref[
                    c, pl.ds(0, half), lanes
                ]

    def band(n):
        i = lax.broadcasted_iota(jnp.int32, (n, n), 0)
        j = lax.broadcasted_iota(jnp.int32, (n, n), 1)
        return jnp.maximum(R + 1 - jnp.abs(i - j), 0).astype(F32).astype(BF16)

    unit = float((R + 1) ** 4)
    weighted = twice(w_ref[...], band(nx))

    tiles = cells
    owner = jnp.concatenate([got_ref[c, pl.ds(half, 1), pl.ds(0, tiles)] for c in range(columns)], 0)
    mine = owner == me_ref[0].astype(F32)
    flag = jnp.where(mine, 1.0, 0.0)
    a = lax.broadcasted_iota(jnp.int32, (tiles, tiles), 0)
    b = lax.broadcasted_iota(jnp.int32, (tiles, tiles), 1)
    rank = mm(flag.astype(BF16), jnp.where(a < b, 1.0, 0.0).astype(BF16))
    number = lanes_of((columns, tiles))
    column = lax.broadcasted_iota(jnp.int32, (columns, 1), 0)
    rows, blocks = [], []
    for k in range(MOST):
        chosen = mine & (rank == float(k))
        tile = jnp.sum(jnp.where(chosen, number, 0), axis=1, keepdims=True)
        there = jnp.sum(jnp.where(chosen, 1, 0), axis=1, keepdims=True)
        rows.append((column % ngy) * cells + (tile % (cells // TS)) * TS)
        block = (column // ngy) * (cells // TS) + tile // (cells // TS)
        blocks.append(jnp.where(there > 0, block, -1))
    row = jnp.concatenate(rows, 0)
    block = jnp.concatenate(blocks, 0)
    slots = MOST * columns
    across = lax.broadcasted_iota(jnp.int32, (slots, ny), 1)
    lefts = [
        jnp.maximum(R + 1 - jnp.abs(row + j - across), 0).astype(F32).astype(BF16)
        for j in range(TS)
    ]
    lines = left_twice(jnp.concatenate(lefts, 0), weighted)
    keep = lanes_of((slots, nx)) // TS == block
    from_x = lax.broadcasted_iota(jnp.int32, (nx, TS * TS), 0) % TS
    to_q = lanes_of((nx, TS * TS))
    out = jnp.zeros((slots, TS * TS), F32)
    for j in range(TS):
        fold = jnp.where(to_q == from_x * TS + j, 1.0, 0.0).astype(BF16)
        out = out + twice(jnp.where(keep, lines[j * slots : (j + 1) * slots], 0.0), fold)
    out = out / unit
    for k in range(MOST):
        out_ref[0, :, pl.ds(k * TS * TS, TS * TS)] = out[k * columns : (k + 1) * columns]


def on_device(fields, sources, material, shift_real, shift_imag, design_share, density, owner_map):
    ngx, ngy = lax.axis_size("gx"), lax.axis_size("gy")
    columns = ngx * ngy
    cells = density.shape[0]
    tables = (shift_real, shift_imag)
    owners = jnp.broadcast_to(owner_map.reshape(1, -1), (8, cells))
    held, faces = pack(fields, density)
    halos = exchange(*faces)
    middle, *faces = sweep(False, tables, held, sources, material, halos, [density])
    final, partial = sweep(
        True, tables, middle, sources, material, exchange(*faces), [design_share, faces[2], owners]
    )
    partial = jnp.sum(lax.all_gather(partial, "gz"), 0)
    copies = jnp.broadcast_to(partial[None], (columns, *partial.shape))
    plane = lax.all_to_all(copies, ("gx", "gy"), split_axis=0, concat_axis=0)
    me = (lax.axis_index("gx") * ngy + lax.axis_index("gy")).reshape(1)
    owned = pl.pallas_call(
        functools.partial(plane_kernel, ngx, ngy),
        in_specs=[SMEM_SPEC, VMEM_SPEC],
        out_specs=VMEM_SPEC,
        out_shape=jax.ShapeDtypeStruct((1, columns, MOST * TS * TS), F32),
        scratch_shapes=[pltpu.VMEM((ngy * cells, ngx * cells), F32)],
        compiler_params=pltpu.CompilerParams(vmem_limit_bytes=16 << 20),
        name="plane",
    )(me, plane)
    return (final, owned)


def solution(mesh):
    placed = (
        P(None, "gx", "gy", "gz"),
        P(None, "gx", "gy", "gz"),
        P("gx", "gy", "gz"),
        P(),
        P(),
        P(),
        P("gx", "gy"),
        P("gx", "gy", None, None),
    )
    return jax.shard_map(
        on_device,
        mesh=mesh,
        in_specs=placed,
        out_specs=(P(None, "gx", "gy", "gz"), P(("gx", "gy"), None, None)),
        check_vma=False,
    )
```

```python
import functools
import math

import jax
import jax.numpy as jnp
from jax import lax
from jax.experimental import pallas as pl
from jax.experimental.pallas import tpu as pltpu
from jax.sharding import PartitionSpec as P

R = 8
TS = 8
MOST = 8
RELAXATION = 0.8
SHARPNESS = 8.0
THRESHOLD = 0.5
PB = 8
RC = 16
F32 = jnp.float32
BF16 = jnp.bfloat16


def lanes_of(shape):
    return lax.broadcasted_iota(jnp.int32, shape, len(shape) - 1)


def ends_matrix(depth):
    k = lax.broadcasted_iota(jnp.int32, (PB * depth, depth), 0)
    j = lax.broadcasted_iota(jnp.int32, (PB * depth, depth), 1) % (2 * PB)
    even = (k % depth == 0) & (j == 2 * (k // depth))
    odd = (k % depth == depth - 1) & (j == 2 * (k // depth) + 1)
    return jnp.where(even | odd, 1.0, 0.0).astype(BF16)


def beside_matrix(depth):
    z = lax.broadcasted_iota(jnp.int32, (depth, depth), 0)
    j = lax.broadcasted_iota(jnp.int32, (depth, depth), 1)
    return jnp.where(jnp.abs(z - j) == 1, 1.0, 0.0).astype(BF16)


def halo_matrix(depth):
    j = lax.broadcasted_iota(jnp.int32, (depth, depth), 0)
    z = lax.broadcasted_iota(jnp.int32, (depth, depth), 1)
    even = (z == 0) & (j % 2 == 0)
    odd = (z == depth - 1) & (j % 2 == 1)
    return jnp.where(even | odd, 1.0, 0.0).astype(BF16)


def sum_matrix(depth):
    k = lax.broadcasted_iota(jnp.int32, (2 * PB * depth, depth), 0) // (2 * depth)
    j = lax.broadcasted_iota(jnp.int32, (2 * PB * depth, depth), 1) % PB
    return jnp.where(k == j, 1.0, 0.0).astype(BF16)


def split(value):
    high = value.astype(BF16)
    return high, (value - high.astype(F32)).astype(BF16)


def mm(a, b):
    return lax.dot_general(a, b, (((1,), (0,)), ((), ())), preferred_element_type=F32)


def put_ends(first, ref, ends, gs):
    rows, depth = ref.shape[2:]
    high = ref[:, pl.ds(first, PB)].astype(BF16)
    beside = [high[:, p].reshape(4 * rows, depth) for p in range(PB)]
    picked = mm(jnp.concatenate(beside, 1), ends).reshape(4, rows, depth)
    here = lanes_of((rows, depth)) // (2 * PB) == first // PB
    for c in range(4):
        gs[c] = jnp.where(here, picked[c], gs[c])


def paired(value):
    high = value.astype(BF16).astype(F32)
    return jnp.concatenate([high, value - high], 1)


PLANES = 13


def x_kernel(v_ref, s_ref, m_ref, d_ref, xlo_ref, xhi_ref, vs, ss, ms, sems):
    last = v_ref.shape[1] - 1
    rows, depth = v_ref.shape[2:]
    sides = ((0, 0, 1), (last, last - 1, 0))
    copies = []
    for i, (x, second, _) in enumerate(sides):
        copies.append(
            [
                pltpu.make_async_copy(
                    v_ref.at[:, pl.ds(min(x, second), 2)], vs.at[i], sems.at[3 * i]
                ),
                pltpu.make_async_copy(s_ref.at[:, x], ss.at[i], sems.at[3 * i + 1]),
                pltpu.make_async_copy(m_ref.at[x], ms.at[i], sems.at[3 * i + 2]),
            ]
        )
    for side in copies:
        for copy in side:
            copy.start()
    cells = d_ref.shape[0]
    none = jnp.zeros((R, depth), F32)
    for i, (out_ref, start) in enumerate(((xlo_ref, 0), (xhi_ref, cells - R))):
        strip = jnp.concatenate([paired(d_ref[start : start + R, :]), none], 0)
        out_ref[PLANES * rows :] = strip.astype(BF16)
        for copy in copies[i]:
            copy.wait()
        inner = sides[i][2]
        out_ref[: 4 * rows] = vs[i, :, 1 - inner].astype(BF16).reshape(4 * rows, depth)
        out_ref[4 * rows : 8 * rows] = vs[i, :, inner].astype(BF16).reshape(4 * rows, depth)
        out_ref[8 * rows : 12 * rows] = ss[i].reshape(4 * rows, depth)
        out_ref[12 * rows : 13 * rows] = (ms[i] + 1).astype(F32).astype(BF16)


def pack_kernel(v_ref, s_ref, m_ref, d_ref, xl_ref, xr_ref, ylo_ref, yhi_ref, g_ref, gs, ylo, yhi, ends):
    rows, depth = v_ref.shape[2:]
    gs[...] = jnp.zeros_like(gs)
    ends[...] = ends_matrix(depth)

    def group(i, carry):
        first = i * PB
        put_ends(first, v_ref, ends[...], gs)
        for p in range(PB):
            x = first + p
            here = pl.ds(x, 1)
            level = (m_ref[x] + 1).astype(F32)
            for out, edge, inner, low in ((ylo, 0, 1, 0), (yhi, rows - 1, rows - 2, rows - 16)):
                for c in range(4):
                    out[c, here, :] = v_ref[c, x, edge : edge + 1, :]
                    out[4 + c, here, :] = v_ref[c, x, inner : inner + 1, :]
                    near_edge = s_ref[c, x, low : low + 16, :].astype(F32)
                    out[8 + c, here, :] = near_edge[edge - low : edge - low + 1]
                out[12, here, :] = level[edge : edge + 1]
        return carry

    lax.fori_loop(0, v_ref.shape[1] // PB, group, 0)
    g_ref[...] = gs[...].astype(BF16)
    nx = v_ref.shape[1]
    cells = d_ref.shape[0]
    strips = [r[PLANES * rows :].astype(F32)[:R] for r in (xl_ref, xr_ref)]
    filler = jnp.zeros((cells - 2 * R, depth), F32)
    tall = jnp.concatenate([strips[0], paired(d_ref[...]), strips[1], filler], 0).astype(BF16)
    for out_ref, rows_out, edge, low in ((ylo_ref, ylo, 0, 0), (yhi_ref, yhi, rows - 1, rows - 16)):
        out_ref[: PLANES * nx] = rows_out[...].astype(BF16).reshape(PLANES * nx, depth)
        corners = [
            r[c * rows + low : c * rows + low + 16].astype(F32)[edge - low : edge - low + 1]
            for r in (xl_ref, xr_ref)
            for c in range(4)
        ]
        corners.append(jnp.zeros((2 * R - 8, depth), F32))
        out_ref[PLANES * nx : PLANES * nx + 2 * R] = jnp.concatenate(corners, 0).astype(BF16)
        out_ref[PLANES * nx + 2 * R :] = tall


def edge_kernel(g_ref, xl_ref, xr_ref, yl_ref, yr_ref, out_ref):
    parts, rows, depth = g_ref.shape
    beside = [r[: 4 * rows] for r in (xl_ref, xr_ref, yl_ref, yr_ref)]
    picked = mm(jnp.concatenate(beside, 1), ends_matrix(depth)[: 4 * depth])
    out_ref[:4] = g_ref[...]
    out_ref[4:] = picked.astype(BF16).reshape(4, rows, depth)


def sweep_kernel(last, nz, scale, *refs):
    sr_ref, si_ref, v_ref, s_ref, m_ref, gl_ref, gr_ref = refs[:7]
    if last:
        ext_ref, mid_ref, yl_ref, yr_ref, sh_ref, own_ref, o_ref, sens_ref = refs[7:15]
        hs, yl, yr, near, far, zt0, zt1, sens, value, news, sums, sems = refs[15:]
    else:
        xl_ref, xr_ref, yl_ref, yr_ref, ylo_ref, yhi_ref, o_ref, ext_ref, g_ref = refs[7:16]
        hs, yl, yr, near, far, zt0, zt1, gs, ends = refs[16:]
    planes_here, rows, depth = v_ref.shape[1:]
    lane = lanes_of((rows, depth))

    if nz == 2:
        here = lax.axis_index("gz").astype(F32)
        keep_l, keep_r = here, 1.0 - here
    else:
        keep_l, keep_r = 1.0, 1.0
    for c in range(gl_ref.shape[0]):
        left = pltpu.roll(gl_ref[c].astype(F32), depth - 1, 1) * keep_l
        right = pltpu.roll(gr_ref[c].astype(F32), 1, 1) * keep_r
        hs[c] = jnp.where(lane % 2 == 0, left, right)
    near[...] = jnp.concatenate([beside_matrix(depth)] * 2, 0)
    far[...] = halo_matrix(depth)
    if last:
        sens[...] = jnp.zeros_like(sens)
        sums[...] = sum_matrix(depth)
    else:
        gs[...] = jnp.zeros_like(gs)
        ends[...] = ends_matrix(depth)
    face = 4 * rows
    if last:
        yl[...] = ext_ref[2 * face : 3 * face].reshape(4, rows, depth)
        yr[...] = ext_ref[3 * face : 4 * face].reshape(4, rows, depth)
    else:
        yl[...] = yl_ref[:face].astype(F32).reshape(4, rows, depth)
        yr[...] = yr_ref[:face].astype(F32).reshape(4, rows, depth)

    def x_halo(side, low):
        if last:
            return ext_ref[side * face + low : side * face + low + RC]
        return (xl_ref, xr_ref)[side][low : low + RC].astype(F32)

    levels = sr_ref.shape[0]
    tile = (8, depth)
    wr, wi, share = [], [], []
    for m in range(levels):
        d = 6.0 + jnp.full(tile, sr_ref[m], F32)
        s = jnp.full(tile, si_ref[m], F32)
        mag = d * d + s * s
        wr.append(RELAXATION * d / mag)
        wi.append(-RELAXATION * s / mag)
        if last:
            share.append(jnp.full(tile, sh_ref[m], F32))

    def lookup(masks, table):
        out = jnp.broadcast_to(table[0], masks[0].shape)
        for mask, entry in zip(masks, table[1:]):
            out = jnp.where(mask, entry, out)
        return out.reshape(-1, depth)

    row8 = lax.broadcasted_iota(jnp.int32, tile, 0)

    def along_z(first, zt):
        v = v_ref[:, pl.ds(first, PB)].reshape(4 * PB * rows, depth)
        masked = [
            jnp.where(lane // 2 == first + p, hs[c], 0.0).astype(BF16)
            for c in range(4)
            for p in range(PB)
        ]
        out = mm(jnp.concatenate(split(v), 1), near[...]) + mm(jnp.concatenate(masked, 0), far[...])
        zt[...] = out.reshape(4, PB, rows, depth)

    def plane(first, p, zt, put):
        for low in range(0, rows, RC):
            chunk(first, p, low, zt, put)

    def chunk(first, p, low, zt, put):
        x = first + p
        span = slice(low, low + RC)
        mat = m_ref[x, span].reshape(RC // 8, 8, depth)
        masks = [mat == m for m in range(1, levels)]
        w_r, w_i = lookup(masks, wr), lookup(masks, wi)

        def drive(c):
            v = v_ref[c, x, span]
            if p == 0:
                before = v_ref[c, jnp.maximum(x - 1, 0), span]
                before = jnp.where(x == 0, x_halo(0, c * rows + low), before)
            else:
                before = v_ref[c, x - 1, span]
            if p == PB - 1:
                after = v_ref[c, jnp.minimum(x + 1, planes_here - 1), span]
                after = jnp.where(x == planes_here - 1, x_halo(1, c * rows + low), after)
            else:
                after = v_ref[c, x + 1, span]
            total = before + after + s_ref[c, x, span].astype(F32) + zt[c, p, span]
            if low == 0:
                up = pltpu.roll(v, 1, 0)
                top = jnp.where(row8 == 0, yl[c, pl.ds(x, 1), :], up[:8])
                up = jnp.concatenate([top, up[8:]], 0)
            else:
                up = v_ref[c, x, low - 1 : low - 1 + RC]
            if low == rows - RC:
                down = pltpu.roll(v, RC - 1, 0)
                tail = jnp.where(row8 == 7, yr[c, pl.ds(x, 1), :], down[-8:])
                down = jnp.concatenate([down[:-8], tail], 0)
            else:
                down = v_ref[c, x, low + 1 : low + 1 + RC]
            return v, total + up + down

        new = []
        for re in (0, 2):
            v_r, t_r = drive(re)
            v_i, t_i = drive(re + 1)
            keep = 1.0 - RELAXATION
            n_r = keep * v_r + (w_r * t_r - w_i * t_i)
            n_i = keep * v_i + (w_r * t_i + w_i * t_r)
            put(re, span, n_r)
            put(re + 1, span, n_i)
            new += [n_r, n_i]
        if last:
            value[p, span] = lookup(masks, share) * (new[0] * new[2] - new[1] * new[3])

    groups = planes_here // PB

    def store(i):
        part = pl.ds(i * PB, PB)
        return pltpu.make_async_copy(news.at[:, part], o_ref.at[:, part], sems.at[i])

    result = news if last else o_ref

    def group(i, zt, zt_next):
        first = i * PB
        along_z(jnp.minimum(first + PB, planes_here - PB), zt_next)
        for p in range(PB):

            def put(c, span, new, p=p):
                result[c, first + p, span] = new

            plane(first, p, zt, put)
        if last:
            store(i).start()
            parts = [part for p in range(PB) for part in split(value[p])]
            picked = mm(jnp.concatenate(parts, 1), sums[...])
            sens[...] = jnp.where(lane // PB == i, picked, sens[...])
        else:
            put_ends(first, o_ref, ends[...], gs)

    def two(i, carry):
        group(2 * i, zt0, zt1)
        group(2 * i + 1, zt1, zt0)
        return carry

    along_z(0, zt0)
    lax.fori_loop(0, groups // 2, two, 0)

    if not last:
        g_ref[...] = gs[...].astype(BF16)
        sides = (xl_ref, xr_ref, yl_ref, yr_ref)
        centres = jnp.concatenate([r[:face] for r in sides], 0)
        masked = [
            jnp.where(lane // 2 == e, hs[4 + c], 0.0).astype(BF16) for e in range(4) for c in range(4)
        ]
        along = mm(centres, near[:depth]) + mm(jnp.concatenate(masked, 0), far[...])
        for e in range(4):
            zt0[:, e] = along[e * face : (e + 1) * face].reshape(4, rows, depth)
        block = PLANES * planes_here
        corner_l = yl_ref[block : block + 2 * R].astype(F32)
        corner_r = yr_ref[block : block + 2 * R].astype(F32)
        zero = jnp.zeros(tile, F32)
        for e, ref in enumerate(sides):
            level = ref[3 * face : 3 * face + rows].astype(F32).reshape(rows // 8, 8, depth)
            masks = [level == float(m + 1) for m in range(levels)]
            w_r, w_i = lookup(masks, [zero] + wr), lookup(masks, [zero] + wi)

            def near_plane(c, e=e, ref=ref):
                part = slice(c * rows, (c + 1) * rows)
                v = ref[part].astype(F32)
                beyond = ref[face + c * rows : face + (c + 1) * rows].astype(F32)
                if e < 2:
                    inside = v_ref[c, 0 if e == 0 else planes_here - 1]
                    top, low = corner_l[4 * e + c : 4 * e + c + 1], corner_r[4 * e + c : 4 * e + c + 1]
                else:
                    inside = (ylo_ref, yhi_ref)[e - 2][part].astype(F32)
                    corner = corner_l if e == 2 else corner_r
                    top, low = corner[c : c + 1], corner[4 + c : 5 + c]
                source = ref[2 * face + c * rows : 2 * face + (c + 1) * rows].astype(F32)
                total = beyond + inside + source + zt0[c, e]
                up = pltpu.roll(v, 1, 0)
                down = pltpu.roll(v, rows - 1, 0)
                up = jnp.concatenate([jnp.where(row8 == 0, top, up[:8]), up[8:]], 0)
                down = jnp.concatenate([down[:-8], jnp.where(row8 == 7, low, down[-8:])], 0)
                return v, total + up + down

            for re in (0, 2):
                v_r, t_r = near_plane(re)
                v_i, t_i = near_plane(re + 1)
                keep = 1.0 - RELAXATION
                at = e * face + re * rows
                ext_ref[at : at + rows] = keep * v_r + (w_r * t_r - w_i * t_i)
                ext_ref[at + rows : at + 2 * rows] = keep * v_i + (w_r * t_i + w_i * t_r)
    else:
        cells = rows
        row = lax.broadcasted_iota(jnp.int32, (cells, 2 * cells), 0)
        col = lanes_of((cells, 2 * cells))
        half_sum = jnp.zeros((cells, 2 * cells), F32)
        for shift, ref in ((-cells, yl_ref), (0, mid_ref), (cells, yr_ref)):
            weight = jnp.maximum(R + 1 - jnp.abs(col % cells + shift - row), 0)
            tall = ref[PLANES * planes_here + 2 * R :]
            half_sum = half_sum + lax.dot_general(
                weight.astype(F32).astype(BF16),
                tall,
                (((1,), (1,)), ((), ())),
                preferred_element_type=F32,
            )
        row = lax.broadcasted_iota(jnp.int32, (2 * cells, depth), 0)
        col = lanes_of((2 * cells, depth))
        weight = jnp.maximum(R + 1 - jnp.abs(row - R - col), 0).astype(F32).astype(BF16)
        filtered = twice(half_sum, weight) / float((R + 1) ** 4)
        tangent = jnp.tanh(SHARPNESS * (filtered - THRESHOLD))
        total = math.tanh(SHARPNESS * THRESHOLD) + math.tanh(SHARPNESS * (1.0 - THRESHOLD))
        slope = SHARPNESS * (1.0 - tangent * tangent) / total
        weighted = slope * sens[...] * scale
        half = rows // 2
        both = pltpu.roll(weighted[half:], depth // 2, 1)
        sens_ref[:half] = jnp.where(lane[:half] < depth // 2, weighted[:half], both)
        mine = jnp.where(lax.axis_index("gz") == 0, own_ref[...].astype(F32), 0.0)
        sens_ref[half:] = jnp.concatenate([mine, jnp.zeros((8, depth - rows), F32)], 1)
        for i in range(groups):
            store(i).wait()


def twice(value, right):
    high, low = split(value)
    return mm(high, right) + mm(low, right)


def left_twice(left, value):
    high, low = split(value)
    return mm(left, high) + mm(left, low)


SMEM_SPEC = pl.BlockSpec(memory_space=pltpu.SMEM)
VMEM_SPEC = pl.BlockSpec(memory_space=pltpu.VMEM)


def near(value):
    return pltpu.with_memory_space_constraint(value, pltpu.VMEM)


def far_away(value):
    return pltpu.with_memory_space_constraint(value, pltpu.HBM)


def local(kernel, name, operands, specs, shapes, out_specs, scratch, limit, cost):
    return pl.pallas_call(
        kernel,
        in_specs=specs,
        out_specs=out_specs,
        out_shape=shapes,
        scratch_shapes=scratch,
        compiler_params=pltpu.CompilerParams(vmem_limit_bytes=limit << 20),
        cost_estimate=pl.CostEstimate(flops=cost, bytes_accessed=cost, transcendentals=0),
        name=name,
    )(*operands)


def shift(value, axis, up):
    count = lax.axis_size(axis)
    pairs = [(i, i + 1) for i in range(count - 1)]
    return lax.ppermute(value, axis, pairs if up else [(j, i) for i, j in pairs])


def shift_z(g):
    if lax.axis_size("gz") == 2:
        other = lax.ppermute(g, "gz", [(0, 1), (1, 0)])
        return other, other
    return shift(g, "gz", True), shift(g, "gz", False)


def sweeps(tables, share, fields, sources, material, density, owners):
    _, nx, ny, nz = fields.shape
    nz_parts = lax.axis_size("gz")
    hbm = pl.BlockSpec(memory_space=pltpu.HBM)
    held = [near(a) for a in (fields, sources, material)]

    x_shape = jax.ShapeDtypeStruct((PLANES * ny + 2 * R, nz), BF16)
    y_shape = jax.ShapeDtypeStruct((PLANES * nx + 2 * R + 2 * nx, nz), BF16)
    g_shape = jax.ShapeDtypeStruct((4, ny, nz), BF16)
    wide_g = jax.ShapeDtypeStruct((8, ny, nz), BF16)
    xlo, xhi = local(
        x_kernel,
        "x_faces",
        [far_away(a) for a in (fields, sources, material)] + [density],
        [hbm] * 3 + [VMEM_SPEC],
        [x_shape] * 2,
        [VMEM_SPEC] * 2,
        [
            pltpu.VMEM((2, 4, 2, ny, nz), F32),
            pltpu.VMEM((2, 4, ny, nz), BF16),
            pltpu.VMEM((2, ny, nz), jnp.int32),
            pltpu.SemaphoreType.DMA((6,)),
        ],
        8,
        ny * nz * 100,
    )
    xl, xr = shift(xhi, "gx", True), shift(xlo, "gx", False)
    ylo, yhi, g = local(
        pack_kernel,
        "pack_faces",
        held + [density, xl, xr],
        [VMEM_SPEC] * 6,
        [y_shape, y_shape, g_shape],
        [VMEM_SPEC] * 3,
        [
            pltpu.VMEM((4, ny, nz), F32),
            pltpu.VMEM((PLANES, nx, nz), F32),
            pltpu.VMEM((PLANES, nx, nz), F32),
            pltpu.VMEM((PB * nz, nz), BF16),
        ],
        12,
        fields.size * 4,
    )
    yl, yr = shift(yhi, "gy", True), shift(ylo, "gy", False)
    g = local(
        edge_kernel,
        "edge_faces",
        [g, xl, xr, yl, yr],
        [VMEM_SPEC] * 5,
        wide_g,
        VMEM_SPEC,
        [],
        8,
        ny * nz * 40,
    )
    gl, gr = shift_z(g)

    def scratch(parts):
        return [
            pltpu.VMEM((parts, ny, nz), F32),
            pltpu.VMEM((4, nx, nz), F32),
            pltpu.VMEM((4, nx, nz), F32),
            pltpu.VMEM((2 * nz, nz), BF16),
            pltpu.VMEM((nz, nz), BF16),
            pltpu.VMEM((4, PB, ny, nz), F32),
            pltpu.VMEM((4, PB, ny, nz), F32),
        ]

    scale = 1.0 / math.sqrt(nz * nz_parts)
    middle, ext, g = local(
        functools.partial(sweep_kernel, False, nz_parts, scale),
        "sweep_first",
        [*tables, *held, gl, gr, xl, xr, yl, yr, ylo, yhi],
        [SMEM_SPEC] * 2 + [VMEM_SPEC] * 11,
        [pltpu.VMEM(fields.shape, F32), jax.ShapeDtypeStruct((16 * ny, nz), F32), g_shape],
        [VMEM_SPEC] * 3,
        scratch(8) + [pltpu.VMEM((4, ny, nz), F32), pltpu.VMEM((PB * nz, nz), BF16)],
        20,
        fields.size * 20,
    )
    gl, gr = shift_z(g)
    return local(
        functools.partial(sweep_kernel, True, nz_parts, scale),
        "sweep_last",
        [*tables, near(middle), *held[1:], gl, gr, ext, ylo, yl, yr, share, owners],
        [SMEM_SPEC] * 2 + [VMEM_SPEC] * 9 + [SMEM_SPEC, VMEM_SPEC],
        [
            jax.ShapeDtypeStruct(fields.shape, F32),
            jax.ShapeDtypeStruct((ny // 2 + 8, nz), F32),
        ],
        [hbm, VMEM_SPEC],
        scratch(4)
        + [
            pltpu.VMEM((ny, nz), F32),
            pltpu.VMEM((PB, ny, nz), F32),
            pltpu.VMEM(fields.shape, F32),
            pltpu.VMEM((2 * PB * nz, nz), BF16),
            pltpu.SemaphoreType.DMA((nx // PB,)),
        ],
        20,
        fields.size * 20,
    )


def plane_kernel(ngx, ngy, me_ref, got_ref, out_ref, w_ref):
    cells = 64
    nx, ny = ngx * cells, ngy * cells
    columns = ngx * ngy
    half = cells // 2
    for cx in range(ngx):
        for cy in range(ngy):
            c = cx * ngy + cy
            for part in range(2):
                lanes = pl.ds(part * cells, cells)
                w_ref[pl.ds(cy * cells + part * half, half), pl.ds(cx * cells, cells)] = got_ref[
                    c, pl.ds(0, half), lanes
                ]

    def band(n):
        i = lax.broadcasted_iota(jnp.int32, (n, n), 0)
        j = lax.broadcasted_iota(jnp.int32, (n, n), 1)
        return jnp.maximum(R + 1 - jnp.abs(i - j), 0).astype(F32).astype(BF16)

    unit = float((R + 1) ** 4)
    weighted = twice(w_ref[...], band(nx))

    tiles = cells
    owner = jnp.concatenate([got_ref[c, pl.ds(half, 1), pl.ds(0, tiles)] for c in range(columns)], 0)
    mine = owner == me_ref[0].astype(F32)
    flag = jnp.where(mine, 1.0, 0.0)
    a = lax.broadcasted_iota(jnp.int32, (tiles, tiles), 0)
    b = lax.broadcasted_iota(jnp.int32, (tiles, tiles), 1)
    rank = mm(flag.astype(BF16), jnp.where(a < b, 1.0, 0.0).astype(BF16))
    number = lanes_of((columns, tiles))
    column = lax.broadcasted_iota(jnp.int32, (columns, 1), 0)
    rows, blocks = [], []
    for k in range(MOST):
        chosen = mine & (rank == float(k))
        tile = jnp.sum(jnp.where(chosen, number, 0), axis=1, keepdims=True)
        there = jnp.sum(jnp.where(chosen, 1, 0), axis=1, keepdims=True)
        rows.append((column % ngy) * cells + (tile % (cells // TS)) * TS)
        block = (column // ngy) * (cells // TS) + tile // (cells // TS)
        blocks.append(jnp.where(there > 0, block, -1))
    row = jnp.concatenate(rows, 0)
    block = jnp.concatenate(blocks, 0)
    slots = MOST * columns
    across = lax.broadcasted_iota(jnp.int32, (slots, ny), 1)
    lefts = [
        jnp.maximum(R + 1 - jnp.abs(row + j - across), 0).astype(F32).astype(BF16)
        for j in range(TS)
    ]
    lines = left_twice(jnp.concatenate(lefts, 0), weighted)
    keep = lanes_of((slots, nx)) // TS == block
    from_x = lax.broadcasted_iota(jnp.int32, (nx, TS * TS), 0) % TS
    to_q = lanes_of((nx, TS * TS))
    out = jnp.zeros((slots, TS * TS), F32)
    for j in range(TS):
        fold = jnp.where(to_q == from_x * TS + j, 1.0, 0.0).astype(BF16)
        out = out + twice(jnp.where(keep, lines[j * slots : (j + 1) * slots], 0.0), fold)
    out = out / unit
    for k in range(MOST):
        out_ref[0, :, pl.ds(k * TS * TS, TS * TS)] = out[k * columns : (k + 1) * columns]


def on_device(fields, sources, material, shift_real, shift_imag, design_share, density, owner_map):
    ngx, ngy = lax.axis_size("gx"), lax.axis_size("gy")
    columns = ngx * ngy
    cells = density.shape[0]
    tables = (shift_real, shift_imag)
    owners = jnp.broadcast_to(owner_map.reshape(1, -1), (8, cells))
    final, partial = sweeps(tables, design_share, fields, sources, material, density, owners)
    partial = jnp.sum(lax.all_gather(partial, "gz"), 0)
    copies = jnp.broadcast_to(partial[None], (columns, *partial.shape))
    plane = lax.all_to_all(copies, ("gx", "gy"), split_axis=0, concat_axis=0)
    me = (lax.axis_index("gx") * ngy + lax.axis_index("gy")).reshape(1)
    owned = pl.pallas_call(
        functools.partial(plane_kernel, ngx, ngy),
        in_specs=[SMEM_SPEC, VMEM_SPEC],
        out_specs=VMEM_SPEC,
        out_shape=jax.ShapeDtypeStruct((1, columns, MOST * TS * TS), F32),
        scratch_shapes=[pltpu.VMEM((ngy * cells, ngx * cells), F32)],
        compiler_params=pltpu.CompilerParams(vmem_limit_bytes=16 << 20),
        name="plane",
    )(me, plane)
    return (final, owned)


def solution(mesh):
    placed = (
        P(None, "gx", "gy", "gz"),
        P(None, "gx", "gy", "gz"),
        P("gx", "gy", "gz"),
        P(),
        P(),
        P(),
        P("gx", "gy"),
        P("gx", "gy", None, None),
    )
    return jax.shard_map(
        on_device,
        mesh=mesh,
        in_specs=placed,
        out_specs=(P(None, "gx", "gy", "gz"), P(("gx", "gy"), None, None)),
        check_vma=False,
    )
```

```python
import functools
import math

import jax
import jax.numpy as jnp
from jax import lax
from jax.experimental import pallas as pl
from jax.experimental.pallas import tpu as pltpu
from jax.sharding import PartitionSpec as P

R = 8
TS = 8
MOST = 8
RELAXATION = 0.8
SHARPNESS = 8.0
THRESHOLD = 0.5
PB = 8
RC = 16
F32 = jnp.float32
BF16 = jnp.bfloat16


def lanes_of(shape):
    return lax.broadcasted_iota(jnp.int32, shape, len(shape) - 1)


def ends_matrix(depth):
    k = lax.broadcasted_iota(jnp.int32, (PB * depth, depth), 0)
    j = lax.broadcasted_iota(jnp.int32, (PB * depth, depth), 1) % (2 * PB)
    even = (k % depth == 0) & (j == 2 * (k // depth))
    odd = (k % depth == depth - 1) & (j == 2 * (k // depth) + 1)
    return jnp.where(even | odd, 1.0, 0.0).astype(BF16)


def beside_matrix(depth):
    z = lax.broadcasted_iota(jnp.int32, (depth, depth), 0)
    j = lax.broadcasted_iota(jnp.int32, (depth, depth), 1)
    return jnp.where(jnp.abs(z - j) == 1, 1.0, 0.0).astype(BF16)


def halo_matrix(depth):
    j = lax.broadcasted_iota(jnp.int32, (depth, depth), 0)
    z = lax.broadcasted_iota(jnp.int32, (depth, depth), 1)
    even = (z == 0) & (j % 2 == 0)
    odd = (z == depth - 1) & (j % 2 == 1)
    return jnp.where(even | odd, 1.0, 0.0).astype(BF16)


def sum_matrix(depth):
    k = lax.broadcasted_iota(jnp.int32, (2 * PB * depth, depth), 0) // (2 * depth)
    j = lax.broadcasted_iota(jnp.int32, (2 * PB * depth, depth), 1) % PB
    return jnp.where(k == j, 1.0, 0.0).astype(BF16)


def split(value):
    high = value.astype(BF16)
    return high, (value - high.astype(F32)).astype(BF16)


def mm(a, b):
    return lax.dot_general(a, b, (((1,), (0,)), ((), ())), preferred_element_type=F32)


def put_ends(first, ref, ends, gs):
    rows, depth = ref.shape[2:]
    high = ref[:, pl.ds(first, PB)].astype(BF16)
    beside = [high[:, p].reshape(4 * rows, depth) for p in range(PB)]
    picked = mm(jnp.concatenate(beside, 1), ends).reshape(4, rows, depth)
    here = lanes_of((rows, depth)) // (2 * PB) == first // PB
    for c in range(4):
        gs[c] = jnp.where(here, picked[c], gs[c])


def paired(value):
    high = value.astype(BF16).astype(F32)
    return jnp.concatenate([high, value - high], 1)


PLANES = 13


def x_kernel(v_ref, s_ref, m_ref, d_ref, xlo_ref, xhi_ref, vs, ss, ms, sems):
    last = v_ref.shape[1] - 1
    rows, depth = v_ref.shape[2:]
    sides = ((0, 0, 1), (last, last - 1, 0))
    copies = []
    for i, (x, second, _) in enumerate(sides):
        copies.append(
            [
                pltpu.make_async_copy(
                    v_ref.at[:, pl.ds(min(x, second), 2)], vs.at[i], sems.at[3 * i]
                ),
                pltpu.make_async_copy(s_ref.at[:, x], ss.at[i], sems.at[3 * i + 1]),
                pltpu.make_async_copy(m_ref.at[x], ms.at[i], sems.at[3 * i + 2]),
            ]
        )
    for side in copies:
        for copy in side:
            copy.start()
    cells = d_ref.shape[0]
    none = jnp.zeros((R, depth), F32)
    for i, (out_ref, start) in enumerate(((xlo_ref, 0), (xhi_ref, cells - R))):
        strip = jnp.concatenate([paired(d_ref[start : start + R, :]), none], 0)
        out_ref[PLANES * rows :] = strip.astype(BF16)
        for copy in copies[i]:
            copy.wait()
        inner = sides[i][2]
        out_ref[: 4 * rows] = vs[i, :, 1 - inner].astype(BF16).reshape(4 * rows, depth)
        out_ref[4 * rows : 8 * rows] = vs[i, :, inner].astype(BF16).reshape(4 * rows, depth)
        out_ref[8 * rows : 12 * rows] = ss[i].reshape(4 * rows, depth)
        out_ref[12 * rows : 13 * rows] = (ms[i] + 1).astype(F32).astype(BF16)


def pack_kernel(v_ref, s_ref, m_ref, ylo_ref, yhi_ref, g_ref, gs, ylo, yhi, ends):
    rows, depth = v_ref.shape[2:]
    gs[...] = jnp.zeros_like(gs)
    ends[...] = ends_matrix(depth)

    def group(i, carry):
        first = i * PB
        put_ends(first, v_ref, ends[...], gs)
        for p in range(PB):
            x = first + p
            here = pl.ds(x, 1)
            level = (m_ref[x] + 1).astype(F32)
            for out, edge, inner, low in ((ylo, 0, 1, 0), (yhi, rows - 1, rows - 2, rows - 16)):
                for c in range(4):
                    out[c, here, :] = v_ref[c, x, edge : edge + 1, :]
                    out[4 + c, here, :] = v_ref[c, x, inner : inner + 1, :]
                    near_edge = s_ref[c, x, low : low + 16, :].astype(F32)
                    out[8 + c, here, :] = near_edge[edge - low : edge - low + 1]
                out[12, here, :] = level[edge : edge + 1]
        return carry

    lax.fori_loop(0, v_ref.shape[1] // PB, group, 0)
    g_ref[...] = gs[...].astype(BF16)
    for out_ref, rows_out in ((ylo_ref, ylo), (yhi_ref, yhi)):
        out_ref[...] = rows_out[...].astype(BF16).reshape(out_ref.shape)


def corner_kernel(lo_ref, hi_ref, d_ref, xl_ref, xr_ref, _, ylo_ref, yhi_ref):
    block, depth = lo_ref.shape
    cells = d_ref.shape[0]
    rows = (xl_ref.shape[0] - 2 * R) // PLANES
    strips = [r[PLANES * rows :].astype(F32)[:R] for r in (xl_ref, xr_ref)]
    filler = jnp.zeros((cells - 2 * R, depth), F32)
    tall = jnp.concatenate([strips[0], paired(d_ref[...]), strips[1], filler], 0).astype(BF16)
    for out_ref, from_ref, edge, low in (
        (ylo_ref, lo_ref, 0, 0),
        (yhi_ref, hi_ref, rows - 1, rows - 16),
    ):
        out_ref[:block] = from_ref[...]
        corners = [
            r[c * rows + low : c * rows + low + 16].astype(F32)[edge - low : edge - low + 1]
            for r in (xl_ref, xr_ref)
            for c in range(4)
        ]
        corners.append(jnp.zeros((2 * R - 8, depth), F32))
        out_ref[block : block + 2 * R] = jnp.concatenate(corners, 0).astype(BF16)
        out_ref[block + 2 * R :] = tall


def inside_kernel(start, v_ref, s_ref, t_ref, token_ref, near, zt0, zt1):
    planes_here, rows, depth = v_ref.shape[1:]
    token_ref[...] = jnp.zeros_like(token_ref)
    near[...] = jnp.concatenate([beside_matrix(depth)] * 2, 0)
    row8 = lax.broadcasted_iota(jnp.int32, (8, depth), 0)
    count = t_ref.shape[1]

    def along_z(first, zt):
        v = v_ref[:, pl.ds(first, PB)].reshape(4 * PB * rows, depth)
        zt[...] = mm(jnp.concatenate(split(v), 1), near[...]).reshape(4, PB, rows, depth)

    def group(i, zt, zt_next):
        first = start + i * PB
        along_z(jnp.minimum(first + PB, start + count - PB), zt_next)
        for p in range(PB):
            x = first + p
            for low in range(0, rows, RC):
                span = slice(low, low + RC)
                for c in range(4):
                    v = v_ref[c, x, span]
                    before = v_ref[c, jnp.maximum(x - 1, 0), span]
                    after = v_ref[c, jnp.minimum(x + 1, planes_here - 1), span]
                    if p == 0:
                        before = jnp.where(x == 0, 0.0, before)
                    if p == PB - 1:
                        after = jnp.where(x == planes_here - 1, 0.0, after)
                    if low == 0:
                        up = pltpu.roll(v, 1, 0)
                        up = jnp.concatenate([jnp.where(row8 == 0, 0.0, up[:8]), up[8:]], 0)
                    else:
                        up = v_ref[c, x, low - 1 : low - 1 + RC]
                    if low == rows - RC:
                        down = pltpu.roll(v, RC - 1, 0)
                        down = jnp.concatenate([down[:-8], jnp.where(row8 == 7, 0.0, down[-8:])], 0)
                    else:
                        down = v_ref[c, x, low + 1 : low + 1 + RC]
                    total = before + after + s_ref[c, x, span].astype(F32) + zt[c, p, span]
                    t_ref[c, i * PB + p, span] = total + up + down

    def two(i, carry):
        group(2 * i, zt0, zt1)
        group(2 * i + 1, zt1, zt0)
        return carry

    along_z(start, zt0)
    lax.fori_loop(0, count // (2 * PB), two, 0)


def edge_kernel(g_ref, xl_ref, xr_ref, yl_ref, yr_ref, _, out_ref):
    parts, rows, depth = g_ref.shape
    beside = [r[: 4 * rows] for r in (xl_ref, xr_ref, yl_ref, yr_ref)]
    picked = mm(jnp.concatenate(beside, 1), ends_matrix(depth)[: 4 * depth])
    out_ref[:4] = g_ref[...]
    out_ref[4:] = picked.astype(BF16).reshape(4, rows, depth)


def sweep_kernel(last, nz, scale, *refs):
    sr_ref, si_ref, v_ref, s_ref, m_ref, gl_ref, gr_ref = refs[:7]
    if last:
        ext_ref, mid_ref, yl_ref, yr_ref, sh_ref, own_ref, o_ref, sens_ref = refs[7:15]
        hs, yl, yr, near, far, zt0, zt1, sens, value, news, sums, sems = refs[15:]
    else:
        xl_ref, xr_ref, yl_ref, yr_ref, ylo_ref, yhi_ref = refs[7:13]
        ta_ref, tb_ref, o_ref, ext_ref, g_ref = refs[13:18]
        hs, yl, yr, near, far, zt0, zt1, gs, ends = refs[18:]
    planes_here, rows, depth = v_ref.shape[1:]
    lane = lanes_of((rows, depth))

    if nz == 2:
        here = lax.axis_index("gz").astype(F32)
        keep_l, keep_r = here, 1.0 - here
    else:
        keep_l, keep_r = 1.0, 1.0
    for c in range(gl_ref.shape[0]):
        left = pltpu.roll(gl_ref[c].astype(F32), depth - 1, 1) * keep_l
        right = pltpu.roll(gr_ref[c].astype(F32), 1, 1) * keep_r
        hs[c] = jnp.where(lane % 2 == 0, left, right)
    near[...] = jnp.concatenate([beside_matrix(depth)] * 2, 0)
    far[...] = halo_matrix(depth)
    if last:
        sens[...] = jnp.zeros_like(sens)
        sums[...] = sum_matrix(depth)
    else:
        gs[...] = jnp.zeros_like(gs)
        ends[...] = ends_matrix(depth)
    face = 4 * rows
    if last:
        yl[...] = ext_ref[2 * face : 3 * face].reshape(4, rows, depth)
        yr[...] = ext_ref[3 * face : 4 * face].reshape(4, rows, depth)
    else:
        yl[...] = yl_ref[:face].astype(F32).reshape(4, rows, depth)
        yr[...] = yr_ref[:face].astype(F32).reshape(4, rows, depth)

    def x_halo(side, low):
        if last:
            return ext_ref[side * face + low : side * face + low + RC]
        return (xl_ref, xr_ref)[side][low : low + RC].astype(F32)

    levels = sr_ref.shape[0]
    tile = (8, depth)
    wr, wi, share = [], [], []
    for m in range(levels):
        d = 6.0 + jnp.full(tile, sr_ref[m], F32)
        s = jnp.full(tile, si_ref[m], F32)
        mag = d * d + s * s
        wr.append(RELAXATION * d / mag)
        wi.append(-RELAXATION * s / mag)
        if last:
            share.append(jnp.full(tile, sh_ref[m], F32))

    def lookup(masks, table):
        out = jnp.broadcast_to(table[0], masks[0].shape)
        for mask, entry in zip(masks, table[1:]):
            out = jnp.where(mask, entry, out)
        return out.reshape(-1, depth)

    row8 = lax.broadcasted_iota(jnp.int32, tile, 0)

    def along_z(first, zt):
        masked = [
            jnp.where(lane // 2 == first + p, hs[c], 0.0).astype(BF16)
            for c in range(4)
            for p in range(PB)
        ]
        out = mm(jnp.concatenate(masked, 0), far[...])
        if last:
            v = v_ref[:, pl.ds(first, PB)].reshape(4 * PB * rows, depth)
            out = out + mm(jnp.concatenate(split(v), 1), near[...])
        zt[...] = out.reshape(4, PB, rows, depth)

    def plane(first, p, zt, put, inside=None):
        for low in range(0, rows, RC):
            chunk(first, p, low, zt, put, inside)

    def chunk(first, p, low, zt, put, inside):
        x = first + p
        span = slice(low, low + RC)
        mat = m_ref[x, span].reshape(RC // 8, 8, depth)
        masks = [mat == m for m in range(1, levels)]
        w_r, w_i = lookup(masks, wr), lookup(masks, wi)

        def join(c):
            t_ref, t_start = inside
            total = t_ref[c, x - t_start, span] + zt[c, p, span]
            if p == 0:
                total = total + jnp.where(x == 0, x_halo(0, c * rows + low), 0.0)
            if p == PB - 1:
                total = total + jnp.where(x == planes_here - 1, x_halo(1, c * rows + low), 0.0)
            if low == 0:
                top = total[:8] + jnp.where(row8 == 0, yl[c, pl.ds(x, 1), :], 0.0)
                total = jnp.concatenate([top, total[8:]], 0)
            if low == rows - RC:
                tail = total[-8:] + jnp.where(row8 == 7, yr[c, pl.ds(x, 1), :], 0.0)
                total = jnp.concatenate([total[:-8], tail], 0)
            return v_ref[c, x, span], total

        def drive(c):
            if not last:
                return join(c)
            v = v_ref[c, x, span]
            if p == 0:
                before = v_ref[c, jnp.maximum(x - 1, 0), span]
                before = jnp.where(x == 0, x_halo(0, c * rows + low), before)
            else:
                before = v_ref[c, x - 1, span]
            if p == PB - 1:
                after = v_ref[c, jnp.minimum(x + 1, planes_here - 1), span]
                after = jnp.where(x == planes_here - 1, x_halo(1, c * rows + low), after)
            else:
                after = v_ref[c, x + 1, span]
            total = before + after + s_ref[c, x, span].astype(F32) + zt[c, p, span]
            if low == 0:
                up = pltpu.roll(v, 1, 0)
                top = jnp.where(row8 == 0, yl[c, pl.ds(x, 1), :], up[:8])
                up = jnp.concatenate([top, up[8:]], 0)
            else:
                up = v_ref[c, x, low - 1 : low - 1 + RC]
            if low == rows - RC:
                down = pltpu.roll(v, RC - 1, 0)
                tail = jnp.where(row8 == 7, yr[c, pl.ds(x, 1), :], down[-8:])
                down = jnp.concatenate([down[:-8], tail], 0)
            else:
                down = v_ref[c, x, low + 1 : low + 1 + RC]
            return v, total + up + down

        new = []
        for re in (0, 2):
            v_r, t_r = drive(re)
            v_i, t_i = drive(re + 1)
            keep = 1.0 - RELAXATION
            n_r = keep * v_r + (w_r * t_r - w_i * t_i)
            n_i = keep * v_i + (w_r * t_i + w_i * t_r)
            put(re, span, n_r)
            put(re + 1, span, n_i)
            new += [n_r, n_i]
        if last:
            value[p, span] = lookup(masks, share) * (new[0] * new[2] - new[1] * new[3])

    groups = planes_here // PB

    def store(i):
        part = pl.ds(i * PB, PB)
        return pltpu.make_async_copy(news.at[:, part], o_ref.at[:, part], sems.at[i])

    result = news if last else o_ref

    def group(i, zt, zt_next, inside=None):
        first = i * PB
        along_z(jnp.minimum(first + PB, planes_here - PB), zt_next)
        for p in range(PB):

            def put(c, span, new, p=p):
                result[c, first + p, span] = new

            plane(first, p, zt, put, inside)
        if last:
            store(i).start()
            parts = [part for p in range(PB) for part in split(value[p])]
            picked = mm(jnp.concatenate(parts, 1), sums[...])
            sens[...] = jnp.where(lane // PB == i, picked, sens[...])
        else:
            put_ends(first, o_ref, ends[...], gs)

    def pairs(begin, end, inside=None):
        def two(i, carry):
            group(2 * i, zt0, zt1, inside)
            group(2 * i + 1, zt1, zt0, inside)
            return carry

        lax.fori_loop(begin, end, two, 0)

    along_z(0, zt0)
    if last:
        pairs(0, groups // 2)
    else:
        cut = ta_ref.shape[1]
        pairs(0, cut // (2 * PB), (ta_ref, 0))
        pairs(cut // (2 * PB), groups // 2, (tb_ref, cut))

    if not last:
        g_ref[...] = gs[...].astype(BF16)
        sides = (xl_ref, xr_ref, yl_ref, yr_ref)
        centres = jnp.concatenate([r[:face] for r in sides], 0)
        masked = [
            jnp.where(lane // 2 == e, hs[4 + c], 0.0).astype(BF16) for e in range(4) for c in range(4)
        ]
        along = mm(centres, near[:depth]) + mm(jnp.concatenate(masked, 0), far[...])
        for e in range(4):
            zt0[:, e] = along[e * face : (e + 1) * face].reshape(4, rows, depth)
        block = PLANES * planes_here
        corner_l = yl_ref[block : block + 2 * R].astype(F32)
        corner_r = yr_ref[block : block + 2 * R].astype(F32)
        zero = jnp.zeros(tile, F32)
        for e, ref in enumerate(sides):
            level = ref[3 * face : 3 * face + rows].astype(F32).reshape(rows // 8, 8, depth)
            masks = [level == float(m + 1) for m in range(levels)]
            w_r, w_i = lookup(masks, [zero] + wr), lookup(masks, [zero] + wi)

            def near_plane(c, e=e, ref=ref):
                part = slice(c * rows, (c + 1) * rows)
                v = ref[part].astype(F32)
                beyond = ref[face + c * rows : face + (c + 1) * rows].astype(F32)
                if e < 2:
                    inside = v_ref[c, 0 if e == 0 else planes_here - 1]
                    top, low = corner_l[4 * e + c : 4 * e + c + 1], corner_r[4 * e + c : 4 * e + c + 1]
                else:
                    inside = (ylo_ref, yhi_ref)[e - 2][part].astype(F32)
                    corner = corner_l if e == 2 else corner_r
                    top, low = corner[c : c + 1], corner[4 + c : 5 + c]
                source = ref[2 * face + c * rows : 2 * face + (c + 1) * rows].astype(F32)
                total = beyond + inside + source + zt0[c, e]
                up = pltpu.roll(v, 1, 0)
                down = pltpu.roll(v, rows - 1, 0)
                up = jnp.concatenate([jnp.where(row8 == 0, top, up[:8]), up[8:]], 0)
                down = jnp.concatenate([down[:-8], jnp.where(row8 == 7, low, down[-8:])], 0)
                return v, total + up + down

            for re in (0, 2):
                v_r, t_r = near_plane(re)
                v_i, t_i = near_plane(re + 1)
                keep = 1.0 - RELAXATION
                at = e * face + re * rows
                ext_ref[at : at + rows] = keep * v_r + (w_r * t_r - w_i * t_i)
                ext_ref[at + rows : at + 2 * rows] = keep * v_i + (w_r * t_i + w_i * t_r)
    else:
        cells = rows
        row = lax.broadcasted_iota(jnp.int32, (cells, 2 * cells), 0)
        col = lanes_of((cells, 2 * cells))
        half_sum = jnp.zeros((cells, 2 * cells), F32)
        for shift, ref in ((-cells, yl_ref), (0, mid_ref), (cells, yr_ref)):
            weight = jnp.maximum(R + 1 - jnp.abs(col % cells + shift - row), 0)
            tall = ref[PLANES * planes_here + 2 * R :]
            half_sum = half_sum + lax.dot_general(
                weight.astype(F32).astype(BF16),
                tall,
                (((1,), (1,)), ((), ())),
                preferred_element_type=F32,
            )
        row = lax.broadcasted_iota(jnp.int32, (2 * cells, depth), 0)
        col = lanes_of((2 * cells, depth))
        weight = jnp.maximum(R + 1 - jnp.abs(row - R - col), 0).astype(F32).astype(BF16)
        filtered = twice(half_sum, weight) / float((R + 1) ** 4)
        tangent = jnp.tanh(SHARPNESS * (filtered - THRESHOLD))
        total = math.tanh(SHARPNESS * THRESHOLD) + math.tanh(SHARPNESS * (1.0 - THRESHOLD))
        slope = SHARPNESS * (1.0 - tangent * tangent) / total
        weighted = slope * sens[...] * scale
        half = rows // 2
        both = pltpu.roll(weighted[half:], depth // 2, 1)
        sens_ref[:half] = jnp.where(lane[:half] < depth // 2, weighted[:half], both)
        mine = jnp.where(lax.axis_index("gz") == 0, own_ref[...].astype(F32), 0.0)
        sens_ref[half:] = jnp.concatenate([mine, jnp.zeros((8, depth - rows), F32)], 1)
        for i in range(groups):
            store(i).wait()


def twice(value, right):
    high, low = split(value)
    return mm(high, right) + mm(low, right)


def left_twice(left, value):
    high, low = split(value)
    return mm(left, high) + mm(left, low)


SMEM_SPEC = pl.BlockSpec(memory_space=pltpu.SMEM)
VMEM_SPEC = pl.BlockSpec(memory_space=pltpu.VMEM)


def near(value):
    return pltpu.with_memory_space_constraint(value, pltpu.VMEM)


def far_away(value):
    return pltpu.with_memory_space_constraint(value, pltpu.HBM)


def local(kernel, name, operands, specs, shapes, out_specs, scratch, limit, cost):
    return pl.pallas_call(
        kernel,
        in_specs=specs,
        out_specs=out_specs,
        out_shape=shapes,
        scratch_shapes=scratch,
        compiler_params=pltpu.CompilerParams(vmem_limit_bytes=limit << 20),
        cost_estimate=pl.CostEstimate(flops=cost, bytes_accessed=cost, transcendentals=0),
        name=name,
    )(*operands)


def shift(value, axis, up):
    count = lax.axis_size(axis)
    pairs = [(i, i + 1) for i in range(count - 1)]
    return lax.ppermute(value, axis, pairs if up else [(j, i) for i, j in pairs])


def shift_z(g):
    if lax.axis_size("gz") == 2:
        other = lax.ppermute(g, "gz", [(0, 1), (1, 0)])
        return other, other
    return shift(g, "gz", True), shift(g, "gz", False)


def sweeps(tables, share, fields, sources, material, density, owners):
    _, nx, ny, nz = fields.shape
    nz_parts = lax.axis_size("gz")
    hbm = pl.BlockSpec(memory_space=pltpu.HBM)
    held = [near(a) for a in (fields, sources, material)]

    x_shape = jax.ShapeDtypeStruct((PLANES * ny + 2 * R, nz), BF16)
    y_shape = jax.ShapeDtypeStruct((PLANES * nx + 2 * R + 2 * nx, nz), BF16)
    g_shape = jax.ShapeDtypeStruct((4, ny, nz), BF16)
    wide_g = jax.ShapeDtypeStruct((8, ny, nz), BF16)
    xlo, xhi = local(
        x_kernel,
        "x_faces",
        [far_away(a) for a in (fields, sources, material)] + [density],
        [hbm] * 3 + [VMEM_SPEC],
        [x_shape] * 2,
        [VMEM_SPEC] * 2,
        [
            pltpu.VMEM((2, 4, 2, ny, nz), F32),
            pltpu.VMEM((2, 4, ny, nz), BF16),
            pltpu.VMEM((2, ny, nz), jnp.int32),
            pltpu.SemaphoreType.DMA((6,)),
        ],
        8,
        ny * nz * 100,
    )
    xl, xr = shift(xhi, "gx", True), shift(xlo, "gx", False)
    part_shape = jax.ShapeDtypeStruct((PLANES * nx, nz), BF16)
    lo, hi, g = local(
        pack_kernel,
        "pack_faces",
        held,
        [VMEM_SPEC] * 3,
        [part_shape, part_shape, g_shape],
        [VMEM_SPEC] * 3,
        [
            pltpu.VMEM((4, ny, nz), F32),
            pltpu.VMEM((PLANES, nx, nz), F32),
            pltpu.VMEM((PLANES, nx, nz), F32),
            pltpu.VMEM((PB * nz, nz), BF16),
        ],
        12,
        fields.size * 4,
    )
    cut = nx // 2
    inside = [
        local(
            functools.partial(inside_kernel, start),
            "inside",
            held[:2],
            [VMEM_SPEC] * 2,
            [pltpu.VMEM((4, cut, ny, nz), F32), jax.ShapeDtypeStruct((8, nz), F32)],
            [VMEM_SPEC] * 2,
            [
                pltpu.VMEM((2 * nz, nz), BF16),
                pltpu.VMEM((4, PB, ny, nz), F32),
                pltpu.VMEM((4, PB, ny, nz), F32),
            ],
            8,
            fields.size * 5,
        )
        for start in (0, cut)
    ]
    ylo, yhi = local(
        corner_kernel,
        "corners",
        [lo, hi, density, xl, xr, inside[0][1]],
        [VMEM_SPEC] * 6,
        [y_shape] * 2,
        [VMEM_SPEC] * 2,
        [],
        8,
        ny * nz * 40,
    )
    yl, yr = shift(yhi, "gy", True), shift(ylo, "gy", False)
    g = local(
        edge_kernel,
        "edge_faces",
        [g, xl, xr, yl, yr, inside[1][1]],
        [VMEM_SPEC] * 6,
        wide_g,
        VMEM_SPEC,
        [],
        8,
        ny * nz * 40,
    )
    gl, gr = shift_z(g)

    def scratch(parts):
        return [
            pltpu.VMEM((parts, ny, nz), F32),
            pltpu.VMEM((4, nx, nz), F32),
            pltpu.VMEM((4, nx, nz), F32),
            pltpu.VMEM((2 * nz, nz), BF16),
            pltpu.VMEM((nz, nz), BF16),
            pltpu.VMEM((4, PB, ny, nz), F32),
            pltpu.VMEM((4, PB, ny, nz), F32),
        ]

    scale = 1.0 / math.sqrt(nz * nz_parts)
    middle, ext, g = local(
        functools.partial(sweep_kernel, False, nz_parts, scale),
        "sweep_first",
        [*tables, held[0], density, held[2], gl, gr, xl, xr, yl, yr, ylo, yhi, *(near(t) for t, _ in inside)],
        [SMEM_SPEC] * 2 + [VMEM_SPEC] * 13,
        [pltpu.VMEM(fields.shape, F32), jax.ShapeDtypeStruct((16 * ny, nz), F32), g_shape],
        [VMEM_SPEC] * 3,
        scratch(8) + [pltpu.VMEM((4, ny, nz), F32), pltpu.VMEM((PB * nz, nz), BF16)],
        20,
        fields.size * 20,
    )
    gl, gr = shift_z(g)
    return local(
        functools.partial(sweep_kernel, True, nz_parts, scale),
        "sweep_last",
        [*tables, near(middle), *held[1:], gl, gr, ext, ylo, yl, yr, share, owners],
        [SMEM_SPEC] * 2 + [VMEM_SPEC] * 9 + [SMEM_SPEC, VMEM_SPEC],
        [
            jax.ShapeDtypeStruct(fields.shape, F32),
            jax.ShapeDtypeStruct((ny // 2 + 8, nz), F32),
        ],
        [hbm, VMEM_SPEC],
        scratch(4)
        + [
            pltpu.VMEM((ny, nz), F32),
            pltpu.VMEM((PB, ny, nz), F32),
            pltpu.VMEM(fields.shape, F32),
            pltpu.VMEM((2 * PB * nz, nz), BF16),
            pltpu.SemaphoreType.DMA((nx // PB,)),
        ],
        20,
        fields.size * 20,
    )


def plane_kernel(ngx, ngy, me_ref, got_ref, out_ref, w_ref):
    cells = 64
    nx, ny = ngx * cells, ngy * cells
    columns = ngx * ngy
    half = cells // 2
    for cx in range(ngx):
        for cy in range(ngy):
            c = cx * ngy + cy
            for part in range(2):
                lanes = pl.ds(part * cells, cells)
                w_ref[pl.ds(cy * cells + part * half, half), pl.ds(cx * cells, cells)] = got_ref[
                    c, pl.ds(0, half), lanes
                ]

    def band(n):
        i = lax.broadcasted_iota(jnp.int32, (n, n), 0)
        j = lax.broadcasted_iota(jnp.int32, (n, n), 1)
        return jnp.maximum(R + 1 - jnp.abs(i - j), 0).astype(F32).astype(BF16)

    unit = float((R + 1) ** 4)
    weighted = twice(w_ref[...], band(nx))

    tiles = cells
    owner = jnp.concatenate([got_ref[c, pl.ds(half, 1), pl.ds(0, tiles)] for c in range(columns)], 0)
    mine = owner == me_ref[0].astype(F32)
    flag = jnp.where(mine, 1.0, 0.0)
    a = lax.broadcasted_iota(jnp.int32, (tiles, tiles), 0)
    b = lax.broadcasted_iota(jnp.int32, (tiles, tiles), 1)
    rank = mm(flag.astype(BF16), jnp.where(a < b, 1.0, 0.0).astype(BF16))
    number = lanes_of((columns, tiles))
    column = lax.broadcasted_iota(jnp.int32, (columns, 1), 0)
    rows, blocks = [], []
    for k in range(MOST):
        chosen = mine & (rank == float(k))
        tile = jnp.sum(jnp.where(chosen, number, 0), axis=1, keepdims=True)
        there = jnp.sum(jnp.where(chosen, 1, 0), axis=1, keepdims=True)
        rows.append((column % ngy) * cells + (tile % (cells // TS)) * TS)
        block = (column // ngy) * (cells // TS) + tile // (cells // TS)
        blocks.append(jnp.where(there > 0, block, -1))
    row = jnp.concatenate(rows, 0)
    block = jnp.concatenate(blocks, 0)
    slots = MOST * columns
    across = lax.broadcasted_iota(jnp.int32, (slots, ny), 1)
    lefts = [
        jnp.maximum(R + 1 - jnp.abs(row + j - across), 0).astype(F32).astype(BF16)
        for j in range(TS)
    ]
    lines = left_twice(jnp.concatenate(lefts, 0), weighted)
    keep = lanes_of((slots, nx)) // TS == block
    from_x = lax.broadcasted_iota(jnp.int32, (nx, TS * TS), 0) % TS
    to_q = lanes_of((nx, TS * TS))
    out = jnp.zeros((slots, TS * TS), F32)
    for j in range(TS):
        fold = jnp.where(to_q == from_x * TS + j, 1.0, 0.0).astype(BF16)
        out = out + twice(jnp.where(keep, lines[j * slots : (j + 1) * slots], 0.0), fold)
    out = out / unit
    for k in range(MOST):
        out_ref[0, :, pl.ds(k * TS * TS, TS * TS)] = out[k * columns : (k + 1) * columns]


def on_device(fields, sources, material, shift_real, shift_imag, design_share, density, owner_map):
    ngx, ngy = lax.axis_size("gx"), lax.axis_size("gy")
    columns = ngx * ngy
    cells = density.shape[0]
    tables = (shift_real, shift_imag)
    owners = jnp.broadcast_to(owner_map.reshape(1, -1), (8, cells))
    final, partial = sweeps(tables, design_share, fields, sources, material, density, owners)
    partial = jnp.sum(lax.all_gather(partial, "gz"), 0)
    copies = jnp.broadcast_to(partial[None], (columns, *partial.shape))
    plane = lax.all_to_all(copies, ("gx", "gy"), split_axis=0, concat_axis=0)
    me = (lax.axis_index("gx") * ngy + lax.axis_index("gy")).reshape(1)
    owned = pl.pallas_call(
        functools.partial(plane_kernel, ngx, ngy),
        in_specs=[SMEM_SPEC, VMEM_SPEC],
        out_specs=VMEM_SPEC,
        out_shape=jax.ShapeDtypeStruct((1, columns, MOST * TS * TS), F32),
        scratch_shapes=[pltpu.VMEM((ngy * cells, ngx * cells), F32)],
        compiler_params=pltpu.CompilerParams(vmem_limit_bytes=16 << 20),
        name="plane",
    )(me, plane)
    return (final, owned)


def solution(mesh):
    placed = (
        P(None, "gx", "gy", "gz"),
        P(None, "gx", "gy", "gz"),
        P("gx", "gy", "gz"),
        P(),
        P(),
        P(),
        P("gx", "gy"),
        P("gx", "gy", None, None),
    )
    return jax.shard_map(
        on_device,
        mesh=mesh,
        in_specs=placed,
        out_specs=(P(None, "gx", "gy", "gz"), P(("gx", "gy"), None, None)),
        check_vma=False,
    )
```

```python
import functools
import math

import jax
import jax.numpy as jnp
from jax import lax
from jax.experimental import pallas as pl
from jax.experimental.pallas import tpu as pltpu
from jax.sharding import PartitionSpec as P

R = 8
TS = 8
MOST = 8
RELAXATION = 0.8
SHARPNESS = 8.0
THRESHOLD = 0.5
PB = 8
RC = 16
F32 = jnp.float32
BF16 = jnp.bfloat16


def lanes_of(shape):
    return lax.broadcasted_iota(jnp.int32, shape, len(shape) - 1)


def ends_matrix(depth):
    k = lax.broadcasted_iota(jnp.int32, (PB * depth, depth), 0)
    j = lax.broadcasted_iota(jnp.int32, (PB * depth, depth), 1) % (2 * PB)
    even = (k % depth == 0) & (j == 2 * (k // depth))
    odd = (k % depth == depth - 1) & (j == 2 * (k // depth) + 1)
    return jnp.where(even | odd, 1.0, 0.0).astype(BF16)


def beside_matrix(depth):
    z = lax.broadcasted_iota(jnp.int32, (depth, depth), 0)
    j = lax.broadcasted_iota(jnp.int32, (depth, depth), 1)
    return jnp.where(jnp.abs(z - j) == 1, 1.0, 0.0).astype(BF16)


def halo_matrix(depth):
    j = lax.broadcasted_iota(jnp.int32, (depth, depth), 0)
    z = lax.broadcasted_iota(jnp.int32, (depth, depth), 1)
    even = (z == 0) & (j % 2 == 0)
    odd = (z == depth - 1) & (j % 2 == 1)
    return jnp.where(even | odd, 1.0, 0.0).astype(BF16)


def split(value):
    high = value.astype(BF16)
    return high, (value - high.astype(F32)).astype(BF16)


def mm(a, b):
    return lax.dot_general(a, b, (((1,), (0,)), ((), ())), preferred_element_type=F32)


def put_ends(first, ref, ends, gs):
    rows, depth = ref.shape[2:]
    high = ref[:, pl.ds(first, PB)].astype(BF16)
    beside = [high[:, p].reshape(4 * rows, depth) for p in range(PB)]
    picked = mm(jnp.concatenate(beside, 1), ends).reshape(4, rows, depth)
    here = lanes_of((rows, depth)) // (2 * PB) == first // PB
    for c in range(4):
        gs[c] = jnp.where(here, picked[c], gs[c])


def paired(value):
    high = value.astype(BF16).astype(F32)
    return jnp.concatenate([high, value - high], 1)


PLANES = 9


def x_kernel(v_ref, s_ref, m_ref, d_ref, xlo_ref, xhi_ref, vs, ss, ms, sems):
    last = v_ref.shape[1] - 1
    rows, depth = v_ref.shape[2:]
    sides = ((0, 0, 1), (last, last - 1, 0))
    copies = []
    for i, (x, second, _) in enumerate(sides):
        copies.append(
            [
                pltpu.make_async_copy(
                    v_ref.at[:, pl.ds(min(x, second), 2)], vs.at[i], sems.at[3 * i]
                ),
                pltpu.make_async_copy(s_ref.at[:, x], ss.at[i], sems.at[3 * i + 1]),
                pltpu.make_async_copy(m_ref.at[x], ms.at[i], sems.at[3 * i + 2]),
            ]
        )
    for side in copies:
        for copy in side:
            copy.start()
    cells = d_ref.shape[0]
    none = jnp.zeros((R, depth), F32)
    for i, (out_ref, start) in enumerate(((xlo_ref, 0), (xhi_ref, cells - R))):
        strip = jnp.concatenate([paired(d_ref[start : start + R, :]), none], 0)
        out_ref[PLANES * rows :] = strip.astype(BF16)
        for copy in copies[i]:
            copy.wait()
        inner = sides[i][2]
        out_ref[: 4 * rows] = vs[i, :, 1 - inner].astype(BF16).reshape(4 * rows, depth)
        beyond = vs[i, :, inner] + ss[i].astype(F32)
        out_ref[4 * rows : 8 * rows] = beyond.astype(BF16).reshape(4 * rows, depth)
        out_ref[8 * rows : 9 * rows] = (ms[i] + 1).astype(F32).astype(BF16)


def pack_kernel(v_ref, s_ref, m_ref, ylo_ref, yhi_ref, g_ref, gs, ylo, yhi, ends):
    rows, depth = v_ref.shape[2:]
    gs[...] = jnp.zeros_like(gs)
    ends[...] = ends_matrix(depth)

    def group(i, carry):
        first = i * PB
        put_ends(first, v_ref, ends[...], gs)
        for p in range(PB):
            x = first + p
            here = pl.ds(x, 1)
            level = (m_ref[x] + 1).astype(F32)
            for out, edge, inner, low in ((ylo, 0, 1, 0), (yhi, rows - 1, rows - 2, rows - 16)):
                for c in range(4):
                    out[c, here, :] = v_ref[c, x, edge : edge + 1, :]
                    source = s_ref[c, x, low : low + 16, :].astype(F32)[edge - low : edge - low + 1]
                    out[4 + c, here, :] = v_ref[c, x, inner : inner + 1, :] + source
                out[8, here, :] = level[edge : edge + 1]
        return carry

    lax.fori_loop(0, v_ref.shape[1] // PB, group, 0)
    g_ref[...] = gs[...].astype(BF16)
    for out_ref, rows_out in ((ylo_ref, ylo), (yhi_ref, yhi)):
        out_ref[...] = rows_out[...].astype(BF16).reshape(out_ref.shape)


def corner_kernel(lo_ref, hi_ref, d_ref, xl_ref, xr_ref, _, ylo_ref, yhi_ref):
    block, depth = lo_ref.shape
    cells = d_ref.shape[0]
    rows = (xl_ref.shape[0] - 2 * R) // PLANES
    strips = [r[PLANES * rows :].astype(F32)[:R] for r in (xl_ref, xr_ref)]
    filler = jnp.zeros((cells - 2 * R, depth), F32)
    tall = jnp.concatenate([strips[0], paired(d_ref[...]), strips[1], filler], 0).astype(BF16)
    for out_ref, from_ref, edge, low in (
        (ylo_ref, lo_ref, 0, 0),
        (yhi_ref, hi_ref, rows - 1, rows - 16),
    ):
        out_ref[:block] = from_ref[...]
        corners = [
            r[c * rows + low : c * rows + low + 16].astype(F32)[edge - low : edge - low + 1]
            for r in (xl_ref, xr_ref)
            for c in range(4)
        ]
        corners.append(jnp.zeros((2 * R - 8, depth), F32))
        out_ref[block : block + 2 * R] = jnp.concatenate(corners, 0).astype(BF16)
        out_ref[block + 2 * R :] = tall


def inside_kernel(start, v_ref, s_ref, t_ref, token_ref, near, zt0, zt1):
    planes_here, rows, depth = v_ref.shape[1:]
    token_ref[...] = jnp.zeros_like(token_ref)
    near[...] = jnp.concatenate([beside_matrix(depth)] * 2, 0)
    row8 = lax.broadcasted_iota(jnp.int32, (8, depth), 0)
    count = t_ref.shape[1]

    def along_z(first, zt):
        v = v_ref[:, pl.ds(first, PB)].reshape(4 * PB * rows, depth)
        zt[...] = mm(jnp.concatenate(split(v), 1), near[...]).reshape(4, PB, rows, depth)

    def group(i, zt, zt_next):
        first = start + i * PB
        along_z(jnp.minimum(first + PB, start + count - PB), zt_next)
        for p in range(PB):
            x = first + p
            for low in range(0, rows, RC):
                span = slice(low, low + RC)
                for c in range(4):
                    v = v_ref[c, x, span]
                    before = v_ref[c, jnp.maximum(x - 1, 0), span]
                    after = v_ref[c, jnp.minimum(x + 1, planes_here - 1), span]
                    if p == 0:
                        before = jnp.where(x == 0, 0.0, before)
                    if p == PB - 1:
                        after = jnp.where(x == planes_here - 1, 0.0, after)
                    if low == 0:
                        up = pltpu.roll(v, 1, 0)
                        up = jnp.concatenate([jnp.where(row8 == 0, 0.0, up[:8]), up[8:]], 0)
                    else:
                        up = v_ref[c, x, low - 1 : low - 1 + RC]
                    if low == rows - RC:
                        down = pltpu.roll(v, RC - 1, 0)
                        down = jnp.concatenate([down[:-8], jnp.where(row8 == 7, 0.0, down[-8:])], 0)
                    else:
                        down = v_ref[c, x, low + 1 : low + 1 + RC]
                    total = before + after + s_ref[c, x, span].astype(F32) + zt[c, p, span]
                    t_ref[c, i * PB + p, span] = total + up + down

    def two(i, carry):
        group(2 * i, zt0, zt1)
        group(2 * i + 1, zt1, zt0)
        return carry

    along_z(start, zt0)
    lax.fori_loop(0, count // (2 * PB), two, 0)


def edge_kernel(g_ref, xl_ref, xr_ref, yl_ref, yr_ref, _, out_ref):
    parts, rows, depth = g_ref.shape
    beside = [r[: 4 * rows] for r in (xl_ref, xr_ref, yl_ref, yr_ref)]
    picked = mm(jnp.concatenate(beside, 1), ends_matrix(depth)[: 4 * depth])
    out_ref[:4] = g_ref[...]
    out_ref[4:] = picked.astype(BF16).reshape(4, rows, depth)


def sweep_kernel(last, nz, scale, *refs):
    sr_ref, si_ref, v_ref, s_ref, m_ref, gl_ref, gr_ref = refs[:7]
    if last:
        ext_ref, mid_ref, yl_ref, yr_ref, sh_ref, own_ref, o_ref, sens_ref = refs[7:15]
        hs, yl, yr, near, far, zt0, zt1, sens, news, sems = refs[15:]
    else:
        xl_ref, xr_ref, yl_ref, yr_ref, ylo_ref, yhi_ref = refs[7:13]
        ta_ref, tb_ref, o_ref, ext_ref, g_ref = refs[13:18]
        hs, yl, yr, near, far, zt0, zt1, gs, ends = refs[18:]
    planes_here, rows, depth = v_ref.shape[1:]
    lane = lanes_of((rows, depth))

    if nz == 2:
        here = lax.axis_index("gz").astype(F32)
        keep_l, keep_r = here, 1.0 - here
    else:
        keep_l, keep_r = 1.0, 1.0
    for c in range(gl_ref.shape[0]):
        left = pltpu.roll(gl_ref[c].astype(F32), depth - 1, 1) * keep_l
        right = pltpu.roll(gr_ref[c].astype(F32), 1, 1) * keep_r
        hs[c] = jnp.where(lane % 2 == 0, left, right)
    near[...] = jnp.concatenate([beside_matrix(depth)] * 2, 0)
    far[...] = halo_matrix(depth)
    if last:
        sens[...] = jnp.zeros_like(sens)
    else:
        gs[...] = jnp.zeros_like(gs)
        ends[...] = ends_matrix(depth)
    face = 4 * rows
    if last:
        yl[...] = ext_ref[2 * face : 3 * face].reshape(4, rows, depth)
        yr[...] = ext_ref[3 * face : 4 * face].reshape(4, rows, depth)
    else:
        yl[...] = yl_ref[:face].astype(F32).reshape(4, rows, depth)
        yr[...] = yr_ref[:face].astype(F32).reshape(4, rows, depth)

    def x_halo(side, low):
        if last:
            return ext_ref[side * face + low : side * face + low + RC]
        return (xl_ref, xr_ref)[side][low : low + RC].astype(F32)

    levels = sr_ref.shape[0]
    tile = (8, depth)
    wr, wi, share = [], [], []
    for m in range(levels):
        d = 6.0 + jnp.full(tile, sr_ref[m], F32)
        s = jnp.full(tile, si_ref[m], F32)
        mag = d * d + s * s
        wr.append(RELAXATION * d / mag)
        wi.append(-RELAXATION * s / mag)
        if last:
            share.append(jnp.full(tile, sh_ref[m], F32))

    def lookup(masks, table):
        out = jnp.broadcast_to(table[0], masks[0].shape)
        for mask, entry in zip(masks, table[1:]):
            out = jnp.where(mask, entry, out)
        return out.reshape(-1, depth)

    row8 = lax.broadcasted_iota(jnp.int32, tile, 0)

    def along_z(first, zt):
        masked = [
            jnp.where(lane // 2 == first + p, hs[c], 0.0).astype(BF16)
            for c in range(4)
            for p in range(PB)
        ]
        out = mm(jnp.concatenate(masked, 0), far[...])
        if last:
            v = v_ref[:, pl.ds(first, PB)].reshape(4 * PB * rows, depth)
            out = out + mm(jnp.concatenate(split(v), 1), near[...])
        zt[...] = out.reshape(4, PB, rows, depth)

    def plane(first, p, zt, put, inside=None):
        for low in range(0, rows, RC):
            chunk(first, p, low, zt, put, inside)

    def chunk(first, p, low, zt, put, inside):
        x = first + p
        span = slice(low, low + RC)
        mat = m_ref[x, span].reshape(RC // 8, 8, depth)
        masks = [mat == m for m in range(1, levels)]
        w_r, w_i = lookup(masks, wr), lookup(masks, wi)

        def join(c):
            t_ref, t_start = inside
            total = t_ref[c, x - t_start, span] + zt[c, p, span]
            if p == 0:
                total = total + jnp.where(x == 0, x_halo(0, c * rows + low), 0.0)
            if p == PB - 1:
                total = total + jnp.where(x == planes_here - 1, x_halo(1, c * rows + low), 0.0)
            if low == 0:
                top = total[:8] + jnp.where(row8 == 0, yl[c, pl.ds(x, 1), :], 0.0)
                total = jnp.concatenate([top, total[8:]], 0)
            if low == rows - RC:
                tail = total[-8:] + jnp.where(row8 == 7, yr[c, pl.ds(x, 1), :], 0.0)
                total = jnp.concatenate([total[:-8], tail], 0)
            return v_ref[c, x, span], total

        def drive(c):
            if not last:
                return join(c)
            v = v_ref[c, x, span]
            if p == 0:
                before = v_ref[c, jnp.maximum(x - 1, 0), span]
                before = jnp.where(x == 0, x_halo(0, c * rows + low), before)
            else:
                before = v_ref[c, x - 1, span]
            if p == PB - 1:
                after = v_ref[c, jnp.minimum(x + 1, planes_here - 1), span]
                after = jnp.where(x == planes_here - 1, x_halo(1, c * rows + low), after)
            else:
                after = v_ref[c, x + 1, span]
            total = before + after + s_ref[c, x, span].astype(F32) + zt[c, p, span]
            if low == 0:
                up = pltpu.roll(v, 1, 0)
                top = jnp.where(row8 == 0, yl[c, pl.ds(x, 1), :], up[:8])
                up = jnp.concatenate([top, up[8:]], 0)
            else:
                up = v_ref[c, x, low - 1 : low - 1 + RC]
            if low == rows - RC:
                down = pltpu.roll(v, RC - 1, 0)
                tail = jnp.where(row8 == 7, yr[c, pl.ds(x, 1), :], down[-8:])
                down = jnp.concatenate([down[:-8], tail], 0)
            else:
                down = v_ref[c, x, low + 1 : low + 1 + RC]
            return v, total + up + down

        new = []
        for re in (0, 2):
            v_r, t_r = drive(re)
            v_i, t_i = drive(re + 1)
            keep = 1.0 - RELAXATION
            n_r = keep * v_r + (w_r * t_r - w_i * t_i)
            n_i = keep * v_i + (w_r * t_i + w_i * t_r)
            put(re, span, n_r)
            put(re + 1, span, n_i)
            new += [n_r, n_i]
        if last:
            value = lookup(masks, share) * (new[0] * new[2] - new[1] * new[3])
            column = jnp.sum(value, axis=1, keepdims=True)
            sens[span] = jnp.where(lane[:RC] == x, column, sens[span])

    groups = planes_here // PB

    def store(i):
        part = pl.ds(i * PB, PB)
        return pltpu.make_async_copy(news.at[:, part], o_ref.at[:, part], sems.at[i])

    result = news if last else o_ref

    def group(i, zt, zt_next, inside=None):
        first = i * PB
        along_z(jnp.minimum(first + PB, planes_here - PB), zt_next)
        for p in range(PB):

            def put(c, span, new, p=p):
                result[c, first + p, span] = new

            plane(first, p, zt, put, inside)
        if last:
            store(i).start()
        else:
            put_ends(first, o_ref, ends[...], gs)

    def pairs(begin, end, inside=None):
        def two(i, carry):
            group(2 * i, zt0, zt1, inside)
            group(2 * i + 1, zt1, zt0, inside)
            return carry

        lax.fori_loop(begin, end, two, 0)

    along_z(0, zt0)
    if last:
        pairs(0, groups // 2)
    else:
        cut = ta_ref.shape[1]
        pairs(0, cut // (2 * PB), (ta_ref, 0))
        pairs(cut // (2 * PB), groups // 2, (tb_ref, cut))

    if not last:
        g_ref[...] = gs[...].astype(BF16)
        sides = (xl_ref, xr_ref, yl_ref, yr_ref)
        centres = jnp.concatenate([r[:face] for r in sides], 0)
        masked = [
            jnp.where(lane // 2 == e, hs[4 + c], 0.0).astype(BF16) for e in range(4) for c in range(4)
        ]
        along = mm(centres, near[:depth]) + mm(jnp.concatenate(masked, 0), far[...])
        for e in range(4):
            zt0[:, e] = along[e * face : (e + 1) * face].reshape(4, rows, depth)
        block = PLANES * planes_here
        corner_l = yl_ref[block : block + 2 * R].astype(F32)
        corner_r = yr_ref[block : block + 2 * R].astype(F32)
        zero = jnp.zeros(tile, F32)
        for e, ref in enumerate(sides):
            level = ref[2 * face : 2 * face + rows].astype(F32).reshape(rows // 8, 8, depth)
            masks = [level == float(m + 1) for m in range(levels)]
            w_r, w_i = lookup(masks, [zero] + wr), lookup(masks, [zero] + wi)

            def near_plane(c, e=e, ref=ref):
                part = slice(c * rows, (c + 1) * rows)
                v = ref[part].astype(F32)
                beyond = ref[face + c * rows : face + (c + 1) * rows].astype(F32)
                if e < 2:
                    inside = v_ref[c, 0 if e == 0 else planes_here - 1]
                    top, low = corner_l[4 * e + c : 4 * e + c + 1], corner_r[4 * e + c : 4 * e + c + 1]
                else:
                    inside = (ylo_ref, yhi_ref)[e - 2][part].astype(F32)
                    corner = corner_l if e == 2 else corner_r
                    top, low = corner[c : c + 1], corner[4 + c : 5 + c]
                total = beyond + inside + zt0[c, e]
                up = pltpu.roll(v, 1, 0)
                down = pltpu.roll(v, rows - 1, 0)
                up = jnp.concatenate([jnp.where(row8 == 0, top, up[:8]), up[8:]], 0)
                down = jnp.concatenate([down[:-8], jnp.where(row8 == 7, low, down[-8:])], 0)
                return v, total + up + down

            for re in (0, 2):
                v_r, t_r = near_plane(re)
                v_i, t_i = near_plane(re + 1)
                keep = 1.0 - RELAXATION
                at = e * face + re * rows
                ext_ref[at : at + rows] = keep * v_r + (w_r * t_r - w_i * t_i)
                ext_ref[at + rows : at + 2 * rows] = keep * v_i + (w_r * t_i + w_i * t_r)
    else:
        cells = rows
        row = lax.broadcasted_iota(jnp.int32, (cells, 2 * cells), 0)
        col = lanes_of((cells, 2 * cells))
        half_sum = jnp.zeros((cells, 2 * cells), F32)
        for shift, ref in ((-cells, yl_ref), (0, mid_ref), (cells, yr_ref)):
            weight = jnp.maximum(R + 1 - jnp.abs(col % cells + shift - row), 0)
            tall = ref[PLANES * planes_here + 2 * R :]
            half_sum = half_sum + lax.dot_general(
                weight.astype(F32).astype(BF16),
                tall,
                (((1,), (1,)), ((), ())),
                preferred_element_type=F32,
            )
        row = lax.broadcasted_iota(jnp.int32, (2 * cells, depth), 0)
        col = lanes_of((2 * cells, depth))
        weight = jnp.maximum(R + 1 - jnp.abs(row - R - col), 0).astype(F32).astype(BF16)
        filtered = twice(half_sum, weight) / float((R + 1) ** 4)
        tangent = jnp.tanh(SHARPNESS * (filtered - THRESHOLD))
        total = math.tanh(SHARPNESS * THRESHOLD) + math.tanh(SHARPNESS * (1.0 - THRESHOLD))
        slope = SHARPNESS * (1.0 - tangent * tangent) / total
        weighted = slope * sens[...] * scale
        half = rows // 2
        both = pltpu.roll(weighted[half:], depth // 2, 1)
        sens_ref[:half] = jnp.where(lane[:half] < depth // 2, weighted[:half], both)
        mine = jnp.where(lax.axis_index("gz") == 0, own_ref[...].astype(F32), 0.0)
        sens_ref[half:] = jnp.concatenate([mine, jnp.zeros((8, depth - rows), F32)], 1)
        for i in range(groups):
            store(i).wait()


def twice(value, right):
    high, low = split(value)
    return mm(high, right) + mm(low, right)


def left_twice(left, value):
    high, low = split(value)
    return mm(left, high) + mm(left, low)


SMEM_SPEC = pl.BlockSpec(memory_space=pltpu.SMEM)
VMEM_SPEC = pl.BlockSpec(memory_space=pltpu.VMEM)


def near(value):
    return pltpu.with_memory_space_constraint(value, pltpu.VMEM)


def far_away(value):
    return pltpu.with_memory_space_constraint(value, pltpu.HBM)


def local(kernel, name, operands, specs, shapes, out_specs, scratch, limit, cost):
    return pl.pallas_call(
        kernel,
        in_specs=specs,
        out_specs=out_specs,
        out_shape=shapes,
        scratch_shapes=scratch,
        compiler_params=pltpu.CompilerParams(vmem_limit_bytes=limit << 20),
        cost_estimate=pl.CostEstimate(flops=cost, bytes_accessed=cost, transcendentals=0),
        name=name,
    )(*operands)


def shift(value, axis, up):
    count = lax.axis_size(axis)
    pairs = [(i, i + 1) for i in range(count - 1)]
    return lax.ppermute(value, axis, pairs if up else [(j, i) for i, j in pairs])


def shift_z(g):
    if lax.axis_size("gz") == 2:
        other = lax.ppermute(g, "gz", [(0, 1), (1, 0)])
        return other, other
    return shift(g, "gz", True), shift(g, "gz", False)


def sweeps(tables, share, fields, sources, material, density, owners):
    _, nx, ny, nz = fields.shape
    nz_parts = lax.axis_size("gz")
    hbm = pl.BlockSpec(memory_space=pltpu.HBM)
    held = [near(a) for a in (fields, sources, material)]

    x_shape = jax.ShapeDtypeStruct((PLANES * ny + 2 * R, nz), BF16)
    y_shape = jax.ShapeDtypeStruct((PLANES * nx + 2 * R + 2 * nx, nz), BF16)
    g_shape = jax.ShapeDtypeStruct((4, ny, nz), BF16)
    wide_g = jax.ShapeDtypeStruct((8, ny, nz), BF16)
    xlo, xhi = local(
        x_kernel,
        "x_faces",
        [far_away(a) for a in (fields, sources, material)] + [density],
        [hbm] * 3 + [VMEM_SPEC],
        [x_shape] * 2,
        [VMEM_SPEC] * 2,
        [
            pltpu.VMEM((2, 4, 2, ny, nz), F32),
            pltpu.VMEM((2, 4, ny, nz), BF16),
            pltpu.VMEM((2, ny, nz), jnp.int32),
            pltpu.SemaphoreType.DMA((6,)),
        ],
        8,
        ny * nz * 100,
    )
    xl, xr = shift(xhi, "gx", True), shift(xlo, "gx", False)
    part_shape = jax.ShapeDtypeStruct((PLANES * nx, nz), BF16)
    lo, hi, g = local(
        pack_kernel,
        "pack_faces",
        held,
        [VMEM_SPEC] * 3,
        [part_shape, part_shape, g_shape],
        [VMEM_SPEC] * 3,
        [
            pltpu.VMEM((4, ny, nz), F32),
            pltpu.VMEM((PLANES, nx, nz), F32),
            pltpu.VMEM((PLANES, nx, nz), F32),
            pltpu.VMEM((PB * nz, nz), BF16),
        ],
        12,
        fields.size * 4,
    )
    cut = nx // 2
    inside = [
        local(
            functools.partial(inside_kernel, start),
            "inside",
            held[:2],
            [VMEM_SPEC] * 2,
            [pltpu.VMEM((4, cut, ny, nz), F32), jax.ShapeDtypeStruct((8, nz), F32)],
            [VMEM_SPEC] * 2,
            [
                pltpu.VMEM((2 * nz, nz), BF16),
                pltpu.VMEM((4, PB, ny, nz), F32),
                pltpu.VMEM((4, PB, ny, nz), F32),
            ],
            8,
            fields.size * 5,
        )
        for start in (0, cut)
    ]
    ylo, yhi = local(
        corner_kernel,
        "corners",
        [lo, hi, density, xl, xr, inside[0][1]],
        [VMEM_SPEC] * 6,
        [y_shape] * 2,
        [VMEM_SPEC] * 2,
        [],
        8,
        ny * nz * 40,
    )
    yl, yr = shift(yhi, "gy", True), shift(ylo, "gy", False)
    g = local(
        edge_kernel,
        "edge_faces",
        [g, xl, xr, yl, yr, inside[1][1]],
        [VMEM_SPEC] * 6,
        wide_g,
        VMEM_SPEC,
        [],
        8,
        ny * nz * 40,
    )
    gl, gr = shift_z(g)

    def scratch(parts):
        return [
            pltpu.VMEM((parts, ny, nz), F32),
            pltpu.VMEM((4, nx, nz), F32),
            pltpu.VMEM((4, nx, nz), F32),
            pltpu.VMEM((2 * nz, nz), BF16),
            pltpu.VMEM((nz, nz), BF16),
            pltpu.VMEM((4, PB, ny, nz), F32),
            pltpu.VMEM((4, PB, ny, nz), F32),
        ]

    scale = 1.0 / math.sqrt(nz * nz_parts)
    middle, ext, g = local(
        functools.partial(sweep_kernel, False, nz_parts, scale),
        "sweep_first",
        [*tables, held[0], density, held[2], gl, gr, xl, xr, yl, yr, ylo, yhi, *(near(t) for t, _ in inside)],
        [SMEM_SPEC] * 2 + [VMEM_SPEC] * 13,
        [pltpu.VMEM(fields.shape, F32), jax.ShapeDtypeStruct((16 * ny, nz), F32), g_shape],
        [VMEM_SPEC] * 3,
        scratch(8) + [pltpu.VMEM((4, ny, nz), F32), pltpu.VMEM((PB * nz, nz), BF16)],
        20,
        fields.size * 20,
    )
    gl, gr = shift_z(g)
    return local(
        functools.partial(sweep_kernel, True, nz_parts, scale),
        "sweep_last",
        [*tables, near(middle), *held[1:], gl, gr, ext, ylo, yl, yr, share, owners],
        [SMEM_SPEC] * 2 + [VMEM_SPEC] * 9 + [SMEM_SPEC, VMEM_SPEC],
        [
            jax.ShapeDtypeStruct(fields.shape, F32),
            jax.ShapeDtypeStruct((ny // 2 + 8, nz), F32),
        ],
        [hbm, VMEM_SPEC],
        scratch(4)
        + [
            pltpu.VMEM((ny, nz), F32),
            pltpu.VMEM(fields.shape, F32),
            pltpu.SemaphoreType.DMA((nx // PB,)),
        ],
        20,
        fields.size * 20,
    )


def plane_kernel(ngx, ngy, me_ref, got_ref, out_ref, w_ref):
    cells = 64
    nx, ny = ngx * cells, ngy * cells
    columns = ngx * ngy
    half = cells // 2
    for cx in range(ngx):
        for cy in range(ngy):
            c = cx * ngy + cy
            for part in range(2):
                lanes = pl.ds(part * cells, cells)
                w_ref[pl.ds(cy * cells + part * half, half), pl.ds(cx * cells, cells)] = got_ref[
                    c, pl.ds(0, half), lanes
                ]

    def band(n):
        i = lax.broadcasted_iota(jnp.int32, (n, n), 0)
        j = lax.broadcasted_iota(jnp.int32, (n, n), 1)
        return jnp.maximum(R + 1 - jnp.abs(i - j), 0).astype(F32).astype(BF16)

    unit = float((R + 1) ** 4)
    weighted = twice(w_ref[...], band(nx))

    tiles = cells
    owner = jnp.concatenate([got_ref[c, pl.ds(half, 1), pl.ds(0, tiles)] for c in range(columns)], 0)
    mine = owner == me_ref[0].astype(F32)
    flag = jnp.where(mine, 1.0, 0.0)
    a = lax.broadcasted_iota(jnp.int32, (tiles, tiles), 0)
    b = lax.broadcasted_iota(jnp.int32, (tiles, tiles), 1)
    rank = mm(flag.astype(BF16), jnp.where(a < b, 1.0, 0.0).astype(BF16))
    number = lanes_of((columns, tiles))
    column = lax.broadcasted_iota(jnp.int32, (columns, 1), 0)
    rows, blocks = [], []
    for k in range(MOST):
        chosen = mine & (rank == float(k))
        tile = jnp.sum(jnp.where(chosen, number, 0), axis=1, keepdims=True)
        there = jnp.sum(jnp.where(chosen, 1, 0), axis=1, keepdims=True)
        rows.append((column % ngy) * cells + (tile % (cells // TS)) * TS)
        block = (column // ngy) * (cells // TS) + tile // (cells // TS)
        blocks.append(jnp.where(there > 0, block, -1))
    row = jnp.concatenate(rows, 0)
    block = jnp.concatenate(blocks, 0)
    slots = MOST * columns
    across = lax.broadcasted_iota(jnp.int32, (slots, ny), 1)
    lefts = [
        jnp.maximum(R + 1 - jnp.abs(row + j - across), 0).astype(F32).astype(BF16)
        for j in range(TS)
    ]
    lines = left_twice(jnp.concatenate(lefts, 0), weighted)
    keep = lanes_of((slots, nx)) // TS == block
    from_x = lax.broadcasted_iota(jnp.int32, (nx, TS * TS), 0) % TS
    to_q = lanes_of((nx, TS * TS))
    out = jnp.zeros((slots, TS * TS), F32)
    for j in range(TS):
        fold = jnp.where(to_q == from_x * TS + j, 1.0, 0.0).astype(BF16)
        out = out + twice(jnp.where(keep, lines[j * slots : (j + 1) * slots], 0.0), fold)
    out = out / unit
    for k in range(MOST):
        out_ref[0, :, pl.ds(k * TS * TS, TS * TS)] = out[k * columns : (k + 1) * columns]


def on_device(fields, sources, material, shift_real, shift_imag, design_share, density, owner_map):
    ngx, ngy = lax.axis_size("gx"), lax.axis_size("gy")
    columns = ngx * ngy
    cells = density.shape[0]
    tables = (shift_real, shift_imag)
    owners = jnp.broadcast_to(owner_map.reshape(1, -1), (8, cells))
    final, partial = sweeps(tables, design_share, fields, sources, material, density, owners)
    partial = jnp.sum(lax.all_gather(partial, "gz"), 0)
    copies = jnp.broadcast_to(partial[None], (columns, *partial.shape))
    plane = lax.all_to_all(copies, ("gx", "gy"), split_axis=0, concat_axis=0)
    me = (lax.axis_index("gx") * ngy + lax.axis_index("gy")).reshape(1)
    owned = pl.pallas_call(
        functools.partial(plane_kernel, ngx, ngy),
        in_specs=[SMEM_SPEC, VMEM_SPEC],
        out_specs=VMEM_SPEC,
        out_shape=jax.ShapeDtypeStruct((1, columns, MOST * TS * TS), F32),
        scratch_shapes=[pltpu.VMEM((ngy * cells, ngx * cells), F32)],
        compiler_params=pltpu.CompilerParams(vmem_limit_bytes=16 << 20),
        name="plane",
    )(me, plane)
    return (final, owned)


def solution(mesh):
    placed = (
        P(None, "gx", "gy", "gz"),
        P(None, "gx", "gy", "gz"),
        P("gx", "gy", "gz"),
        P(),
        P(),
        P(),
        P("gx", "gy"),
        P("gx", "gy", None, None),
    )
    return jax.shard_map(
        on_device,
        mesh=mesh,
        in_specs=placed,
        out_specs=(P(None, "gx", "gy", "gz"), P(("gx", "gy"), None, None)),
        check_vma=False,
    )
```

```python
import functools
import math

import jax
import jax.numpy as jnp
from jax import lax
from jax.experimental import pallas as pl
from jax.experimental.pallas import tpu as pltpu
from jax.sharding import PartitionSpec as P

R = 8
TS = 8
MOST = 8
RELAXATION = 0.8
SHARPNESS = 8.0
THRESHOLD = 0.5
PB = 8
RC = 16
F32 = jnp.float32
BF16 = jnp.bfloat16


def lanes_of(shape):
    return lax.broadcasted_iota(jnp.int32, shape, len(shape) - 1)


def ends_matrix(depth):
    k = lax.broadcasted_iota(jnp.int32, (PB * depth, depth), 0)
    j = lax.broadcasted_iota(jnp.int32, (PB * depth, depth), 1) % (2 * PB)
    even = (k % depth == 0) & (j == 2 * (k // depth))
    odd = (k % depth == depth - 1) & (j == 2 * (k // depth) + 1)
    return jnp.where(even | odd, 1.0, 0.0).astype(BF16)


def beside_matrix(depth):
    z = lax.broadcasted_iota(jnp.int32, (depth, depth), 0)
    j = lax.broadcasted_iota(jnp.int32, (depth, depth), 1)
    return jnp.where(jnp.abs(z - j) == 1, 1.0, 0.0).astype(BF16)


def halo_matrix(depth):
    j = lax.broadcasted_iota(jnp.int32, (depth, depth), 0)
    z = lax.broadcasted_iota(jnp.int32, (depth, depth), 1)
    even = (z == 0) & (j % 2 == 0)
    odd = (z == depth - 1) & (j % 2 == 1)
    return jnp.where(even | odd, 1.0, 0.0).astype(BF16)


def split(value):
    high = value.astype(BF16)
    return high, (value - high.astype(F32)).astype(BF16)


def mm(a, b):
    return lax.dot_general(a, b, (((1,), (0,)), ((), ())), preferred_element_type=F32)


def put_ends(first, ref, ends, gs):
    rows, depth = ref.shape[2:]
    high = ref[:, pl.ds(first, PB)].astype(BF16)
    beside = [high[:, p].reshape(4 * rows, depth) for p in range(PB)]
    picked = mm(jnp.concatenate(beside, 1), ends).reshape(4, rows, depth)
    here = lanes_of((rows, depth)) // (2 * PB) == first // PB
    for c in range(4):
        gs[c] = jnp.where(here, picked[c], gs[c])


def paired(value):
    high = value.astype(BF16).astype(F32)
    return jnp.concatenate([high, value - high], 1)


PLANES = 9


def x_kernel(v_ref, s_ref, m_ref, d_ref, xlo_ref, xhi_ref, vs, ss, ms, sems):
    last = v_ref.shape[1] - 1
    rows, depth = v_ref.shape[2:]
    sides = ((0, 0, 1), (last, last - 1, 0))
    copies = []
    for i, (x, second, _) in enumerate(sides):
        copies.append(
            [
                pltpu.make_async_copy(
                    v_ref.at[:, pl.ds(min(x, second), 2)], vs.at[i], sems.at[3 * i]
                ),
                pltpu.make_async_copy(s_ref.at[:, x], ss.at[i], sems.at[3 * i + 1]),
                pltpu.make_async_copy(m_ref.at[x], ms.at[i], sems.at[3 * i + 2]),
            ]
        )
    for side in copies:
        for copy in side:
            copy.start()
    cells = d_ref.shape[0]
    none = jnp.zeros((R, depth), F32)
    for i, (out_ref, start) in enumerate(((xlo_ref, 0), (xhi_ref, cells - R))):
        strip = jnp.concatenate([paired(d_ref[start : start + R, :]), none], 0)
        out_ref[PLANES * rows :] = strip.astype(BF16)
        for copy in copies[i]:
            copy.wait()
        inner = sides[i][2]
        out_ref[: 4 * rows] = vs[i, :, 1 - inner].astype(BF16).reshape(4 * rows, depth)
        beyond = vs[i, :, inner] + ss[i].astype(F32)
        out_ref[4 * rows : 8 * rows] = beyond.astype(BF16).reshape(4 * rows, depth)
        out_ref[8 * rows : 9 * rows] = (ms[i] + 1).astype(F32).astype(BF16)


def pack_kernel(v_ref, s_ref, m_ref, ylo_ref, yhi_ref, g_ref, gs, ylo, yhi, ends):
    rows, depth = v_ref.shape[2:]
    gs[...] = jnp.zeros_like(gs)
    ends[...] = ends_matrix(depth)

    def group(i, carry):
        first = i * PB
        put_ends(first, v_ref, ends[...], gs)
        for p in range(PB):
            x = first + p
            here = pl.ds(x, 1)
            level = (m_ref[x] + 1).astype(F32)
            for out, edge, inner, low in ((ylo, 0, 1, 0), (yhi, rows - 1, rows - 2, rows - 16)):
                for c in range(4):
                    out[c, here, :] = v_ref[c, x, edge : edge + 1, :]
                    source = s_ref[c, x, low : low + 16, :].astype(F32)[edge - low : edge - low + 1]
                    out[4 + c, here, :] = v_ref[c, x, inner : inner + 1, :] + source
                out[8, here, :] = level[edge : edge + 1]
        return carry

    lax.fori_loop(0, v_ref.shape[1] // PB, group, 0)
    g_ref[...] = gs[...].astype(BF16)
    for out_ref, rows_out in ((ylo_ref, ylo), (yhi_ref, yhi)):
        out_ref[...] = rows_out[...].astype(BF16).reshape(out_ref.shape)


def corner_kernel(lo_ref, hi_ref, d_ref, xl_ref, xr_ref, _, ylo_ref, yhi_ref):
    block, depth = lo_ref.shape
    cells = d_ref.shape[0]
    rows = (xl_ref.shape[0] - 2 * R) // PLANES
    strips = [r[PLANES * rows :].astype(F32)[:R] for r in (xl_ref, xr_ref)]
    filler = jnp.zeros((cells - 2 * R, depth), F32)
    tall = jnp.concatenate([strips[0], paired(d_ref[...]), strips[1], filler], 0).astype(BF16)
    for out_ref, from_ref, edge, low in (
        (ylo_ref, lo_ref, 0, 0),
        (yhi_ref, hi_ref, rows - 1, rows - 16),
    ):
        out_ref[:block] = from_ref[...]
        corners = [
            r[c * rows + low : c * rows + low + 16].astype(F32)[edge - low : edge - low + 1]
            for r in (xl_ref, xr_ref)
            for c in range(4)
        ]
        corners.append(jnp.zeros((2 * R - 8, depth), F32))
        out_ref[block : block + 2 * R] = jnp.concatenate(corners, 0).astype(BF16)
        out_ref[block + 2 * R :] = tall


def inside_kernel(start, v_ref, s_ref, t_ref, token_ref, near, zt0, zt1):
    planes_here, rows, depth = v_ref.shape[1:]
    token_ref[...] = jnp.zeros_like(token_ref)
    near[...] = jnp.concatenate([beside_matrix(depth)] * 2, 0)
    row8 = lax.broadcasted_iota(jnp.int32, (8, depth), 0)
    count = t_ref.shape[1]

    def along_z(first, zt):
        v = v_ref[:, pl.ds(first, PB)].reshape(4 * PB * rows, depth)
        zt[...] = mm(jnp.concatenate(split(v), 1), near[...]).reshape(4, PB, rows, depth)

    def group(i, zt, zt_next):
        first = start + i * PB
        along_z(jnp.minimum(first + PB, start + count - PB), zt_next)
        for p in range(PB):
            x = first + p
            for low in range(0, rows, RC):
                span = slice(low, low + RC)
                for c in range(4):
                    v = v_ref[c, x, span]
                    before = v_ref[c, jnp.maximum(x - 1, 0), span]
                    after = v_ref[c, jnp.minimum(x + 1, planes_here - 1), span]
                    if p == 0:
                        before = jnp.where(x == 0, 0.0, before)
                    if p == PB - 1:
                        after = jnp.where(x == planes_here - 1, 0.0, after)
                    if low == 0:
                        up = pltpu.roll(v, 1, 0)
                        up = jnp.concatenate([jnp.where(row8 == 0, 0.0, up[:8]), up[8:]], 0)
                    else:
                        up = v_ref[c, x, low - 1 : low - 1 + RC]
                    if low == rows - RC:
                        down = pltpu.roll(v, RC - 1, 0)
                        down = jnp.concatenate([down[:-8], jnp.where(row8 == 7, 0.0, down[-8:])], 0)
                    else:
                        down = v_ref[c, x, low + 1 : low + 1 + RC]
                    total = before + after + s_ref[c, x, span].astype(F32) + zt[c, p, span]
                    t_ref[c, i * PB + p, span] = total + up + down

    def two(i, carry):
        group(2 * i, zt0, zt1)
        group(2 * i + 1, zt1, zt0)
        return carry

    along_z(start, zt0)
    lax.fori_loop(0, count // (2 * PB), two, 0)


def edge_kernel(g_ref, xl_ref, xr_ref, yl_ref, yr_ref, _, out_ref):
    parts, rows, depth = g_ref.shape
    beside = [r[: 4 * rows] for r in (xl_ref, xr_ref, yl_ref, yr_ref)]
    picked = mm(jnp.concatenate(beside, 1), ends_matrix(depth)[: 4 * depth])
    out_ref[:4] = g_ref[...]
    out_ref[4:] = picked.astype(BF16).reshape(4, rows, depth)


def sweep_kernel(last, nz, scale, *refs):
    sr_ref, si_ref, v_ref, s_ref, m_ref, gl_ref, gr_ref = refs[:7]
    if last:
        ext_ref, mid_ref, yl_ref, yr_ref, sh_ref, own_ref, o_ref, sens_ref = refs[7:15]
        hs, yl, yr, near, far, zt0, zt1, sens, news, sems = refs[15:]
    else:
        xl_ref, xr_ref, yl_ref, yr_ref, ylo_ref, yhi_ref = refs[7:13]
        ta_ref, tb_ref, o_ref, ext_ref, g_ref = refs[13:18]
        hs, yl, yr, near, far, zt0, zt1, gs, ends = refs[18:]
    planes_here, rows, depth = v_ref.shape[1:]
    lane = lanes_of((rows, depth))

    if nz == 2:
        here = lax.axis_index("gz").astype(F32)
        keep_l, keep_r = here, 1.0 - here
    else:
        keep_l, keep_r = 1.0, 1.0
    for c in range(gl_ref.shape[0]):
        left = pltpu.roll(gl_ref[c].astype(F32), depth - 1, 1) * keep_l
        right = pltpu.roll(gr_ref[c].astype(F32), 1, 1) * keep_r
        hs[c] = jnp.where(lane % 2 == 0, left, right)
    near[...] = jnp.concatenate([beside_matrix(depth)] * 2, 0)
    far[...] = halo_matrix(depth)
    if last:
        sens[...] = jnp.zeros_like(sens)
    else:
        gs[...] = jnp.zeros_like(gs)
        ends[...] = ends_matrix(depth)
    face = 4 * rows
    if last:
        yl[...] = ext_ref[2 * face : 3 * face].reshape(4, rows, depth)
        yr[...] = ext_ref[3 * face : 4 * face].reshape(4, rows, depth)
    else:
        yl[...] = yl_ref[:face].astype(F32).reshape(4, rows, depth)
        yr[...] = yr_ref[:face].astype(F32).reshape(4, rows, depth)

    def x_halo(side, low):
        if last:
            return ext_ref[side * face + low : side * face + low + RC]
        return (xl_ref, xr_ref)[side][low : low + RC].astype(F32)

    levels = sr_ref.shape[0]
    tile = (8, depth)
    wr, wi, share = [], [], []
    for m in range(levels):
        d = 6.0 + jnp.full(tile, sr_ref[m], F32)
        s = jnp.full(tile, si_ref[m], F32)
        mag = d * d + s * s
        wr.append(RELAXATION * d / mag)
        wi.append(-RELAXATION * s / mag)
        if last:
            share.append(jnp.full(tile, sh_ref[m], F32))

    def lookup(masks, table):
        out = jnp.broadcast_to(table[0], masks[0].shape)
        for mask, entry in zip(masks, table[1:]):
            out = jnp.where(mask, entry, out)
        return out.reshape(-1, depth)

    row8 = lax.broadcasted_iota(jnp.int32, tile, 0)

    def along_z(first, zt):
        masked = [
            jnp.where(lane // 2 == first + p, hs[c], 0.0).astype(BF16)
            for c in range(4)
            for p in range(PB)
        ]
        out = mm(jnp.concatenate(masked, 0), far[...])
        if last:
            v = v_ref[:, pl.ds(first, PB)].reshape(4 * PB * rows, depth)
            out = out + mm(jnp.concatenate(split(v), 1), near[...])
        zt[...] = out.reshape(4, PB, rows, depth)

    def plane(first, p, zt, put, inside=None):
        for low in range(0, rows, RC):
            chunk(first, p, low, zt, put, inside)

    def chunk(first, p, low, zt, put, inside):
        x = first + p
        span = slice(low, low + RC)
        mat = m_ref[x, span].reshape(RC // 8, 8, depth)
        masks = [mat == m for m in range(1, levels)]
        w_r, w_i = lookup(masks, wr), lookup(masks, wi)

        def join(c):
            t_ref, t_start = inside
            total = t_ref[c, x - t_start, span] + zt[c, p, span]
            if p == 0:
                total = total + jnp.where(x == 0, x_halo(0, c * rows + low), 0.0)
            if p == PB - 1:
                total = total + jnp.where(x == planes_here - 1, x_halo(1, c * rows + low), 0.0)
            if low == 0:
                top = total[:8] + jnp.where(row8 == 0, yl[c, pl.ds(x, 1), :], 0.0)
                total = jnp.concatenate([top, total[8:]], 0)
            if low == rows - RC:
                tail = total[-8:] + jnp.where(row8 == 7, yr[c, pl.ds(x, 1), :], 0.0)
                total = jnp.concatenate([total[:-8], tail], 0)
            return v_ref[c, x, span], total

        def drive(c):
            if not last:
                return join(c)
            v = v_ref[c, x, span]
            if p == 0:
                before = v_ref[c, jnp.maximum(x - 1, 0), span]
                before = jnp.where(x == 0, x_halo(0, c * rows + low), before)
            else:
                before = v_ref[c, x - 1, span]
            if p == PB - 1:
                after = v_ref[c, jnp.minimum(x + 1, planes_here - 1), span]
                after = jnp.where(x == planes_here - 1, x_halo(1, c * rows + low), after)
            else:
                after = v_ref[c, x + 1, span]
            total = before + after + s_ref[c, x, span].astype(F32) + zt[c, p, span]
            if low == 0:
                up = pltpu.roll(v, 1, 0)
                top = jnp.where(row8 == 0, yl[c, pl.ds(x, 1), :], up[:8])
                up = jnp.concatenate([top, up[8:]], 0)
            else:
                up = v_ref[c, x, low - 1 : low - 1 + RC]
            if low == rows - RC:
                down = pltpu.roll(v, RC - 1, 0)
                tail = jnp.where(row8 == 7, yr[c, pl.ds(x, 1), :], down[-8:])
                down = jnp.concatenate([down[:-8], tail], 0)
            else:
                down = v_ref[c, x, low + 1 : low + 1 + RC]
            return v, total + up + down

        new = []
        for re in (0, 2):
            v_r, t_r = drive(re)
            v_i, t_i = drive(re + 1)
            keep = 1.0 - RELAXATION
            n_r = keep * v_r + (w_r * t_r - w_i * t_i)
            n_i = keep * v_i + (w_r * t_i + w_i * t_r)
            put(re, span, n_r)
            put(re + 1, span, n_i)
            new += [n_r, n_i]
        if last:
            value = lookup(masks, share) * (new[0] * new[2] - new[1] * new[3])
            column = jnp.sum(value, axis=1, keepdims=True)
            sens[span] = jnp.where(lane[:RC] == x, column, sens[span])

    groups = planes_here // PB

    def store(i):
        part = pl.ds(i * PB, PB)
        return pltpu.make_async_copy(news.at[:, part], o_ref.at[:, part], sems.at[i])

    result = news if last else o_ref

    def group(i, zt, zt_next, inside=None):
        first = i * PB
        along_z(jnp.minimum(first + PB, planes_here - PB), zt_next)
        for p in range(PB):

            def put(c, span, new, p=p):
                result[c, first + p, span] = new

            plane(first, p, zt, put, inside)
        if last:
            store(i).start()
        else:
            put_ends(first, o_ref, ends[...], gs)

    def pairs(begin, end, inside=None):
        def two(i, carry):
            group(2 * i, zt0, zt1, inside)
            group(2 * i + 1, zt1, zt0, inside)
            return carry

        lax.fori_loop(begin, end, two, 0)

    along_z(0, zt0)
    if last:
        pairs(0, groups // 2)
    else:
        cut = ta_ref.shape[1]
        pairs(0, cut // (2 * PB), (ta_ref, 0))
        pairs(cut // (2 * PB), groups // 2, (tb_ref, cut))

    if not last:
        g_ref[...] = gs[...].astype(BF16)
        sides = (xl_ref, xr_ref, yl_ref, yr_ref)
        centres = jnp.concatenate([r[:face] for r in sides], 0)
        masked = [
            jnp.where(lane // 2 == e, hs[4 + c], 0.0).astype(BF16) for e in range(4) for c in range(4)
        ]
        along = mm(centres, near[:depth]) + mm(jnp.concatenate(masked, 0), far[...])
        for e in range(4):
            zt0[:, e] = along[e * face : (e + 1) * face].reshape(4, rows, depth)
        block = PLANES * planes_here
        corner_l = yl_ref[block : block + 2 * R].astype(F32)
        corner_r = yr_ref[block : block + 2 * R].astype(F32)
        zero = jnp.zeros(tile, F32)
        for e, ref in enumerate(sides):
            level = ref[2 * face : 2 * face + rows].astype(F32).reshape(rows // 8, 8, depth)
            masks = [level == float(m + 1) for m in range(levels)]
            w_r, w_i = lookup(masks, [zero] + wr), lookup(masks, [zero] + wi)

            def near_plane(c, e=e, ref=ref):
                part = slice(c * rows, (c + 1) * rows)
                v = ref[part].astype(F32)
                beyond = ref[face + c * rows : face + (c + 1) * rows].astype(F32)
                if e < 2:
                    inside = v_ref[c, 0 if e == 0 else planes_here - 1]
                    top, low = corner_l[4 * e + c : 4 * e + c + 1], corner_r[4 * e + c : 4 * e + c + 1]
                else:
                    inside = (ylo_ref, yhi_ref)[e - 2][part].astype(F32)
                    corner = corner_l if e == 2 else corner_r
                    top, low = corner[c : c + 1], corner[4 + c : 5 + c]
                total = beyond + inside + zt0[c, e]
                up = pltpu.roll(v, 1, 0)
                down = pltpu.roll(v, rows - 1, 0)
                up = jnp.concatenate([jnp.where(row8 == 0, top, up[:8]), up[8:]], 0)
                down = jnp.concatenate([down[:-8], jnp.where(row8 == 7, low, down[-8:])], 0)
                return v, total + up + down

            for re in (0, 2):
                v_r, t_r = near_plane(re)
                v_i, t_i = near_plane(re + 1)
                keep = 1.0 - RELAXATION
                at = e * face + re * rows
                ext_ref[at : at + rows] = keep * v_r + (w_r * t_r - w_i * t_i)
                ext_ref[at + rows : at + 2 * rows] = keep * v_i + (w_r * t_i + w_i * t_r)
    else:
        cells = rows
        row = lax.broadcasted_iota(jnp.int32, (cells, 2 * cells), 0)
        col = lanes_of((cells, 2 * cells))
        half_sum = jnp.zeros((cells, 2 * cells), F32)
        for shift, ref in ((-cells, yl_ref), (0, mid_ref), (cells, yr_ref)):
            weight = jnp.maximum(R + 1 - jnp.abs(col % cells + shift - row), 0)
            tall = ref[PLANES * planes_here + 2 * R :]
            half_sum = half_sum + lax.dot_general(
                weight.astype(F32).astype(BF16),
                tall,
                (((1,), (1,)), ((), ())),
                preferred_element_type=F32,
            )
        row = lax.broadcasted_iota(jnp.int32, (2 * cells, depth), 0)
        col = lanes_of((2 * cells, depth))
        weight = jnp.maximum(R + 1 - jnp.abs(row - R - col), 0).astype(F32).astype(BF16)
        filtered = twice(half_sum, weight) / float((R + 1) ** 4)
        tangent = jnp.tanh(SHARPNESS * (filtered - THRESHOLD))
        total = math.tanh(SHARPNESS * THRESHOLD) + math.tanh(SHARPNESS * (1.0 - THRESHOLD))
        slope = SHARPNESS * (1.0 - tangent * tangent) / total
        weighted = slope * sens[...] * scale
        half = rows // 2
        both = pltpu.roll(weighted[half:], depth // 2, 1)
        sens_ref[:half] = jnp.where(lane[:half] < depth // 2, weighted[:half], both)
        mine = jnp.where(lax.axis_index("gz") == 0, own_ref[...].astype(F32), 0.0)
        sens_ref[half:] = jnp.concatenate([mine, jnp.zeros((8, depth - rows), F32)], 1)
        for i in range(groups):
            store(i).wait()


def twice(value, right):
    high, low = split(value)
    return mm(high, right) + mm(low, right)


def left_twice(left, value):
    high, low = split(value)
    return mm(left, high) + mm(left, low)


SMEM_SPEC = pl.BlockSpec(memory_space=pltpu.SMEM)
VMEM_SPEC = pl.BlockSpec(memory_space=pltpu.VMEM)


def near(value):
    return pltpu.with_memory_space_constraint(value, pltpu.VMEM)


def far_away(value):
    return pltpu.with_memory_space_constraint(value, pltpu.HBM)


def local(kernel, name, operands, specs, shapes, out_specs, scratch, limit, cost):
    return pl.pallas_call(
        kernel,
        in_specs=specs,
        out_specs=out_specs,
        out_shape=shapes,
        scratch_shapes=scratch,
        compiler_params=pltpu.CompilerParams(vmem_limit_bytes=limit << 20),
        cost_estimate=pl.CostEstimate(flops=cost, bytes_accessed=cost, transcendentals=0),
        name=name,
    )(*operands)


def shift(value, axis, up):
    count = lax.axis_size(axis)
    pairs = [(i, i + 1) for i in range(count - 1)]
    return lax.ppermute(value, axis, pairs if up else [(j, i) for i, j in pairs])


def shift_z(g):
    if lax.axis_size("gz") == 2:
        other = lax.ppermute(g, "gz", [(0, 1), (1, 0)])
        return other, other
    return shift(g, "gz", True), shift(g, "gz", False)


def sweeps(tables, share, fields, sources, material, density, owners):
    _, nx, ny, nz = fields.shape
    nz_parts = lax.axis_size("gz")
    hbm = pl.BlockSpec(memory_space=pltpu.HBM)
    held = [near(a) for a in (fields, sources, material)]

    x_shape = jax.ShapeDtypeStruct((PLANES * ny + 2 * R, nz), BF16)
    y_shape = jax.ShapeDtypeStruct((PLANES * nx + 2 * R + 2 * nx, nz), BF16)
    g_shape = jax.ShapeDtypeStruct((4, ny, nz), BF16)
    wide_g = jax.ShapeDtypeStruct((8, ny, nz), BF16)
    xlo, xhi = local(
        x_kernel,
        "x_faces",
        [far_away(a) for a in (fields, sources, material)] + [density],
        [hbm] * 3 + [VMEM_SPEC],
        [x_shape] * 2,
        [VMEM_SPEC] * 2,
        [
            pltpu.VMEM((2, 4, 2, ny, nz), F32),
            pltpu.VMEM((2, 4, ny, nz), BF16),
            pltpu.VMEM((2, ny, nz), jnp.int32),
            pltpu.SemaphoreType.DMA((6,)),
        ],
        8,
        ny * nz * 100,
    )
    xl, xr = shift(xhi, "gx", True), shift(xlo, "gx", False)
    part_shape = jax.ShapeDtypeStruct((PLANES * nx, nz), BF16)
    lo, hi, g = local(
        pack_kernel,
        "pack_faces",
        held,
        [VMEM_SPEC] * 3,
        [part_shape, part_shape, g_shape],
        [VMEM_SPEC] * 3,
        [
            pltpu.VMEM((4, ny, nz), F32),
            pltpu.VMEM((PLANES, nx, nz), F32),
            pltpu.VMEM((PLANES, nx, nz), F32),
            pltpu.VMEM((PB * nz, nz), BF16),
        ],
        12,
        fields.size * 4,
    )
    cut = nx // 2
    inside = [
        local(
            functools.partial(inside_kernel, start),
            "inside",
            held[:2],
            [VMEM_SPEC] * 2,
            [pltpu.VMEM((4, cut, ny, nz), F32), jax.ShapeDtypeStruct((8, nz), F32)],
            [VMEM_SPEC] * 2,
            [
                pltpu.VMEM((2 * nz, nz), BF16),
                pltpu.VMEM((4, PB, ny, nz), F32),
                pltpu.VMEM((4, PB, ny, nz), F32),
            ],
            8,
            fields.size * 5,
        )
        for start in (0, cut)
    ]
    ylo, yhi = local(
        corner_kernel,
        "corners",
        [lo, hi, density, xl, xr, inside[0][1]],
        [VMEM_SPEC] * 6,
        [y_shape] * 2,
        [VMEM_SPEC] * 2,
        [],
        8,
        ny * nz * 40,
    )
    yl, yr = shift(yhi, "gy", True), shift(ylo, "gy", False)
    g = local(
        edge_kernel,
        "edge_faces",
        [g, xl, xr, yl, yr, inside[1][1]],
        [VMEM_SPEC] * 6,
        wide_g,
        VMEM_SPEC,
        [],
        8,
        ny * nz * 40,
    )
    gl, gr = shift_z(g)

    def scratch(parts):
        return [
            pltpu.VMEM((parts, ny, nz), F32),
            pltpu.VMEM((4, nx, nz), F32),
            pltpu.VMEM((4, nx, nz), F32),
            pltpu.VMEM((2 * nz, nz), BF16),
            pltpu.VMEM((nz, nz), BF16),
            pltpu.VMEM((4, PB, ny, nz), F32),
            pltpu.VMEM((4, PB, ny, nz), F32),
        ]

    scale = 1.0 / math.sqrt(nz * nz_parts)
    middle, ext, g = local(
        functools.partial(sweep_kernel, False, nz_parts, scale),
        "sweep_first",
        [*tables, held[0], density, held[2], gl, gr, xl, xr, yl, yr, ylo, yhi, *(near(t) for t, _ in inside)],
        [SMEM_SPEC] * 2 + [VMEM_SPEC] * 13,
        [pltpu.VMEM(fields.shape, F32), jax.ShapeDtypeStruct((16 * ny, nz), F32), g_shape],
        [VMEM_SPEC] * 3,
        scratch(8) + [pltpu.VMEM((4, ny, nz), F32), pltpu.VMEM((PB * nz, nz), BF16)],
        20,
        fields.size * 20,
    )
    gl, gr = shift_z(g)
    return local(
        functools.partial(sweep_kernel, True, nz_parts, scale),
        "sweep_last",
        [*tables, near(middle), *held[1:], gl, gr, ext, ylo, yl, yr, share, owners],
        [SMEM_SPEC] * 2 + [VMEM_SPEC] * 9 + [SMEM_SPEC, VMEM_SPEC],
        [
            jax.ShapeDtypeStruct(fields.shape, F32),
            jax.ShapeDtypeStruct((ny // 2 + 8, nz), F32),
        ],
        [hbm, VMEM_SPEC],
        scratch(4)
        + [
            pltpu.VMEM((ny, nz), F32),
            pltpu.VMEM(fields.shape, F32),
            pltpu.SemaphoreType.DMA((nx // PB,)),
        ],
        20,
        fields.size * 20,
    )


STEPS = 32767.0


def share_kernel(got_ref, out_ref):
    half = got_ref.shape[1] - 8
    both = got_ref[0]
    for part in range(1, got_ref.shape[0]):
        both = both + got_ref[part]
    value = both[:half]
    top = jnp.max(jnp.abs(value), axis=0, keepdims=True)
    power = jnp.floor(jnp.log(jnp.maximum(top, 1e-30)) * (1.0 / math.log(2.0))) + 1.0
    steps = jnp.floor(value * (STEPS * jnp.exp2(-power)) + 0.5)
    steps = jnp.clip(steps, -STEPS, STEPS)
    power = jnp.broadcast_to(power, (8, value.shape[1]))
    block = jnp.concatenate([steps, power, both[half:]], 0).astype(jnp.int32).astype(jnp.int16)
    for c in range(out_ref.shape[0]):
        out_ref[c] = block


def plane_kernel(ngx, ngy, me_ref, got_ref, out_ref, w_ref):
    cells = 64
    nx, ny = ngx * cells, ngy * cells
    columns = ngx * ngy
    half = cells // 2
    owners = []
    for cx in range(ngx):
        for cy in range(ngy):
            c = cx * ngy + cy
            got = got_ref[c].astype(jnp.int32).astype(F32)
            value = got[:half] * (jnp.exp2(got[half : half + 1]) * (1.0 / STEPS))
            for part in range(2):
                w_ref[pl.ds(cy * cells + part * half, half), pl.ds(cx * cells, cells)] = value[
                    :, part * cells : (part + 1) * cells
                ]
            owners.append(got[half + 8 : half + 9, :cells])

    def band(n):
        i = lax.broadcasted_iota(jnp.int32, (n, n), 0)
        j = lax.broadcasted_iota(jnp.int32, (n, n), 1)
        return jnp.maximum(R + 1 - jnp.abs(i - j), 0).astype(F32).astype(BF16)

    unit = float((R + 1) ** 4)
    weighted = twice(w_ref[...], band(nx))

    tiles = cells
    owner = jnp.concatenate(owners, 0)
    mine = owner == me_ref[0].astype(F32)
    flag = jnp.where(mine, 1.0, 0.0)
    a = lax.broadcasted_iota(jnp.int32, (tiles, tiles), 0)
    b = lax.broadcasted_iota(jnp.int32, (tiles, tiles), 1)
    rank = mm(flag.astype(BF16), jnp.where(a < b, 1.0, 0.0).astype(BF16))
    number = lanes_of((columns, tiles))
    column = lax.broadcasted_iota(jnp.int32, (columns, 1), 0)
    rows, blocks = [], []
    for k in range(MOST):
        chosen = mine & (rank == float(k))
        tile = jnp.sum(jnp.where(chosen, number, 0), axis=1, keepdims=True)
        there = jnp.sum(jnp.where(chosen, 1, 0), axis=1, keepdims=True)
        rows.append((column % ngy) * cells + (tile % (cells // TS)) * TS)
        block = (column // ngy) * (cells // TS) + tile // (cells // TS)
        blocks.append(jnp.where(there > 0, block, -1))
    row = jnp.concatenate(rows, 0)
    block = jnp.concatenate(blocks, 0)
    slots = MOST * columns
    across = lax.broadcasted_iota(jnp.int32, (slots, ny), 1)
    lefts = [
        jnp.maximum(R + 1 - jnp.abs(row + j - across), 0).astype(F32).astype(BF16)
        for j in range(TS)
    ]
    lines = left_twice(jnp.concatenate(lefts, 0), weighted)
    keep = lanes_of((slots, nx)) // TS == block
    from_x = lax.broadcasted_iota(jnp.int32, (nx, TS * TS), 0) % TS
    to_q = lanes_of((nx, TS * TS))
    out = jnp.zeros((slots, TS * TS), F32)
    for j in range(TS):
        fold = jnp.where(to_q == from_x * TS + j, 1.0, 0.0).astype(BF16)
        out = out + twice(jnp.where(keep, lines[j * slots : (j + 1) * slots], 0.0), fold)
    out = out / unit
    for k in range(MOST):
        out_ref[0, :, pl.ds(k * TS * TS, TS * TS)] = out[k * columns : (k + 1) * columns]


def on_device(fields, sources, material, shift_real, shift_imag, design_share, density, owner_map):
    ngx, ngy = lax.axis_size("gx"), lax.axis_size("gy")
    columns = ngx * ngy
    cells = density.shape[0]
    tables = (shift_real, shift_imag)
    owners = jnp.broadcast_to(owner_map.reshape(1, -1), (8, cells))
    final, partial = sweeps(tables, design_share, fields, sources, material, density, owners)
    partial = lax.all_gather(partial, "gz")
    copies = local(
        share_kernel,
        "share",
        [partial],
        [VMEM_SPEC],
        jax.ShapeDtypeStruct((columns, partial.shape[1] + 8, partial.shape[2]), jnp.int16),
        VMEM_SPEC,
        [],
        8,
        partial.size * 16,
    )
    plane = lax.all_to_all(copies, ("gx", "gy"), split_axis=0, concat_axis=0)
    me = (lax.axis_index("gx") * ngy + lax.axis_index("gy")).reshape(1)
    owned = pl.pallas_call(
        functools.partial(plane_kernel, ngx, ngy),
        in_specs=[SMEM_SPEC, VMEM_SPEC],
        out_specs=VMEM_SPEC,
        out_shape=jax.ShapeDtypeStruct((1, columns, MOST * TS * TS), F32),
        scratch_shapes=[pltpu.VMEM((ngy * cells, ngx * cells), F32)],
        compiler_params=pltpu.CompilerParams(vmem_limit_bytes=16 << 20),
        name="plane",
    )(me, plane)
    return (final, owned)


def solution(mesh):
    placed = (
        P(None, "gx", "gy", "gz"),
        P(None, "gx", "gy", "gz"),
        P("gx", "gy", "gz"),
        P(),
        P(),
        P(),
        P("gx", "gy"),
        P("gx", "gy", None, None),
    )
    return jax.shard_map(
        on_device,
        mesh=mesh,
        in_specs=placed,
        out_specs=(P(None, "gx", "gy", "gz"), P(("gx", "gy"), None, None)),
        check_vma=False,
    )
```

```python
import functools
import math

import jax
import jax.numpy as jnp
from jax import lax
from jax.experimental import pallas as pl
from jax.experimental.pallas import tpu as pltpu
from jax.sharding import PartitionSpec as P

R = 8
TS = 8
MOST = 8
RELAXATION = 0.8
SHARPNESS = 8.0
THRESHOLD = 0.5
PB = 8
RC = 16
F32 = jnp.float32
BF16 = jnp.bfloat16


def lanes_of(shape):
    return lax.broadcasted_iota(jnp.int32, shape, len(shape) - 1)


def ends_matrix(depth):
    k = lax.broadcasted_iota(jnp.int32, (PB * depth, depth), 0)
    j = lax.broadcasted_iota(jnp.int32, (PB * depth, depth), 1) % (2 * PB)
    even = (k % depth == 0) & (j == 2 * (k // depth))
    odd = (k % depth == depth - 1) & (j == 2 * (k // depth) + 1)
    return jnp.where(even | odd, 1.0, 0.0).astype(BF16)


def beside_matrix(depth):
    z = lax.broadcasted_iota(jnp.int32, (depth, depth), 0)
    j = lax.broadcasted_iota(jnp.int32, (depth, depth), 1)
    return jnp.where(jnp.abs(z - j) == 1, 1.0, 0.0).astype(BF16)


def halo_matrix(depth):
    j = lax.broadcasted_iota(jnp.int32, (depth, depth), 0)
    z = lax.broadcasted_iota(jnp.int32, (depth, depth), 1)
    even = (z == 0) & (j % 2 == 0)
    odd = (z == depth - 1) & (j % 2 == 1)
    return jnp.where(even | odd, 1.0, 0.0).astype(BF16)


def split(value):
    high = value.astype(BF16)
    return high, (value - high.astype(F32)).astype(BF16)


def mm(a, b):
    return lax.dot_general(a, b, (((1,), (0,)), ((), ())), preferred_element_type=F32)


def put_ends(first, ref, ends, gs):
    rows, depth = ref.shape[2:]
    high = ref[:, pl.ds(first, PB)].astype(BF16)
    beside = [high[:, p].reshape(4 * rows, depth) for p in range(PB)]
    picked = mm(jnp.concatenate(beside, 1), ends).reshape(4, rows, depth)
    here = lanes_of((rows, depth)) // (2 * PB) == first // PB
    for c in range(4):
        gs[c] = jnp.where(here, picked[c], gs[c])


def paired(value):
    high = value.astype(BF16).astype(F32)
    return jnp.concatenate([high, value - high], 1)


PLANES = 9


def x_kernel(v_ref, s_ref, m_ref, d_ref, xlo_ref, xhi_ref, vs, ss, ms, ds, sems):
    last = v_ref.shape[1] - 1
    rows, depth = v_ref.shape[2:]
    sides = ((0, 0, 1), (last, last - 1, 0))
    copies = []
    for i, (x, second, _) in enumerate(sides):
        copies.append(
            [
                pltpu.make_async_copy(
                    v_ref.at[:, pl.ds(min(x, second), 2)], vs.at[i], sems.at[3 * i]
                ),
                pltpu.make_async_copy(s_ref.at[:, x], ss.at[i], sems.at[3 * i + 1]),
                pltpu.make_async_copy(m_ref.at[x], ms.at[i], sems.at[3 * i + 2]),
            ]
        )
    for side in copies:
        for copy in side:
            copy.start()
    plane = pltpu.make_async_copy(d_ref, ds, sems.at[6])
    plane.start()
    plane.wait()
    cells = d_ref.shape[0]
    none = jnp.zeros((R, depth), F32)
    for i, (out_ref, start) in enumerate(((xlo_ref, 0), (xhi_ref, cells - R))):
        strip = jnp.concatenate([paired(ds[start : start + R, :]), none], 0)
        out_ref[PLANES * rows :] = strip.astype(BF16)
        for copy in copies[i]:
            copy.wait()
        inner = sides[i][2]
        out_ref[: 4 * rows] = vs[i, :, 1 - inner].astype(BF16).reshape(4 * rows, depth)
        beyond = vs[i, :, inner] + ss[i].astype(F32)
        out_ref[4 * rows : 8 * rows] = beyond.astype(BF16).reshape(4 * rows, depth)
        out_ref[8 * rows : 9 * rows] = (ms[i] + 1).astype(F32).astype(BF16)


def pack_kernel(v_ref, s_ref, m_ref, ylo_ref, yhi_ref, g_ref, gs, ylo, yhi, ends):
    rows, depth = v_ref.shape[2:]
    gs[...] = jnp.zeros_like(gs)
    ends[...] = ends_matrix(depth)

    def group(i, carry):
        first = i * PB
        put_ends(first, v_ref, ends[...], gs)
        for p in range(PB):
            x = first + p
            here = pl.ds(x, 1)
            level = (m_ref[x] + 1).astype(F32)
            for out, edge, inner, low in ((ylo, 0, 1, 0), (yhi, rows - 1, rows - 2, rows - 16)):
                for c in range(4):
                    out[c, here, :] = v_ref[c, x, edge : edge + 1, :]
                    source = s_ref[c, x, low : low + 16, :].astype(F32)[edge - low : edge - low + 1]
                    out[4 + c, here, :] = v_ref[c, x, inner : inner + 1, :] + source
                out[8, here, :] = level[edge : edge + 1]
        return carry

    lax.fori_loop(0, v_ref.shape[1] // PB, group, 0)
    g_ref[...] = gs[...].astype(BF16)
    for out_ref, rows_out in ((ylo_ref, ylo), (yhi_ref, yhi)):
        out_ref[...] = rows_out[...].astype(BF16).reshape(out_ref.shape)


def corner_kernel(lo_ref, hi_ref, d_ref, xl_ref, xr_ref, _, ylo_ref, yhi_ref):
    block, depth = lo_ref.shape
    cells = d_ref.shape[0]
    rows = (xl_ref.shape[0] - 2 * R) // PLANES
    strips = [r[PLANES * rows :].astype(F32)[:R] for r in (xl_ref, xr_ref)]
    filler = jnp.zeros((cells - 2 * R, depth), F32)
    tall = jnp.concatenate([strips[0], paired(d_ref[...]), strips[1], filler], 0).astype(BF16)
    for out_ref, from_ref, edge, low in (
        (ylo_ref, lo_ref, 0, 0),
        (yhi_ref, hi_ref, rows - 1, rows - 16),
    ):
        out_ref[:block] = from_ref[...]
        corners = [
            r[c * rows + low : c * rows + low + 16].astype(F32)[edge - low : edge - low + 1]
            for r in (xl_ref, xr_ref)
            for c in range(4)
        ]
        corners.append(jnp.zeros((2 * R - 8, depth), F32))
        out_ref[block : block + 2 * R] = jnp.concatenate(corners, 0).astype(BF16)
        out_ref[block + 2 * R :] = tall


def inside_kernel(start, v_ref, s_ref, t_ref, token_ref, near, zt0, zt1):
    planes_here, rows, depth = v_ref.shape[1:]
    token_ref[...] = jnp.zeros_like(token_ref)
    near[...] = jnp.concatenate([beside_matrix(depth)] * 2, 0)
    row8 = lax.broadcasted_iota(jnp.int32, (8, depth), 0)
    count = t_ref.shape[1]

    def along_z(first, zt):
        v = v_ref[:, pl.ds(first, PB)].reshape(4 * PB * rows, depth)
        zt[...] = mm(jnp.concatenate(split(v), 1), near[...]).reshape(4, PB, rows, depth)

    def group(i, zt, zt_next):
        first = start + i * PB
        along_z(jnp.minimum(first + PB, start + count - PB), zt_next)
        for p in range(PB):
            x = first + p
            for low in range(0, rows, RC):
                span = slice(low, low + RC)
                for c in range(4):
                    v = v_ref[c, x, span]
                    before = v_ref[c, jnp.maximum(x - 1, 0), span]
                    after = v_ref[c, jnp.minimum(x + 1, planes_here - 1), span]
                    if p == 0:
                        before = jnp.where(x == 0, 0.0, before)
                    if p == PB - 1:
                        after = jnp.where(x == planes_here - 1, 0.0, after)
                    if low == 0:
                        up = pltpu.roll(v, 1, 0)
                        up = jnp.concatenate([jnp.where(row8 == 0, 0.0, up[:8]), up[8:]], 0)
                    else:
                        up = v_ref[c, x, low - 1 : low - 1 + RC]
                    if low == rows - RC:
                        down = pltpu.roll(v, RC - 1, 0)
                        down = jnp.concatenate([down[:-8], jnp.where(row8 == 7, 0.0, down[-8:])], 0)
                    else:
                        down = v_ref[c, x, low + 1 : low + 1 + RC]
                    total = before + after + s_ref[c, x, span].astype(F32) + zt[c, p, span]
                    t_ref[c, i * PB + p, span] = total + up + down

    def two(i, carry):
        group(2 * i, zt0, zt1)
        group(2 * i + 1, zt1, zt0)
        return carry

    along_z(start, zt0)
    lax.fori_loop(0, count // (2 * PB), two, 0)


def edge_kernel(g_ref, xl_ref, xr_ref, yl_ref, yr_ref, _, out_ref):
    parts, rows, depth = g_ref.shape
    beside = [r[: 4 * rows] for r in (xl_ref, xr_ref, yl_ref, yr_ref)]
    picked = mm(jnp.concatenate(beside, 1), ends_matrix(depth)[: 4 * depth])
    out_ref[:4] = g_ref[...]
    out_ref[4:] = picked.astype(BF16).reshape(4, rows, depth)


def sweep_kernel(last, nz, scale, *refs):
    sr_ref, si_ref, v_ref, s_ref, m_ref, gl_ref, gr_ref = refs[:7]
    if last:
        ext_ref, mid_ref, yl_ref, yr_ref, sh_ref, own_ref, o_ref, sens_ref = refs[7:15]
        hs, yl, yr, near, far, zt0, zt1, sens, news, sems = refs[15:]
    else:
        xl_ref, xr_ref, yl_ref, yr_ref, ylo_ref, yhi_ref = refs[7:13]
        ta_ref, tb_ref, o_ref, ext_ref, g_ref = refs[13:18]
        hs, yl, yr, near, far, zt0, zt1, gs, ends = refs[18:]
    planes_here, rows, depth = v_ref.shape[1:]
    lane = lanes_of((rows, depth))

    if nz == 2:
        here = lax.axis_index("gz").astype(F32)
        keep_l, keep_r = here, 1.0 - here
    else:
        keep_l, keep_r = 1.0, 1.0
    for c in range(gl_ref.shape[0]):
        left = pltpu.roll(gl_ref[c].astype(F32), depth - 1, 1) * keep_l
        right = pltpu.roll(gr_ref[c].astype(F32), 1, 1) * keep_r
        hs[c] = jnp.where(lane % 2 == 0, left, right)
    near[...] = jnp.concatenate([beside_matrix(depth)] * 2, 0)
    far[...] = halo_matrix(depth)
    if last:
        sens[...] = jnp.zeros_like(sens)
    else:
        gs[...] = jnp.zeros_like(gs)
        ends[...] = ends_matrix(depth)
    face = 4 * rows
    if last:
        yl[...] = ext_ref[2 * face : 3 * face].reshape(4, rows, depth)
        yr[...] = ext_ref[3 * face : 4 * face].reshape(4, rows, depth)
    else:
        yl[...] = yl_ref[:face].astype(F32).reshape(4, rows, depth)
        yr[...] = yr_ref[:face].astype(F32).reshape(4, rows, depth)

    def x_halo(side, low):
        if last:
            return ext_ref[side * face + low : side * face + low + RC]
        return (xl_ref, xr_ref)[side][low : low + RC].astype(F32)

    levels = sr_ref.shape[0]
    tile = (8, depth)
    wr, wi, share = [], [], []
    for m in range(levels):
        d = 6.0 + jnp.full(tile, sr_ref[m], F32)
        s = jnp.full(tile, si_ref[m], F32)
        mag = d * d + s * s
        wr.append(RELAXATION * d / mag)
        wi.append(-RELAXATION * s / mag)
        if last:
            share.append(jnp.full(tile, sh_ref[m], F32))

    def lookup(masks, table):
        out = jnp.broadcast_to(table[0], masks[0].shape)
        for mask, entry in zip(masks, table[1:]):
            out = jnp.where(mask, entry, out)
        return out.reshape(-1, depth)

    row8 = lax.broadcasted_iota(jnp.int32, tile, 0)

    def along_z(first, zt):
        masked = [
            jnp.where(lane // 2 == first + p, hs[c], 0.0).astype(BF16)
            for c in range(4)
            for p in range(PB)
        ]
        out = mm(jnp.concatenate(masked, 0), far[...])
        if last:
            v = v_ref[:, pl.ds(first, PB)].reshape(4 * PB * rows, depth)
            out = out + mm(jnp.concatenate(split(v), 1), near[...])
        zt[...] = out.reshape(4, PB, rows, depth)

    def plane(first, p, zt, put, inside=None):
        for low in range(0, rows, RC):
            chunk(first, p, low, zt, put, inside)

    def chunk(first, p, low, zt, put, inside):
        x = first + p
        span = slice(low, low + RC)
        mat = m_ref[x, span].reshape(RC // 8, 8, depth)
        masks = [mat == m for m in range(1, levels)]
        w_r, w_i = lookup(masks, wr), lookup(masks, wi)

        def join(c):
            t_ref, t_start = inside
            total = t_ref[c, x - t_start, span] + zt[c, p, span]
            if p == 0:
                total = total + jnp.where(x == 0, x_halo(0, c * rows + low), 0.0)
            if p == PB - 1:
                total = total + jnp.where(x == planes_here - 1, x_halo(1, c * rows + low), 0.0)
            if low == 0:
                top = total[:8] + jnp.where(row8 == 0, yl[c, pl.ds(x, 1), :], 0.0)
                total = jnp.concatenate([top, total[8:]], 0)
            if low == rows - RC:
                tail = total[-8:] + jnp.where(row8 == 7, yr[c, pl.ds(x, 1), :], 0.0)
                total = jnp.concatenate([total[:-8], tail], 0)
            return v_ref[c, x, span], total

        def drive(c):
            if not last:
                return join(c)
            v = v_ref[c, x, span]
            if p == 0:
                before = v_ref[c, jnp.maximum(x - 1, 0), span]
                before = jnp.where(x == 0, x_halo(0, c * rows + low), before)
            else:
                before = v_ref[c, x - 1, span]
            if p == PB - 1:
                after = v_ref[c, jnp.minimum(x + 1, planes_here - 1), span]
                after = jnp.where(x == planes_here - 1, x_halo(1, c * rows + low), after)
            else:
                after = v_ref[c, x + 1, span]
            total = before + after + s_ref[c, x, span].astype(F32) + zt[c, p, span]
            if low == 0:
                up = pltpu.roll(v, 1, 0)
                top = jnp.where(row8 == 0, yl[c, pl.ds(x, 1), :], up[:8])
                up = jnp.concatenate([top, up[8:]], 0)
            else:
                up = v_ref[c, x, low - 1 : low - 1 + RC]
            if low == rows - RC:
                down = pltpu.roll(v, RC - 1, 0)
                tail = jnp.where(row8 == 7, yr[c, pl.ds(x, 1), :], down[-8:])
                down = jnp.concatenate([down[:-8], tail], 0)
            else:
                down = v_ref[c, x, low + 1 : low + 1 + RC]
            return v, total + up + down

        new = []
        for re in (0, 2):
            v_r, t_r = drive(re)
            v_i, t_i = drive(re + 1)
            keep = 1.0 - RELAXATION
            n_r = keep * v_r + (w_r * t_r - w_i * t_i)
            n_i = keep * v_i + (w_r * t_i + w_i * t_r)
            put(re, span, n_r)
            put(re + 1, span, n_i)
            new += [n_r, n_i]
        if last:
            value = lookup(masks, share) * (new[0] * new[2] - new[1] * new[3])
            column = jnp.sum(value, axis=1, keepdims=True)
            sens[span] = jnp.where(lane[:RC] == x, column, sens[span])

    groups = planes_here // PB

    def store(i):
        part = pl.ds(i * PB, PB)
        return pltpu.make_async_copy(news.at[:, part], o_ref.at[:, part], sems.at[i])

    result = news if last else o_ref

    def group(i, zt, zt_next, inside=None):
        first = i * PB
        along_z(jnp.minimum(first + PB, planes_here - PB), zt_next)
        for p in range(PB):

            def put(c, span, new, p=p):
                result[c, first + p, span] = new

            plane(first, p, zt, put, inside)
        if last:
            store(i).start()
        else:
            put_ends(first, o_ref, ends[...], gs)

    def pairs(begin, end, inside=None):
        def two(i, carry):
            group(2 * i, zt0, zt1, inside)
            group(2 * i + 1, zt1, zt0, inside)
            return carry

        lax.fori_loop(begin, end, two, 0)

    along_z(0, zt0)
    if last:
        pairs(0, groups // 2)
    else:
        cut = ta_ref.shape[1]
        pairs(0, cut // (2 * PB), (ta_ref, 0))
        pairs(cut // (2 * PB), groups // 2, (tb_ref, cut))

    if not last:
        g_ref[...] = gs[...].astype(BF16)
        sides = (xl_ref, xr_ref, yl_ref, yr_ref)
        centres = jnp.concatenate([r[:face] for r in sides], 0)
        masked = [
            jnp.where(lane // 2 == e, hs[4 + c], 0.0).astype(BF16) for e in range(4) for c in range(4)
        ]
        along = mm(centres, near[:depth]) + mm(jnp.concatenate(masked, 0), far[...])
        for e in range(4):
            zt0[:, e] = along[e * face : (e + 1) * face].reshape(4, rows, depth)
        block = PLANES * planes_here
        corner_l = yl_ref[block : block + 2 * R].astype(F32)
        corner_r = yr_ref[block : block + 2 * R].astype(F32)
        zero = jnp.zeros(tile, F32)
        for e, ref in enumerate(sides):
            level = ref[2 * face : 2 * face + rows].astype(F32).reshape(rows // 8, 8, depth)
            masks = [level == float(m + 1) for m in range(levels)]
            w_r, w_i = lookup(masks, [zero] + wr), lookup(masks, [zero] + wi)

            def near_plane(c, e=e, ref=ref):
                part = slice(c * rows, (c + 1) * rows)
                v = ref[part].astype(F32)
                beyond = ref[face + c * rows : face + (c + 1) * rows].astype(F32)
                if e < 2:
                    inside = v_ref[c, 0 if e == 0 else planes_here - 1]
                    top, low = corner_l[4 * e + c : 4 * e + c + 1], corner_r[4 * e + c : 4 * e + c + 1]
                else:
                    inside = (ylo_ref, yhi_ref)[e - 2][part].astype(F32)
                    corner = corner_l if e == 2 else corner_r
                    top, low = corner[c : c + 1], corner[4 + c : 5 + c]
                total = beyond + inside + zt0[c, e]
                up = pltpu.roll(v, 1, 0)
                down = pltpu.roll(v, rows - 1, 0)
                up = jnp.concatenate([jnp.where(row8 == 0, top, up[:8]), up[8:]], 0)
                down = jnp.concatenate([down[:-8], jnp.where(row8 == 7, low, down[-8:])], 0)
                return v, total + up + down

            for re in (0, 2):
                v_r, t_r = near_plane(re)
                v_i, t_i = near_plane(re + 1)
                keep = 1.0 - RELAXATION
                at = e * face + re * rows
                ext_ref[at : at + rows] = keep * v_r + (w_r * t_r - w_i * t_i)
                ext_ref[at + rows : at + 2 * rows] = keep * v_i + (w_r * t_i + w_i * t_r)
    else:
        cells = rows
        row = lax.broadcasted_iota(jnp.int32, (cells, 2 * cells), 0)
        col = lanes_of((cells, 2 * cells))
        half_sum = jnp.zeros((cells, 2 * cells), F32)
        for shift, ref in ((-cells, yl_ref), (0, mid_ref), (cells, yr_ref)):
            weight = jnp.maximum(R + 1 - jnp.abs(col % cells + shift - row), 0)
            tall = ref[PLANES * planes_here + 2 * R :]
            half_sum = half_sum + lax.dot_general(
                weight.astype(F32).astype(BF16),
                tall,
                (((1,), (1,)), ((), ())),
                preferred_element_type=F32,
            )
        row = lax.broadcasted_iota(jnp.int32, (2 * cells, depth), 0)
        col = lanes_of((2 * cells, depth))
        weight = jnp.maximum(R + 1 - jnp.abs(row - R - col), 0).astype(F32).astype(BF16)
        filtered = twice(half_sum, weight) / float((R + 1) ** 4)
        tangent = jnp.tanh(SHARPNESS * (filtered - THRESHOLD))
        total = math.tanh(SHARPNESS * THRESHOLD) + math.tanh(SHARPNESS * (1.0 - THRESHOLD))
        slope = SHARPNESS * (1.0 - tangent * tangent) / total
        weighted = slope * sens[...] * scale
        half = rows // 2
        both = pltpu.roll(weighted[half:], depth // 2, 1)
        sens_ref[:half] = jnp.where(lane[:half] < depth // 2, weighted[:half], both)
        mine = jnp.where(lax.axis_index("gz") == 0, own_ref[...].astype(F32), 0.0)
        sens_ref[half:] = jnp.concatenate([mine, jnp.zeros((8, depth - rows), F32)], 1)
        for i in range(groups):
            store(i).wait()


def twice(value, right):
    high, low = split(value)
    return mm(high, right) + mm(low, right)


def left_twice(left, value):
    high, low = split(value)
    return mm(left, high) + mm(left, low)


SMEM_SPEC = pl.BlockSpec(memory_space=pltpu.SMEM)
VMEM_SPEC = pl.BlockSpec(memory_space=pltpu.VMEM)


def near(value):
    return pltpu.with_memory_space_constraint(value, pltpu.VMEM)


def far_away(value):
    return pltpu.with_memory_space_constraint(value, pltpu.HBM)


def local(kernel, name, operands, specs, shapes, out_specs, scratch, limit, cost):
    return pl.pallas_call(
        kernel,
        in_specs=specs,
        out_specs=out_specs,
        out_shape=shapes,
        scratch_shapes=scratch,
        compiler_params=pltpu.CompilerParams(vmem_limit_bytes=limit << 20),
        cost_estimate=pl.CostEstimate(flops=cost, bytes_accessed=cost, transcendentals=0),
        name=name,
    )(*operands)


def shift(value, axis, up):
    count = lax.axis_size(axis)
    pairs = [(i, i + 1) for i in range(count - 1)]
    return lax.ppermute(value, axis, pairs if up else [(j, i) for i, j in pairs])


def shift_z(g):
    if lax.axis_size("gz") == 2:
        other = lax.ppermute(g, "gz", [(0, 1), (1, 0)])
        return other, other
    return shift(g, "gz", True), shift(g, "gz", False)


def sweeps(tables, share, fields, sources, material, density, owners):
    _, nx, ny, nz = fields.shape
    nz_parts = lax.axis_size("gz")
    hbm = pl.BlockSpec(memory_space=pltpu.HBM)
    held = [near(a) for a in (fields, sources, material)]

    x_shape = jax.ShapeDtypeStruct((PLANES * ny + 2 * R, nz), BF16)
    y_shape = jax.ShapeDtypeStruct((PLANES * nx + 2 * R + 2 * nx, nz), BF16)
    g_shape = jax.ShapeDtypeStruct((4, ny, nz), BF16)
    wide_g = jax.ShapeDtypeStruct((8, ny, nz), BF16)
    xlo, xhi = local(
        x_kernel,
        "x_faces",
        [far_away(a) for a in (fields, sources, material, density)],
        [hbm] * 4,
        [x_shape] * 2,
        [VMEM_SPEC] * 2,
        [
            pltpu.VMEM((2, 4, 2, ny, nz), F32),
            pltpu.VMEM((2, 4, ny, nz), BF16),
            pltpu.VMEM((2, ny, nz), jnp.int32),
            pltpu.VMEM(density.shape, F32),
            pltpu.SemaphoreType.DMA((7,)),
        ],
        8,
        ny * nz * 100,
    )
    xl, xr = shift(xhi, "gx", True), shift(xlo, "gx", False)
    part_shape = jax.ShapeDtypeStruct((PLANES * nx, nz), BF16)
    lo, hi, g = local(
        pack_kernel,
        "pack_faces",
        held,
        [VMEM_SPEC] * 3,
        [part_shape, part_shape, g_shape],
        [VMEM_SPEC] * 3,
        [
            pltpu.VMEM((4, ny, nz), F32),
            pltpu.VMEM((PLANES, nx, nz), F32),
            pltpu.VMEM((PLANES, nx, nz), F32),
            pltpu.VMEM((PB * nz, nz), BF16),
        ],
        12,
        fields.size * 4,
    )
    cut = nx // 2
    inside = [
        local(
            functools.partial(inside_kernel, start),
            "inside",
            held[:2],
            [VMEM_SPEC] * 2,
            [pltpu.VMEM((4, cut, ny, nz), F32), jax.ShapeDtypeStruct((8, nz), F32)],
            [VMEM_SPEC] * 2,
            [
                pltpu.VMEM((2 * nz, nz), BF16),
                pltpu.VMEM((4, PB, ny, nz), F32),
                pltpu.VMEM((4, PB, ny, nz), F32),
            ],
            8,
            fields.size * 5,
        )
        for start in (0, cut)
    ]
    ylo, yhi = local(
        corner_kernel,
        "corners",
        [lo, hi, density, xl, xr, inside[0][1]],
        [VMEM_SPEC] * 6,
        [y_shape] * 2,
        [VMEM_SPEC] * 2,
        [],
        8,
        ny * nz * 40,
    )
    yl, yr = shift(yhi, "gy", True), shift(ylo, "gy", False)
    g = local(
        edge_kernel,
        "edge_faces",
        [g, xl, xr, yl, yr, inside[1][1]],
        [VMEM_SPEC] * 6,
        wide_g,
        VMEM_SPEC,
        [],
        8,
        ny * nz * 40,
    )
    gl, gr = shift_z(g)

    def scratch(parts):
        return [
            pltpu.VMEM((parts, ny, nz), F32),
            pltpu.VMEM((4, nx, nz), F32),
            pltpu.VMEM((4, nx, nz), F32),
            pltpu.VMEM((2 * nz, nz), BF16),
            pltpu.VMEM((nz, nz), BF16),
            pltpu.VMEM((4, PB, ny, nz), F32),
            pltpu.VMEM((4, PB, ny, nz), F32),
        ]

    scale = 1.0 / math.sqrt(nz * nz_parts)
    middle, ext, g = local(
        functools.partial(sweep_kernel, False, nz_parts, scale),
        "sweep_first",
        [*tables, held[0], density, held[2], gl, gr, xl, xr, yl, yr, ylo, yhi, *(near(t) for t, _ in inside)],
        [SMEM_SPEC] * 2 + [VMEM_SPEC] * 13,
        [pltpu.VMEM(fields.shape, F32), jax.ShapeDtypeStruct((16 * ny, nz), F32), g_shape],
        [VMEM_SPEC] * 3,
        scratch(8) + [pltpu.VMEM((4, ny, nz), F32), pltpu.VMEM((PB * nz, nz), BF16)],
        20,
        fields.size * 20,
    )
    gl, gr = shift_z(g)
    return local(
        functools.partial(sweep_kernel, True, nz_parts, scale),
        "sweep_last",
        [*tables, near(middle), *held[1:], gl, gr, ext, ylo, yl, yr, share, owners],
        [SMEM_SPEC] * 2 + [VMEM_SPEC] * 9 + [SMEM_SPEC, VMEM_SPEC],
        [
            jax.ShapeDtypeStruct(fields.shape, F32),
            jax.ShapeDtypeStruct((ny // 2 + 8, nz), F32),
        ],
        [hbm, VMEM_SPEC],
        scratch(4)
        + [
            pltpu.VMEM((ny, nz), F32),
            pltpu.VMEM(fields.shape, F32),
            pltpu.SemaphoreType.DMA((nx // PB,)),
        ],
        20,
        fields.size * 20,
    )


STEPS = 32767.0


def share_kernel(*refs):
    *parts, out_ref = refs
    half = parts[0].shape[0] - 8
    both = parts[0][...]
    for part in parts[1:]:
        both = both + part[...]
    value = both[:half]
    top = jnp.max(jnp.abs(value), axis=0, keepdims=True)
    power = jnp.floor(jnp.log(jnp.maximum(top, 1e-30)) * (1.0 / math.log(2.0))) + 1.0
    steps = jnp.floor(value * (STEPS * jnp.exp2(-power)) + 0.5)
    steps = jnp.clip(steps, -STEPS, STEPS)
    power = jnp.broadcast_to(power, (8, value.shape[1]))
    block = jnp.concatenate([steps, power, both[half:]], 0).astype(jnp.int32).astype(jnp.int16)
    for c in range(out_ref.shape[0]):
        out_ref[c] = block


def plane_kernel(ngx, ngy, me_ref, got_ref, out_ref, w_ref):
    cells = 64
    nx, ny = ngx * cells, ngy * cells
    columns = ngx * ngy
    half = cells // 2
    owners = []
    for cx in range(ngx):
        for cy in range(ngy):
            c = cx * ngy + cy
            got = got_ref[c].astype(jnp.int32).astype(F32)
            value = got[:half] * (jnp.exp2(got[half : half + 1]) * (1.0 / STEPS))
            for part in range(2):
                w_ref[pl.ds(cy * cells + part * half, half), pl.ds(cx * cells, cells)] = value[
                    :, part * cells : (part + 1) * cells
                ]
            owners.append(got[half + 8 : half + 9, :cells])

    def band(n):
        i = lax.broadcasted_iota(jnp.int32, (n, n), 0)
        j = lax.broadcasted_iota(jnp.int32, (n, n), 1)
        return jnp.maximum(R + 1 - jnp.abs(i - j), 0).astype(F32).astype(BF16)

    unit = float((R + 1) ** 4)
    weighted = twice(w_ref[...], band(nx))

    tiles = cells
    owner = jnp.concatenate(owners, 0)
    mine = owner == me_ref[0].astype(F32)
    flag = jnp.where(mine, 1.0, 0.0)
    a = lax.broadcasted_iota(jnp.int32, (tiles, tiles), 0)
    b = lax.broadcasted_iota(jnp.int32, (tiles, tiles), 1)
    rank = mm(flag.astype(BF16), jnp.where(a < b, 1.0, 0.0).astype(BF16))
    number = lanes_of((columns, tiles))
    column = lax.broadcasted_iota(jnp.int32, (columns, 1), 0)
    rows, blocks = [], []
    for k in range(MOST):
        chosen = mine & (rank == float(k))
        tile = jnp.sum(jnp.where(chosen, number, 0), axis=1, keepdims=True)
        there = jnp.sum(jnp.where(chosen, 1, 0), axis=1, keepdims=True)
        rows.append((column % ngy) * cells + (tile % (cells // TS)) * TS)
        block = (column // ngy) * (cells // TS) + tile // (cells // TS)
        blocks.append(jnp.where(there > 0, block, -1))
    row = jnp.concatenate(rows, 0)
    block = jnp.concatenate(blocks, 0)
    slots = MOST * columns
    across = lax.broadcasted_iota(jnp.int32, (slots, ny), 1)
    lefts = [
        jnp.maximum(R + 1 - jnp.abs(row + j - across), 0).astype(F32).astype(BF16)
        for j in range(TS)
    ]
    lines = left_twice(jnp.concatenate(lefts, 0), weighted)
    keep = lanes_of((slots, nx)) // TS == block
    from_x = lax.broadcasted_iota(jnp.int32, (nx, TS * TS), 0) % TS
    to_q = lanes_of((nx, TS * TS))
    out = jnp.zeros((slots, TS * TS), F32)
    for j in range(TS):
        fold = jnp.where(to_q == from_x * TS + j, 1.0, 0.0).astype(BF16)
        out = out + twice(jnp.where(keep, lines[j * slots : (j + 1) * slots], 0.0), fold)
    out = out / unit
    for k in range(MOST):
        out_ref[0, :, pl.ds(k * TS * TS, TS * TS)] = out[k * columns : (k + 1) * columns]


def on_device(fields, sources, material, shift_real, shift_imag, design_share, density, owner_map):
    ngx, ngy = lax.axis_size("gx"), lax.axis_size("gy")
    columns = ngx * ngy
    cells = density.shape[0]
    tables = (shift_real, shift_imag)
    owners = jnp.broadcast_to(owner_map.reshape(1, -1), (8, cells))
    final, partial = sweeps(tables, design_share, fields, sources, material, density, owners)
    if lax.axis_size("gz") == 2:
        parts = [partial, shift_z(partial)[0]]
    else:
        gathered = lax.all_gather(partial, "gz")
        parts = [gathered[i] for i in range(gathered.shape[0])]
    copies = local(
        share_kernel,
        "share",
        parts,
        [VMEM_SPEC] * len(parts),
        jax.ShapeDtypeStruct((columns, partial.shape[0] + 8, partial.shape[1]), jnp.int16),
        VMEM_SPEC,
        [],
        8,
        partial.size * 16,
    )
    plane = lax.all_to_all(copies, ("gx", "gy"), split_axis=0, concat_axis=0)
    me = (lax.axis_index("gx") * ngy + lax.axis_index("gy")).reshape(1)
    owned = pl.pallas_call(
        functools.partial(plane_kernel, ngx, ngy),
        in_specs=[SMEM_SPEC, VMEM_SPEC],
        out_specs=VMEM_SPEC,
        out_shape=jax.ShapeDtypeStruct((1, columns, MOST * TS * TS), F32),
        scratch_shapes=[pltpu.VMEM((ngy * cells, ngx * cells), F32)],
        compiler_params=pltpu.CompilerParams(vmem_limit_bytes=16 << 20),
        name="plane",
    )(me, plane)
    return (final, owned)


def solution(mesh):
    placed = (
        P(None, "gx", "gy", "gz"),
        P(None, "gx", "gy", "gz"),
        P("gx", "gy", "gz"),
        P(),
        P(),
        P(),
        P("gx", "gy"),
        P("gx", "gy", None, None),
    )
    return jax.shard_map(
        on_device,
        mesh=mesh,
        in_specs=placed,
        out_specs=(P(None, "gx", "gy", "gz"), P(("gx", "gy"), None, None)),
        check_vma=False,
    )
```

```python
import functools
import math

import jax
import jax.numpy as jnp
from jax import lax
from jax.experimental import pallas as pl
from jax.experimental.pallas import tpu as pltpu
from jax.sharding import PartitionSpec as P

R = 8
TS = 8
MOST = 8
RELAXATION = 0.8
SHARPNESS = 8.0
THRESHOLD = 0.5
PB = 8
RC = 16
F32 = jnp.float32
BF16 = jnp.bfloat16


def lanes_of(shape):
    return lax.broadcasted_iota(jnp.int32, shape, len(shape) - 1)


def ends_matrix(depth):
    k = lax.broadcasted_iota(jnp.int32, (PB * depth, depth), 0)
    j = lax.broadcasted_iota(jnp.int32, (PB * depth, depth), 1) % (2 * PB)
    even = (k % depth == 0) & (j == 2 * (k // depth))
    odd = (k % depth == depth - 1) & (j == 2 * (k // depth) + 1)
    return jnp.where(even | odd, 1.0, 0.0).astype(BF16)


def beside_matrix(depth):
    z = lax.broadcasted_iota(jnp.int32, (depth, depth), 0)
    j = lax.broadcasted_iota(jnp.int32, (depth, depth), 1)
    return jnp.where(jnp.abs(z - j) == 1, 1.0, 0.0).astype(BF16)


def halo_matrix(depth):
    j = lax.broadcasted_iota(jnp.int32, (depth, depth), 0)
    z = lax.broadcasted_iota(jnp.int32, (depth, depth), 1)
    even = (z == 0) & (j % 2 == 0)
    odd = (z == depth - 1) & (j % 2 == 1)
    return jnp.where(even | odd, 1.0, 0.0).astype(BF16)


def split(value):
    high = value.astype(BF16)
    return high, (value - high.astype(F32)).astype(BF16)


def mm(a, b):
    return lax.dot_general(a, b, (((1,), (0,)), ((), ())), preferred_element_type=F32)


def put_ends(first, ref, ends, gs):
    rows, depth = ref.shape[2:]
    high = ref[:, pl.ds(first, PB)].astype(BF16)
    beside = [high[:, p].reshape(4 * rows, depth) for p in range(PB)]
    picked = mm(jnp.concatenate(beside, 1), ends).reshape(4, rows, depth)
    here = lanes_of((rows, depth)) // (2 * PB) == first // PB
    for c in range(4):
        gs[c] = jnp.where(here, picked[c], gs[c])


def paired(value):
    high = value.astype(BF16).astype(F32)
    return jnp.concatenate([high, value - high], 1)


PLANES = 9


def x_kernel(v_ref, s_ref, m_ref, d_ref, xlo_ref, xhi_ref, vs, ss, ms, ds, sems):
    last = v_ref.shape[1] - 1
    rows, depth = v_ref.shape[2:]
    sides = ((0, 0, 1), (last, last - 1, 0))
    copies = []
    for i, (x, second, _) in enumerate(sides):
        copies.append(
            [
                pltpu.make_async_copy(
                    v_ref.at[:, pl.ds(min(x, second), 2)], vs.at[i], sems.at[3 * i]
                ),
                pltpu.make_async_copy(s_ref.at[:, x], ss.at[i], sems.at[3 * i + 1]),
                pltpu.make_async_copy(m_ref.at[x], ms.at[i], sems.at[3 * i + 2]),
            ]
        )
    for side in copies:
        for copy in side:
            copy.start()
    plane = pltpu.make_async_copy(d_ref, ds, sems.at[6])
    plane.start()
    plane.wait()
    cells = d_ref.shape[0]
    none = jnp.zeros((R, depth), F32)
    for i, (out_ref, start) in enumerate(((xlo_ref, 0), (xhi_ref, cells - R))):
        strip = jnp.concatenate([paired(ds[start : start + R, :]), none], 0)
        out_ref[PLANES * rows :] = strip.astype(BF16)
        for copy in copies[i]:
            copy.wait()
        inner = sides[i][2]
        out_ref[: 4 * rows] = vs[i, :, 1 - inner].astype(BF16).reshape(4 * rows, depth)
        beyond = vs[i, :, inner] + ss[i].astype(F32)
        out_ref[4 * rows : 8 * rows] = beyond.astype(BF16).reshape(4 * rows, depth)
        out_ref[8 * rows : 9 * rows] = (ms[i] + 1).astype(F32).astype(BF16)


def pack_kernel(v_ref, s_ref, m_ref, ylo_ref, yhi_ref, g_ref, gs, ylo, yhi, ends):
    rows, depth = v_ref.shape[2:]
    gs[...] = jnp.zeros_like(gs)
    ends[...] = ends_matrix(depth)

    def group(i, carry):
        first = i * PB
        put_ends(first, v_ref, ends[...], gs)
        for p in range(PB):
            x = first + p
            here = pl.ds(x, 1)
            level = (m_ref[x] + 1).astype(F32)
            for out, edge, inner, low in ((ylo, 0, 1, 0), (yhi, rows - 1, rows - 2, rows - 16)):
                for c in range(4):
                    out[c, here, :] = v_ref[c, x, edge : edge + 1, :]
                    source = s_ref[c, x, low : low + 16, :].astype(F32)[edge - low : edge - low + 1]
                    out[4 + c, here, :] = v_ref[c, x, inner : inner + 1, :] + source
                out[8, here, :] = level[edge : edge + 1]
        return carry

    lax.fori_loop(0, v_ref.shape[1] // PB, group, 0)
    g_ref[...] = gs[...].astype(BF16)
    for out_ref, rows_out in ((ylo_ref, ylo), (yhi_ref, yhi)):
        out_ref[...] = rows_out[...].astype(BF16).reshape(out_ref.shape)


def corner_kernel(lo_ref, hi_ref, d_ref, xl_ref, xr_ref, _, ylo_ref, yhi_ref):
    block, depth = lo_ref.shape
    cells = d_ref.shape[0]
    rows = (xl_ref.shape[0] - 2 * R) // PLANES
    strips = [r[PLANES * rows :].astype(F32)[:R] for r in (xl_ref, xr_ref)]
    filler = jnp.zeros((cells - 2 * R, depth), F32)
    tall = jnp.concatenate([strips[0], paired(d_ref[...]), strips[1], filler], 0).astype(BF16)
    for out_ref, from_ref, edge, low in (
        (ylo_ref, lo_ref, 0, 0),
        (yhi_ref, hi_ref, rows - 1, rows - 16),
    ):
        out_ref[:block] = from_ref[...]
        corners = [
            r[c * rows + low : c * rows + low + 16].astype(F32)[edge - low : edge - low + 1]
            for r in (xl_ref, xr_ref)
            for c in range(4)
        ]
        corners.append(jnp.zeros((2 * R - 8, depth), F32))
        out_ref[block : block + 2 * R] = jnp.concatenate(corners, 0).astype(BF16)
        out_ref[block + 2 * R :] = tall


def inside_kernel(start, v_ref, s_ref, t_ref, token_ref, near, zt0, zt1):
    planes_here, rows, depth = v_ref.shape[1:]
    token_ref[...] = jnp.zeros_like(token_ref)
    near[...] = jnp.concatenate([beside_matrix(depth)] * 2, 0)
    row8 = lax.broadcasted_iota(jnp.int32, (8, depth), 0)
    count = t_ref.shape[1]

    def along_z(first, zt):
        v = v_ref[:, pl.ds(first, PB)].reshape(4 * PB * rows, depth)
        zt[...] = mm(jnp.concatenate(split(v), 1), near[...]).reshape(4, PB, rows, depth)

    def group(i, zt, zt_next):
        first = start + i * PB
        along_z(jnp.minimum(first + PB, start + count - PB), zt_next)
        for p in range(PB):
            x = first + p
            for low in range(0, rows, RC):
                span = slice(low, low + RC)
                for c in range(4):
                    v = v_ref[c, x, span]
                    before = v_ref[c, jnp.maximum(x - 1, 0), span]
                    after = v_ref[c, jnp.minimum(x + 1, planes_here - 1), span]
                    if p == 0:
                        before = jnp.where(x == 0, 0.0, before)
                    if p == PB - 1:
                        after = jnp.where(x == planes_here - 1, 0.0, after)
                    if low == 0:
                        up = pltpu.roll(v, 1, 0)
                        up = jnp.concatenate([jnp.where(row8 == 0, 0.0, up[:8]), up[8:]], 0)
                    else:
                        up = v_ref[c, x, low - 1 : low - 1 + RC]
                    if low == rows - RC:
                        down = pltpu.roll(v, RC - 1, 0)
                        down = jnp.concatenate([down[:-8], jnp.where(row8 == 7, 0.0, down[-8:])], 0)
                    else:
                        down = v_ref[c, x, low + 1 : low + 1 + RC]
                    total = before + after + s_ref[c, x, span].astype(F32) + zt[c, p, span]
                    t_ref[c, i * PB + p, span] = total + up + down

    def two(i, carry):
        group(2 * i, zt0, zt1)
        group(2 * i + 1, zt1, zt0)
        return carry

    along_z(start, zt0)
    lax.fori_loop(0, count // (2 * PB), two, 0)


def edge_kernel(g_ref, xl_ref, xr_ref, yl_ref, yr_ref, _, out_ref):
    parts, rows, depth = g_ref.shape
    beside = [r[: 4 * rows] for r in (xl_ref, xr_ref, yl_ref, yr_ref)]
    picked = mm(jnp.concatenate(beside, 1), ends_matrix(depth)[: 4 * depth])
    out_ref[:4] = g_ref[...]
    out_ref[4:] = picked.astype(BF16).reshape(4, rows, depth)


def sweep_kernel(last, nz, scale, *refs):
    sr_ref, si_ref, v_ref, s_ref, m_ref, gl_ref, gr_ref = refs[:7]
    if last:
        ext_ref, mid_ref, yl_ref, yr_ref, sh_ref, own_ref, o_ref, sens_ref = refs[7:15]
        hs, yl, yr, near, far, zt0, zt1, sens, news, sems = refs[15:]
    else:
        xl_ref, xr_ref, yl_ref, yr_ref, ylo_ref, yhi_ref = refs[7:13]
        ta_ref, tb_ref, o_ref, ext_ref, g_ref = refs[13:18]
        hs, yl, yr, near, far, zt0, zt1, gs, ends = refs[18:]
    planes_here, rows, depth = v_ref.shape[1:]
    lane = lanes_of((rows, depth))

    if nz == 2:
        here = lax.axis_index("gz").astype(F32)
        keep_l, keep_r = here, 1.0 - here
    else:
        keep_l, keep_r = 1.0, 1.0
    for c in range(gl_ref.shape[0]):
        left = pltpu.roll(gl_ref[c].astype(F32), depth - 1, 1) * keep_l
        right = pltpu.roll(gr_ref[c].astype(F32), 1, 1) * keep_r
        hs[c] = jnp.where(lane % 2 == 0, left, right)
    near[...] = jnp.concatenate([beside_matrix(depth)] * 2, 0)
    far[...] = halo_matrix(depth)
    if last:
        sens[...] = jnp.zeros_like(sens)
    else:
        gs[...] = jnp.zeros_like(gs)
        ends[...] = ends_matrix(depth)
    face = 4 * rows
    if last:
        yl[...] = ext_ref[2 * face : 3 * face].reshape(4, rows, depth)
        yr[...] = ext_ref[3 * face : 4 * face].reshape(4, rows, depth)
    else:
        yl[...] = yl_ref[:face].astype(F32).reshape(4, rows, depth)
        yr[...] = yr_ref[:face].astype(F32).reshape(4, rows, depth)

    def x_halo(side, low):
        if last:
            return ext_ref[side * face + low : side * face + low + RC]
        return (xl_ref, xr_ref)[side][low : low + RC].astype(F32)

    levels = sr_ref.shape[0]
    tile = (8, depth)
    wr, wi, share = [], [], []
    for m in range(levels):
        d = 6.0 + jnp.full(tile, sr_ref[m], F32)
        s = jnp.full(tile, si_ref[m], F32)
        mag = d * d + s * s
        wr.append(RELAXATION * d / mag)
        wi.append(-RELAXATION * s / mag)
        if last:
            share.append(jnp.full(tile, sh_ref[m], F32))

    def lookup(masks, table):
        out = jnp.broadcast_to(table[0], masks[0].shape)
        for mask, entry in zip(masks, table[1:]):
            out = jnp.where(mask, entry, out)
        return out.reshape(-1, depth)

    row8 = lax.broadcasted_iota(jnp.int32, tile, 0)

    def along_z(first, zt):
        masked = [
            jnp.where(lane // 2 == first + p, hs[c], 0.0).astype(BF16)
            for c in range(4)
            for p in range(PB)
        ]
        out = mm(jnp.concatenate(masked, 0), far[...])
        if last:
            v = v_ref[:, pl.ds(first, PB)].reshape(4 * PB * rows, depth)
            out = out + mm(jnp.concatenate(split(v), 1), near[...])
        zt[...] = out.reshape(4, PB, rows, depth)

    def plane(first, p, zt, put, inside=None):
        for low in range(0, rows, RC):
            chunk(first, p, low, zt, put, inside)

    def chunk(first, p, low, zt, put, inside):
        x = first + p
        span = slice(low, low + RC)
        mat = m_ref[x, span].reshape(RC // 8, 8, depth)
        masks = [mat == m for m in range(1, levels)]
        w_r, w_i = lookup(masks, wr), lookup(masks, wi)

        def join(c):
            t_ref, t_start = inside
            total = t_ref[c, x - t_start, span] + zt[c, p, span]
            if p == 0:
                total = total + jnp.where(x == 0, x_halo(0, c * rows + low), 0.0)
            if p == PB - 1:
                total = total + jnp.where(x == planes_here - 1, x_halo(1, c * rows + low), 0.0)
            if low == 0:
                top = total[:8] + jnp.where(row8 == 0, yl[c, pl.ds(x, 1), :], 0.0)
                total = jnp.concatenate([top, total[8:]], 0)
            if low == rows - RC:
                tail = total[-8:] + jnp.where(row8 == 7, yr[c, pl.ds(x, 1), :], 0.0)
                total = jnp.concatenate([total[:-8], tail], 0)
            return v_ref[c, x, span], total

        def drive(c):
            if not last:
                return join(c)
            v = v_ref[c, x, span]
            if p == 0:
                before = v_ref[c, jnp.maximum(x - 1, 0), span]
                before = jnp.where(x == 0, x_halo(0, c * rows + low), before)
            else:
                before = v_ref[c, x - 1, span]
            if p == PB - 1:
                after = v_ref[c, jnp.minimum(x + 1, planes_here - 1), span]
                after = jnp.where(x == planes_here - 1, x_halo(1, c * rows + low), after)
            else:
                after = v_ref[c, x + 1, span]
            total = before + after + s_ref[c, x, span].astype(F32) + zt[c, p, span]
            if low == 0:
                up = pltpu.roll(v, 1, 0)
                top = jnp.where(row8 == 0, yl[c, pl.ds(x, 1), :], up[:8])
                up = jnp.concatenate([top, up[8:]], 0)
            else:
                up = v_ref[c, x, low - 1 : low - 1 + RC]
            if low == rows - RC:
                down = pltpu.roll(v, RC - 1, 0)
                tail = jnp.where(row8 == 7, yr[c, pl.ds(x, 1), :], down[-8:])
                down = jnp.concatenate([down[:-8], tail], 0)
            else:
                down = v_ref[c, x, low + 1 : low + 1 + RC]
            return v, total + up + down

        new = []
        for re in (0, 2):
            v_r, t_r = drive(re)
            v_i, t_i = drive(re + 1)
            keep = 1.0 - RELAXATION
            n_r = keep * v_r + (w_r * t_r - w_i * t_i)
            n_i = keep * v_i + (w_r * t_i + w_i * t_r)
            put(re, span, n_r)
            put(re + 1, span, n_i)
            new += [n_r, n_i]
        if last:
            value = lookup(masks, share) * (new[0] * new[2] - new[1] * new[3])
            column = jnp.sum(value, axis=1, keepdims=True)
            sens[span] = jnp.where(lane[:RC] == x, column, sens[span])

    groups = planes_here // PB

    def store(i):
        part = pl.ds(i * PB, PB)
        return pltpu.make_async_copy(news.at[:, part], o_ref.at[:, part], sems.at[i])

    result = news if last else o_ref

    def group(i, zt, zt_next, inside=None):
        first = i * PB
        along_z(jnp.minimum(first + PB, planes_here - PB), zt_next)
        for p in range(PB):

            def put(c, span, new, p=p):
                result[c, first + p, span] = new

            plane(first, p, zt, put, inside)
        if last:
            store(i).start()
        else:
            put_ends(first, o_ref, ends[...], gs)

    def pairs(begin, end, inside=None):
        def two(i, carry):
            group(2 * i, zt0, zt1, inside)
            group(2 * i + 1, zt1, zt0, inside)
            return carry

        lax.fori_loop(begin, end, two, 0)

    along_z(0, zt0)
    if last:
        pairs(0, groups // 2)
    else:
        cut = ta_ref.shape[1]
        pairs(0, cut // (2 * PB), (ta_ref, 0))
        pairs(cut // (2 * PB), groups // 2, (tb_ref, cut))

    if not last:
        g_ref[...] = gs[...].astype(BF16)
        sides = (xl_ref, xr_ref, yl_ref, yr_ref)
        centres = jnp.concatenate([r[:face] for r in sides], 0)
        masked = [
            jnp.where(lane // 2 == e, hs[4 + c], 0.0).astype(BF16) for e in range(4) for c in range(4)
        ]
        along = mm(centres, near[:depth]) + mm(jnp.concatenate(masked, 0), far[...])
        for e in range(4):
            zt0[:, e] = along[e * face : (e + 1) * face].reshape(4, rows, depth)
        block = PLANES * planes_here
        corner_l = yl_ref[block : block + 2 * R].astype(F32)
        corner_r = yr_ref[block : block + 2 * R].astype(F32)
        zero = jnp.zeros(tile, F32)
        for e, ref in enumerate(sides):
            level = ref[2 * face : 2 * face + rows].astype(F32).reshape(rows // 8, 8, depth)
            masks = [level == float(m + 1) for m in range(levels)]
            w_r, w_i = lookup(masks, [zero] + wr), lookup(masks, [zero] + wi)

            def near_plane(c, e=e, ref=ref):
                part = slice(c * rows, (c + 1) * rows)
                v = ref[part].astype(F32)
                beyond = ref[face + c * rows : face + (c + 1) * rows].astype(F32)
                if e < 2:
                    inside = v_ref[c, 0 if e == 0 else planes_here - 1]
                    top, low = corner_l[4 * e + c : 4 * e + c + 1], corner_r[4 * e + c : 4 * e + c + 1]
                else:
                    inside = (ylo_ref, yhi_ref)[e - 2][part].astype(F32)
                    corner = corner_l if e == 2 else corner_r
                    top, low = corner[c : c + 1], corner[4 + c : 5 + c]
                total = beyond + inside + zt0[c, e]
                up = pltpu.roll(v, 1, 0)
                down = pltpu.roll(v, rows - 1, 0)
                up = jnp.concatenate([jnp.where(row8 == 0, top, up[:8]), up[8:]], 0)
                down = jnp.concatenate([down[:-8], jnp.where(row8 == 7, low, down[-8:])], 0)
                return v, total + up + down

            for re in (0, 2):
                v_r, t_r = near_plane(re)
                v_i, t_i = near_plane(re + 1)
                keep = 1.0 - RELAXATION
                at = e * face + re * rows
                ext_ref[at : at + rows] = keep * v_r + (w_r * t_r - w_i * t_i)
                ext_ref[at + rows : at + 2 * rows] = keep * v_i + (w_r * t_i + w_i * t_r)
    else:
        cells = rows
        row = lax.broadcasted_iota(jnp.int32, (cells, 2 * cells), 0)
        col = lanes_of((cells, 2 * cells))
        half_sum = jnp.zeros((cells, 2 * cells), F32)
        for shift, ref in ((-cells, yl_ref), (0, mid_ref), (cells, yr_ref)):
            weight = jnp.maximum(R + 1 - jnp.abs(col % cells + shift - row), 0)
            tall = ref[PLANES * planes_here + 2 * R :]
            half_sum = half_sum + lax.dot_general(
                weight.astype(F32).astype(BF16),
                tall,
                (((1,), (1,)), ((), ())),
                preferred_element_type=F32,
            )
        row = lax.broadcasted_iota(jnp.int32, (2 * cells, depth), 0)
        col = lanes_of((2 * cells, depth))
        weight = jnp.maximum(R + 1 - jnp.abs(row - R - col), 0).astype(F32).astype(BF16)
        filtered = twice(half_sum, weight) / float((R + 1) ** 4)
        tangent = jnp.tanh(SHARPNESS * (filtered - THRESHOLD))
        total = math.tanh(SHARPNESS * THRESHOLD) + math.tanh(SHARPNESS * (1.0 - THRESHOLD))
        slope = SHARPNESS * (1.0 - tangent * tangent) / total
        weighted = slope * sens[...] * scale
        half = rows // 2
        both = pltpu.roll(weighted[half:], depth // 2, 1)
        sens_ref[:half] = jnp.where(lane[:half] < depth // 2, weighted[:half], both)
        mine = jnp.where(lax.axis_index("gz") == 0, own_ref[...].astype(F32), 0.0)
        sens_ref[half:] = jnp.concatenate([mine, jnp.zeros((8, depth - rows), F32)], 1)
        for i in range(groups):
            store(i).wait()


def twice(value, right):
    high, low = split(value)
    return mm(high, right) + mm(low, right)


def left_twice(left, value):
    high, low = split(value)
    return mm(left, high) + mm(left, low)


SMEM_SPEC = pl.BlockSpec(memory_space=pltpu.SMEM)
VMEM_SPEC = pl.BlockSpec(memory_space=pltpu.VMEM)


def near(value):
    return pltpu.with_memory_space_constraint(value, pltpu.VMEM)


def far_away(value):
    return pltpu.with_memory_space_constraint(value, pltpu.HBM)


def local(kernel, name, operands, specs, shapes, out_specs, scratch, limit, cost):
    return pl.pallas_call(
        kernel,
        in_specs=specs,
        out_specs=out_specs,
        out_shape=shapes,
        scratch_shapes=scratch,
        compiler_params=pltpu.CompilerParams(vmem_limit_bytes=limit << 20),
        cost_estimate=pl.CostEstimate(flops=cost, bytes_accessed=cost, transcendentals=0),
        name=name,
    )(*operands)


def shift(value, axis, up):
    count = lax.axis_size(axis)
    pairs = [(i, i + 1) for i in range(count - 1)]
    return lax.ppermute(value, axis, pairs if up else [(j, i) for i, j in pairs])


def shift_z(g):
    if lax.axis_size("gz") == 2:
        other = lax.ppermute(g, "gz", [(0, 1), (1, 0)])
        return other, other
    return shift(g, "gz", True), shift(g, "gz", False)


def sweeps(tables, share, fields, sources, material, density, owners):
    _, nx, ny, nz = fields.shape
    nz_parts = lax.axis_size("gz")
    hbm = pl.BlockSpec(memory_space=pltpu.HBM)
    held = [near(a) for a in (fields, sources, material)]

    x_shape = jax.ShapeDtypeStruct((PLANES * ny + 2 * R, nz), BF16)
    y_shape = jax.ShapeDtypeStruct((PLANES * nx + 2 * R + 2 * nx, nz), BF16)
    g_shape = jax.ShapeDtypeStruct((4, ny, nz), BF16)
    wide_g = jax.ShapeDtypeStruct((8, ny, nz), BF16)
    xlo, xhi = local(
        x_kernel,
        "x_faces",
        [far_away(a) for a in (fields, sources, material, density)],
        [hbm] * 4,
        [x_shape] * 2,
        [VMEM_SPEC] * 2,
        [
            pltpu.VMEM((2, 4, 2, ny, nz), F32),
            pltpu.VMEM((2, 4, ny, nz), BF16),
            pltpu.VMEM((2, ny, nz), jnp.int32),
            pltpu.VMEM(density.shape, F32),
            pltpu.SemaphoreType.DMA((7,)),
        ],
        8,
        ny * nz * 100,
    )
    xl, xr = shift(xhi, "gx", True), shift(xlo, "gx", False)
    part_shape = jax.ShapeDtypeStruct((PLANES * nx, nz), BF16)
    lo, hi, g = local(
        pack_kernel,
        "pack_faces",
        held,
        [VMEM_SPEC] * 3,
        [part_shape, part_shape, g_shape],
        [VMEM_SPEC] * 3,
        [
            pltpu.VMEM((4, ny, nz), F32),
            pltpu.VMEM((PLANES, nx, nz), F32),
            pltpu.VMEM((PLANES, nx, nz), F32),
            pltpu.VMEM((PB * nz, nz), BF16),
        ],
        12,
        fields.size * 4,
    )
    cut = nx // 2
    inside = [
        local(
            functools.partial(inside_kernel, start),
            "inside",
            held[:2],
            [VMEM_SPEC] * 2,
            [pltpu.VMEM((4, cut, ny, nz), F32), jax.ShapeDtypeStruct((8, nz), F32)],
            [VMEM_SPEC] * 2,
            [
                pltpu.VMEM((2 * nz, nz), BF16),
                pltpu.VMEM((4, PB, ny, nz), F32),
                pltpu.VMEM((4, PB, ny, nz), F32),
            ],
            8,
            fields.size * 5,
        )
        for start in (0, cut)
    ]
    ylo, yhi = local(
        corner_kernel,
        "corners",
        [lo, hi, density, xl, xr, inside[0][1]],
        [VMEM_SPEC] * 6,
        [y_shape] * 2,
        [VMEM_SPEC] * 2,
        [],
        8,
        ny * nz * 40,
    )
    yl, yr = shift(yhi, "gy", True), shift(ylo, "gy", False)
    g = local(
        edge_kernel,
        "edge_faces",
        [g, xl, xr, yl, yr, inside[1][1]],
        [VMEM_SPEC] * 6,
        wide_g,
        VMEM_SPEC,
        [],
        8,
        ny * nz * 40,
    )
    gl, gr = shift_z(g)

    def scratch(parts):
        return [
            pltpu.VMEM((parts, ny, nz), F32),
            pltpu.VMEM((4, nx, nz), F32),
            pltpu.VMEM((4, nx, nz), F32),
            pltpu.VMEM((2 * nz, nz), BF16),
            pltpu.VMEM((nz, nz), BF16),
            pltpu.VMEM((4, PB, ny, nz), F32),
            pltpu.VMEM((4, PB, ny, nz), F32),
        ]

    scale = 1.0 / math.sqrt(nz * nz_parts)
    middle, ext, g = local(
        functools.partial(sweep_kernel, False, nz_parts, scale),
        "sweep_first",
        [*tables, held[0], density, held[2], gl, gr, xl, xr, yl, yr, ylo, yhi, *(near(t) for t, _ in inside)],
        [SMEM_SPEC] * 2 + [VMEM_SPEC] * 13,
        [pltpu.VMEM(fields.shape, F32), jax.ShapeDtypeStruct((16 * ny, nz), F32), g_shape],
        [VMEM_SPEC] * 3,
        scratch(8) + [pltpu.VMEM((4, ny, nz), F32), pltpu.VMEM((PB * nz, nz), BF16)],
        20,
        fields.size * 20,
    )
    gl, gr = shift_z(g)
    return local(
        functools.partial(sweep_kernel, True, nz_parts, scale),
        "sweep_last",
        [*tables, near(middle), *held[1:], gl, gr, ext, ylo, yl, yr, share, owners],
        [SMEM_SPEC] * 2 + [VMEM_SPEC] * 9 + [SMEM_SPEC, VMEM_SPEC],
        [
            jax.ShapeDtypeStruct(fields.shape, F32),
            jax.ShapeDtypeStruct((ny // 2 + 8, nz), F32),
        ],
        [hbm, VMEM_SPEC],
        scratch(4)
        + [
            pltpu.VMEM((ny, nz), F32),
            pltpu.VMEM(fields.shape, F32),
            pltpu.SemaphoreType.DMA((nx // PB,)),
        ],
        20,
        fields.size * 20,
    )


STEPS = 32767.0


def share_kernel(*refs):
    *parts, out_ref = refs
    half = parts[0].shape[0] - 8
    both = parts[0][...]
    for part in parts[1:]:
        both = both + part[...]
    value = both[:half]
    top = jnp.max(jnp.abs(value), axis=0, keepdims=True)
    power = jnp.floor(jnp.log(jnp.maximum(top, 1e-30)) * (1.0 / math.log(2.0))) + 1.0
    steps = jnp.floor(value * (STEPS * jnp.exp2(-power)) + 0.5)
    steps = jnp.clip(steps, -STEPS, STEPS)
    row = lax.broadcasted_iota(jnp.int32, (8, value.shape[1]), 0)
    known = jnp.where(row < 4, power, both[half:])
    block = jnp.concatenate([steps, known], 0).astype(jnp.int32).astype(jnp.int16)
    for c in range(out_ref.shape[0]):
        out_ref[c] = block


def plane_kernel(ngx, ngy, me_ref, got_ref, out_ref, w_ref):
    cells = 64
    nx, ny = ngx * cells, ngy * cells
    columns = ngx * ngy
    half = cells // 2
    owners = []
    for cx in range(ngx):
        for cy in range(ngy):
            c = cx * ngy + cy
            got = got_ref[c].astype(jnp.int32).astype(F32)
            value = got[:half] * (jnp.exp2(got[half : half + 1]) * (1.0 / STEPS))
            for part in range(2):
                w_ref[pl.ds(cy * cells + part * half, half), pl.ds(cx * cells, cells)] = value[
                    :, part * cells : (part + 1) * cells
                ]
            owners.append(got[half + 7 : half + 8, :cells])

    def band(n):
        i = lax.broadcasted_iota(jnp.int32, (n, n), 0)
        j = lax.broadcasted_iota(jnp.int32, (n, n), 1)
        return jnp.maximum(R + 1 - jnp.abs(i - j), 0).astype(F32).astype(BF16)

    unit = float((R + 1) ** 4)
    weighted = twice(w_ref[...], band(nx))

    tiles = cells
    owner = jnp.concatenate(owners, 0)
    mine = owner == me_ref[0].astype(F32)
    flag = jnp.where(mine, 1.0, 0.0)
    a = lax.broadcasted_iota(jnp.int32, (tiles, tiles), 0)
    b = lax.broadcasted_iota(jnp.int32, (tiles, tiles), 1)
    rank = mm(flag.astype(BF16), jnp.where(a < b, 1.0, 0.0).astype(BF16))
    number = lanes_of((columns, tiles))
    column = lax.broadcasted_iota(jnp.int32, (columns, 1), 0)
    rows, blocks = [], []
    for k in range(MOST):
        chosen = mine & (rank == float(k))
        tile = jnp.sum(jnp.where(chosen, number, 0), axis=1, keepdims=True)
        there = jnp.sum(jnp.where(chosen, 1, 0), axis=1, keepdims=True)
        rows.append((column % ngy) * cells + (tile % (cells // TS)) * TS)
        block = (column // ngy) * (cells // TS) + tile // (cells // TS)
        blocks.append(jnp.where(there > 0, block, -1))
    row = jnp.concatenate(rows, 0)
    block = jnp.concatenate(blocks, 0)
    slots = MOST * columns
    across = lax.broadcasted_iota(jnp.int32, (slots, ny), 1)
    lefts = [
        jnp.maximum(R + 1 - jnp.abs(row + j - across), 0).astype(F32).astype(BF16)
        for j in range(TS)
    ]
    lines = left_twice(jnp.concatenate(lefts, 0), weighted)
    keep = lanes_of((slots, nx)) // TS == block
    from_x = lax.broadcasted_iota(jnp.int32, (nx, TS * TS), 0) % TS
    to_q = lanes_of((nx, TS * TS))
    out = jnp.zeros((slots, TS * TS), F32)
    for j in range(TS):
        fold = jnp.where(to_q == from_x * TS + j, 1.0, 0.0).astype(BF16)
        out = out + twice(jnp.where(keep, lines[j * slots : (j + 1) * slots], 0.0), fold)
    out = out / unit
    for k in range(MOST):
        out_ref[0, :, pl.ds(k * TS * TS, TS * TS)] = out[k * columns : (k + 1) * columns]


def on_device(fields, sources, material, shift_real, shift_imag, design_share, density, owner_map):
    ngx, ngy = lax.axis_size("gx"), lax.axis_size("gy")
    columns = ngx * ngy
    cells = density.shape[0]
    tables = (shift_real, shift_imag)
    owners = jnp.broadcast_to(owner_map.reshape(1, -1), (8, cells))
    final, partial = sweeps(tables, design_share, fields, sources, material, density, owners)
    if lax.axis_size("gz") == 2:
        parts = [partial, shift_z(partial)[0]]
    else:
        gathered = lax.all_gather(partial, "gz")
        parts = [gathered[i] for i in range(gathered.shape[0])]
    copies = local(
        share_kernel,
        "share",
        parts,
        [VMEM_SPEC] * len(parts),
        jax.ShapeDtypeStruct((columns, *partial.shape), jnp.int16),
        VMEM_SPEC,
        [],
        8,
        partial.size * 16,
    )
    plane = lax.all_to_all(copies, ("gx", "gy"), split_axis=0, concat_axis=0)
    me = (lax.axis_index("gx") * ngy + lax.axis_index("gy")).reshape(1)
    owned = pl.pallas_call(
        functools.partial(plane_kernel, ngx, ngy),
        in_specs=[SMEM_SPEC, VMEM_SPEC],
        out_specs=VMEM_SPEC,
        out_shape=jax.ShapeDtypeStruct((1, columns, MOST * TS * TS), F32),
        scratch_shapes=[pltpu.VMEM((ngy * cells, ngx * cells), F32)],
        compiler_params=pltpu.CompilerParams(vmem_limit_bytes=16 << 20),
        name="plane",
    )(me, plane)
    return (final, owned)


def solution(mesh):
    placed = (
        P(None, "gx", "gy", "gz"),
        P(None, "gx", "gy", "gz"),
        P("gx", "gy", "gz"),
        P(),
        P(),
        P(),
        P("gx", "gy"),
        P("gx", "gy", None, None),
    )
    return jax.shard_map(
        on_device,
        mesh=mesh,
        in_specs=placed,
        out_specs=(P(None, "gx", "gy", "gz"), P(("gx", "gy"), None, None)),
        check_vma=False,
    )
```
